32 devices in a mesh: groups: 2 (over y), dp: 4 (over z), section: 4 (over x, core).
Axes of the slice: x: 2, y: 2, z: 4, core: 2. Of those that a mesh axis runs over, the one named last changes fastest.
Arguments:
- activations: bfloat16 [4, 32, 16, 16, 512], P('section', ('groups', 'dp')), parts along dimension 1, may hold values from -6 to 6
- depth_small: float32 [4, 3, 3, 512], P('section'), may hold values from -2 to 2
- point_first: bfloat16 [4, 512, 512], P('section'), may hold values from -0.25 to 0.25
- depth_large: float32 [4, 5, 5, 512], P('section'), may hold values from -1.25 to 1.25
- point_second: bfloat16 [4, 512, 512], P('section'), may hold values from -0.25 to 0.25
- head_weight: bfloat16 [1000, 512], replicated, may hold values from -0.25 to 0.25
- offsets: int32 [32], P(('groups', 'dp')), parts along dimension 0, may hold values from 0 to 15
- labels: int32 [32], P(('groups', 'dp')), parts along dimension 0, may hold values from 0 to 999
Outputs:
- grad_first: float32 [4, 1024, 512], P('section', 'groups'), parts along dimension 1
- grad_second: float32 [4, 1024, 512], P('section', 'groups'), parts along dimension 1
- grad_small: float32 [4, 6, 3, 512], P('section', 'groups'), parts along dimension 1
- grad_large: float32 [4, 10, 5, 512], P('section', 'groups'), parts along dimension 1
The draws below stay inside these ranges and needn't reach their ends.
There are 2 independent parts, one for each index of `groups`. The reference program is written for one: setup_inputs(seed, part) draws one part's arguments, and reference() takes and returns one part's arrays. A program takes and returns all parts, laid end to end along the dimension named above; an argument that names none is the same for every part. Nothing has to cross between parts.
All inputs are finite; a program needn't handle non-finite values.
Results may differ from the reference program's by a relative error of at most 0.0028.
Values may be sent and summed in bfloat16 or wider, within the bound.
A program may use at most 64 MiB of HBM per device.

```python
import jax
import jax.numpy as jnp
from jax import lax

CHANNELS = 512
CLASSES = 1000
HEIGHT = 16
WIDTH = 16
BAND = 4
IMAGES = 16
SECTIONS = 4


def touch_ends(values, own_key, smallest, high):
    longest = values.shape.index(max(values.shape))
    spots = []
    for shift in (0, 1):
        where = [jax.random.randint(jax.random.fold_in(own_key, axis), (), 0, length) for axis, length in enumerate(values.shape)]
        where[longest] = (where[longest] + shift) % values.shape[longest]
        spots.append(tuple(where))
    return values.at[spots[0]].set(smallest).at[spots[1]].set(high)


def levels(own_key, dims, shards, low, top_value):
    def one(dim, blocks):
        steps = jax.random.uniform(jax.random.fold_in(jax.random.fold_in(own_key, 6), dim), (blocks,), jnp.float32, low / len(shards), top_value / len(shards))
        return jnp.repeat(jnp.exp(steps), dims[dim] // blocks).reshape((-1,) + (1,) * (len(dims) - dim - 1))

    factor_of = one(*shards[0])
    for cut in shards[1:]:
        factor_of = factor_of * one(*cut)
    return factor_of


def noise(own_key, shape, scale, reach, split=(), held_as=jnp.bfloat16):
    gain = levels(own_key, shape, split, -0.22, 0.18) if split else 1.0
    values = jax.random.normal(own_key, shape, jnp.float32) * scale * gain
    return jnp.minimum(jnp.maximum(values, -reach), reach).astype(held_as)


def setup_inputs(seed: int = 0, part: int = 0) -> dict:
    keys = jax.random.split(jax.random.key(seed), 9)
    part_keys = jax.random.split(jax.random.fold_in(keys[8], part), 9)
    return {
        "activations": noise(part_keys[0], (SECTIONS, IMAGES, HEIGHT, WIDTH, CHANNELS), 1.0, 6.0, ((0, 4), (1, 4))),
        "depth_small": noise(keys[1], (SECTIONS, 3, 3, CHANNELS), 9 ** -0.5, 2.0, ((0, 4),), jnp.float32),
        "point_first": noise(keys[2], (SECTIONS, CHANNELS, CHANNELS), CHANNELS ** -0.5, 0.25, ((0, 4),)),
        "depth_large": noise(keys[3], (SECTIONS, 5, 5, CHANNELS), 25 ** -0.5, 1.25, ((0, 4),), jnp.float32),
        "point_second": noise(keys[4], (SECTIONS, CHANNELS, CHANNELS), CHANNELS ** -0.5, 0.25, ((0, 4),)),
        "head_weight": noise(keys[5], (CLASSES, CHANNELS), CHANNELS ** -0.5, 0.25),
        "offsets": touch_ends(jax.random.randint(part_keys[6], (IMAGES,), 0, WIDTH), jax.random.fold_in(part_keys[6], 1), 0, WIDTH - 1).astype(jnp.int32),
        "labels": touch_ends(jax.random.randint(part_keys[7], (IMAGES,), 0, CLASSES), jax.random.fold_in(part_keys[7], 1), 0, CLASSES - 1).astype(jnp.int32),
    }


loss_scale = 64.0


def depth_conv(inputs, kernel):
    size = kernel.shape[0]
    radius = size // 2
    height, width = inputs.shape[1], inputs.shape[2]
    padded = jnp.pad(inputs, ((0, 0), (radius, radius), (radius, radius), (0, 0)))
    result = jnp.zeros(inputs.shape, jnp.float32)
    for row_tap in range(size):
        for col_tap in range(size):
            result = result + kernel[row_tap, col_tap] * padded[:, row_tap:row_tap + height, col_tap:col_tap + width, :]
    return result


def depth_conv_t(grads, kernel):
    size = kernel.shape[0]
    radius = size // 2
    height, width = grads.shape[1], grads.shape[2]
    padded = jnp.pad(grads, ((0, 0), (radius, radius), (radius, radius), (0, 0)))
    result = jnp.zeros(grads.shape, jnp.float32)
    for row_tap in range(size):
        for col_tap in range(size):
            row_start = 2 * radius - row_tap
            col_start = 2 * radius - col_tap
            result = result + kernel[row_tap, col_tap] * padded[:, row_start:row_start + height, col_start:col_start + width, :]
    return result


def depth_conv_k(inputs, grads, size):
    radius = size // 2
    height, width = inputs.shape[1], inputs.shape[2]
    padded = jnp.pad(inputs, ((0, 0), (radius, radius), (radius, radius), (0, 0)))
    rows_out = []
    for row_tap in range(size):
        taps = []
        for col_tap in range(size):
            taps.append(jnp.sum(padded[:, row_tap:row_tap + height, col_tap:col_tap + width, :] * grads, axis=(0, 1, 2)))
        rows_out.append(jnp.stack(taps))
    return jnp.stack(rows_out)


def section_forward(section_num, activations, depth_small, point_first, depth_large, offsets):
    inputs = activations[section_num].astype(jnp.float32)
    count, height, width, chans = inputs.shape
    if section_num == 0:
        columns = jnp.arange(width, dtype=jnp.int32)
        keep = (jnp.mod(columns[None, :] - offsets[:, None], width) < BAND).astype(jnp.float32)
        inputs = inputs * keep[:, None, :, None]
    first_act = jnp.maximum(inputs, 0.0)
    first_depth = depth_conv(first_act, depth_small[section_num]).astype(jnp.bfloat16)
    first_point = jnp.dot(first_depth.reshape(-1, chans), point_first[section_num], preferred_element_type=jnp.float32)
    second_act = jnp.maximum(first_point, 0.0).astype(jnp.bfloat16).reshape(inputs.shape)
    second_depth = depth_conv(second_act.astype(jnp.float32), depth_large[section_num]).astype(jnp.bfloat16)
    return inputs, first_act, first_depth, second_act, second_depth


def reference(activations, depth_small, point_first, depth_large, point_second, head_weight, offsets, labels):
    contract_last = (((1,), (1,)), ((), ()))
    contract_first = (((0,), (0,)), ((), ()))
    last = SECTIONS - 1
    inputs, first_act, first_depth, second_act, second_depth = section_forward(last, activations, depth_small, point_first, depth_large, offsets)
    count, height, width, chans = inputs.shape
    second_point = jnp.dot(second_depth.reshape(-1, chans), point_second[last], preferred_element_type=jnp.float32)
    output = inputs + second_point.reshape(inputs.shape)
    pooled = jnp.mean(output, axis=(1, 2))
    head_float = head_weight.astype(jnp.float32)
    logits = lax.dot_general(pooled, head_float, contract_last, precision=lax.Precision.HIGHEST)
    onehot = (labels[:, None] == jnp.arange(CLASSES, dtype=jnp.int32)[None, :]).astype(jnp.float32)
    dlog = loss_scale * (logits - onehot)
    grad_pool = jnp.dot(dlog, head_float, precision=lax.Precision.HIGHEST) / (height * width)
    grad_out = jnp.broadcast_to(grad_pool[:, None, None, :], inputs.shape).astype(jnp.bfloat16)
    firsts, seconds, smalls, larges = [], [], [], []
    for section_num in range(last, -1, -1):
        inputs, first_act, first_depth, second_act, second_depth = section_forward(section_num, activations, depth_small, point_first, depth_large, offsets)
        grad_rows = grad_out.reshape(-1, chans)
        grad_depth2 = lax.dot_general(grad_rows, point_second[section_num], contract_last, preferred_element_type=jnp.float32).reshape(inputs.shape)
        seconds.append(lax.dot_general(second_depth.reshape(-1, chans), grad_rows, contract_first, preferred_element_type=jnp.float32))
        larges.append(depth_conv_k(second_act.astype(jnp.float32), grad_depth2, 5))
        back_act2 = depth_conv_t(grad_depth2, depth_large[section_num])
        grad_point1 = jnp.where(second_act > 0, back_act2, 0.0).astype(jnp.bfloat16)
        point_rows = grad_point1.reshape(-1, chans)
        grad_depth1 = lax.dot_general(point_rows, point_first[section_num], contract_last, preferred_element_type=jnp.float32).reshape(inputs.shape)
        firsts.append(lax.dot_general(first_depth.reshape(-1, chans), point_rows, contract_first, preferred_element_type=jnp.float32))
        smalls.append(depth_conv_k(first_act, grad_depth1, 3))
        back_act1 = depth_conv_t(grad_depth1, depth_small[section_num])
        grad_out = (grad_out.astype(jnp.float32) + jnp.where(inputs > 0, back_act1, 0.0)).astype(jnp.bfloat16)
    return (jnp.stack(firsts[::-1]), jnp.stack(seconds[::-1]), jnp.stack(smalls[::-1]), jnp.stack(larges[::-1]))
```

```python
import jax
import jax.numpy as jnp
from jax import lax
from jax.experimental import pallas as pl
from jax.experimental.pallas import tpu as pltpu
from jax.sharding import PartitionSpec as P

BAND = 4
LOSS_SCALE = 64.0
LANES = 128
CHUNK_ROWS = 32
LAG = 1
SPREAD = 4
TAP_ROWS = 40
TAP_SMALL = 25
MASK_ROWS = 32
f32 = jnp.float32
bf16 = jnp.bfloat16
contract_last = (((1,), (1,)), ((), ()))
contract_first = (((0,), (0,)), ((), ()))


def dot(a, b, dims=(((1,), (0,)), ((), ()))):
    return lax.dot_general(a, b, dims, preferred_element_type=f32)


def split_dot(values, matrix, dims):
    rows = values.shape[0]
    high = values.astype(bf16).astype(f32)
    rest = values - high
    mid = rest.astype(bf16).astype(f32)
    low = (rest - mid).astype(bf16).astype(f32)
    parts = jnp.concatenate([high, mid, low, jnp.zeros_like(low)], axis=0).astype(bf16)
    out = dot(parts, matrix, dims)
    return out[:rows] + out[rows : 2 * rows] + out[2 * rows : 3 * rows]


def three_parts(values):
    high = values.astype(bf16).astype(f32)
    rest = values - high
    mid = rest.astype(bf16).astype(f32)
    return high, mid, (rest - mid).astype(bf16).astype(f32)


class Line:
    def __init__(self, place, line, owner, refs, get):
        self.place, self.line, self.owner = place, line, owner
        self.out, self.left, self.right, self.final, self.sems = refs
        self.get = get

    def copy(self, k, src, dst, send, recv, step):
        return pltpu.make_async_remote_copy(
            src_ref=src.at[k],
            dst_ref=dst.at[k],
            send_sem=self.sems.at[send, k],
            recv_sem=self.sems.at[recv, k],
            device_id={"dp": jnp.clip(self.place + step, 0, self.line - 1)},
        )

    def to_right(self, k):
        return self.copy(k, self.out, self.left, 0, 3, 1)

    def to_left(self, k):
        return self.copy(k, self.out, self.right, 0, 4, -1)

    def final_left(self, k):
        return self.copy(k, self.final, self.final, 1, 5, -1)

    def final_right(self, k):
        return self.copy(k, self.final, self.final, 2, 5, 1)

    def ends(self):
        return (self.place == 0) | (self.place == self.line - 1)

    def leaf(self, k):
        place, line, owner, dtype = self.place, self.line, self.owner, self.out.dtype

        @pl.when((place != owner) & self.ends())
        def _():
            self.out[k] = self.get(k).astype(dtype)

        @pl.when((place != owner) & (place == 0))
        def _():
            self.to_right(k).start()

        @pl.when((place != owner) & (place == line - 1) & (place > 0))
        def _():
            self.to_left(k).start()

    def advance(self, phase, step, first, chunks):
        place, line, owner = self.place, self.line, self.owner
        outer = jnp.where(place < owner, place, line - 1 - place)
        apart = jnp.where(place < owner, owner - place, place - owner)
        meet = max(owner, line - 1 - owner)
        if phase == 0:
            lag, active, act = LAG * outer, (place != owner) & jnp.logical_not(self.ends()), self.relay
        elif phase == 1:
            lag, active, act = LAG * meet, place == owner, self.total
        else:
            lag, active, act = LAG * (meet + apart) + SPREAD, place != owner, self.spread
        k = step - lag

        @pl.when(active & (k >= 0) & (k < chunks))
        def _():
            act(k + first)

    def relay(self, k):
        place, line, owner, dtype = self.place, self.line, self.owner, self.out.dtype

        @pl.when(place < owner)
        def _():
            self.to_right(k).wait_recv()
            self.out[k] = (self.get(k) + self.left[k].astype(f32)).astype(dtype)
            self.to_right(k).start()

        @pl.when(place > owner)
        def _():
            self.to_left(k).wait_recv()
            self.out[k] = (self.get(k) + self.right[k].astype(f32)).astype(dtype)
            self.to_left(k).start()

    def total(self, k):
        line, owner, dtype = self.line, self.owner, self.out.dtype
        value = self.get(k)
        if owner > 0:
            self.to_right(k).wait_recv()
            value = value + self.left[k].astype(f32)
        if owner < line - 1:
            self.to_left(k).wait_recv()
            value = value + self.right[k].astype(f32)
        self.final[k] = value.astype(dtype)
        if owner > 0:
            self.final_left(k).start()
        if owner < line - 1:
            self.final_right(k).start()

    def spread(self, k):
        place, line, owner = self.place, self.line, self.owner
        self.final_left(k).wait_recv()

        @pl.when((place < owner) & (place > 0))
        def _():
            self.final_left(k).start()

        @pl.when((place > owner) & (place < line - 1))
        def _():
            self.final_right(k).start()

    def drain(self, k):
        place, line, owner = self.place, self.line, self.owner

        @pl.when(place != owner)
        def _():
            self.to_right(k).wait_send()

        @pl.when((place <= owner) & (place > 0))
        def _():
            self.final_left(k).wait_send()

        @pl.when((place >= owner) & (place < line - 1))
        def _():
            self.final_right(k).wait_send()


def kernel(
    offsets, labels, x, k3, w1, k5, w2, head,
    sums, tap_sums,
    d1, a2, d2, gin, gp1, gout, tmp, s5f, s3f, s5g, s3g, pool, acc3, acc5, taps,
    grads, windows, k5_rows, spread5, push, factors,
    send_sem, recv_sem, factor_send, factor_recv, *line_refs,
):
    section = lax.axis_index("section")
    count = lax.axis_size("section")
    images, height, width, chans = x.shape
    rows = height * width
    blocks = chans // LANES
    last = section == count - 1
    scale = 1.0 / rows

    barrier = pltpu.get_barrier_semaphore()

    @pl.when(section > 0)
    def _():
        pl.semaphore_signal(barrier, inc=1, device_id={"section": section - 1})

    @pl.when(section < count - 1)
    def _():
        pl.semaphore_signal(barrier, inc=1, device_id={"section": section + 1})

    place = lax.axis_index("dp")
    line = lax.axis_size("dp")

    for away in range(1, line):
        pl.semaphore_signal(barrier, inc=1, device_id={"dp": lax.rem(place + away, line)})

    def cols(block):
        return pl.ds(pl.multiple_of(block * LANES, LANES), LANES)

    col_index = lax.broadcasted_iota(jnp.int32, (1, width, LANES), 1)

    def shifted(value, by):
        if by == 0:
            return value
        moved = pltpu.roll(value, (-by) % width, axis=1)
        inside = (col_index + by >= 0) & (col_index + by < width)
        return jnp.where(inside, moved, 0.0)

    def fill(ref, value, size):
        radius = size // 2
        for tap in range(size):
            ref[tap, pl.ds(radius, height)] = shifted(value, tap - radius)

    def clear(ref, size):
        radius = size // 2
        zero = jnp.zeros((radius, width, LANES), f32)
        for tap in range(size):
            ref[tap, pl.ds(0, radius)] = zero
            ref[tap, pl.ds(radius + height, radius)] = zero

    def conv(ref, weights, size, block, flip):
        total = None
        for row_tap in range(size):
            for col_tap in range(size):
                r, c = row_tap, col_tap
                if flip:
                    r, c = size - 1 - r, size - 1 - c
                tap = row_tap * size + col_tap
                part = weights[tap, :, cols(block)] * ref[c, pl.ds(r, height)]
                total = part if total is None else total + part
        return total

    def kept(image):
        away = col_index - offsets[image]
        away = jnp.where(away < 0, away + width, away)
        return jnp.where((away < BAND) | (section > 0), 1.0, 0.0)

    def xin(image, block):
        return x[image, :, :, cols(block)].astype(f32) * kept(image)

    clear(s5f, 5)
    clear(s3f, 3)

    @pl.loop(0, images)
    def _(n):
        @pl.loop(0, blocks)
        def _(b):
            for ref, size in ((s5g, 5), (s3g, 3)):
                clear(ref.at[n, b], size)

    def window_mask():
        tap = lax.broadcasted_iota(jnp.int32, (MASK_ROWS, rows), 0)
        spot = lax.broadcasted_iota(jnp.int32, (MASK_ROWS, rows), 1)
        i, h = jnp.zeros_like(tap), jnp.zeros_like(spot)
        for step in range(1, 5):
            i = i + jnp.where(tap >= 5 * step, 1, 0)
        for step in range(1, height):
            h = h + jnp.where(spot >= width * step, 1, 0)
        down, along = h - i + 2, (spot - width * h) - (tap - 5 * i) + 2
        inside = (down >= 0) & (down < height) & (along >= 0) & (along < width) & (tap < 25)
        return jnp.where(inside, 1.0, 0.0)

    @pl.when(last)
    def _():
        mask = window_mask()
        push[...] = mask.astype(bf16)
        k5_rows[pl.ds(24, 8)] = jnp.zeros((8, chans), f32)
        for tap in range(25):
            k5_rows[pl.ds(tap, 1)] = k5[tap]
        parts = jnp.concatenate(three_parts(k5_rows[...]), axis=0).astype(bf16)
        masks = jnp.concatenate([mask, mask, mask], axis=0).astype(bf16)
        spread5[...] = dot(masks, parts, contract_first)

    @pl.loop(0, images)
    def _(n):
        @pl.loop(0, blocks)
        def _(b):
            value = xin(n, b)
            pool[n, :, cols(b)] = jnp.sum(value.reshape(rows // 8, 8, LANES), axis=0)
            fill(s3f, jnp.maximum(value, 0.0), 3)
            out = conv(s3f, k3, 3, b, False)
            d1[n, :, cols(b)] = out.reshape(rows, LANES).astype(bf16)

        a2[n] = jnp.maximum(dot(d1[n], w1[...]), 0.0).astype(bf16)

        @pl.when(last)
        def _():
            windows[n] = dot(push[...], a2[n])

        @pl.when(jnp.logical_not(last))
        def _():
            @pl.loop(0, blocks)
            def _(b):
                value = a2[n, :, cols(b)].astype(f32).reshape(height, width, LANES)
                fill(s5f, value, 5)
                out = conv(s5f, k5, 5, b, False).reshape(rows, LANES).astype(bf16)
                d2[n, :, cols(b)] = out

    classes = head.shape[0]

    @pl.when(last)
    def _():
        x_sums = [jnp.sum(pool[n], axis=0, keepdims=True) for n in range(images)]
        d2_sums = [
            jnp.sum(k5_rows[...] * windows[n], axis=0, keepdims=True) for n in range(images)
        ]
        twice = -(-2 * images // 8) * 8
        fill_rows = [jnp.zeros((twice - 2 * images, chans), f32)] if twice > 2 * images else []
        x_sum = jnp.concatenate(x_sums + x_sums + fill_rows, axis=0)
        d2_sum = jnp.concatenate(d2_sums + d2_sums + fill_rows, axis=0)
        pooled = (x_sum + split_dot(d2_sum, w2[...], (((1,), (0,)), ((), ())))) * scale
        rest = jnp.zeros((LANES - twice, chans), f32)
        wide = jnp.concatenate([pooled, rest], axis=0)
        high = wide.astype(bf16)
        mid = (wide - high.astype(f32)).astype(bf16)
        logits = dot(head[...], high, contract_last) + dot(head[...], mid, contract_last)
        class_index = lax.broadcasted_iota(jnp.int32, (classes, LANES), 0)
        lane = lax.broadcasted_iota(jnp.int32, (1, LANES), 1)
        label_row = jnp.full((1, LANES), -1, jnp.int32)
        for n in range(images):
            label_row = jnp.where((lane == n) | (lane == n + images), labels[n], label_row)
        dlog = LOSS_SCALE * (logits - jnp.where(class_index == label_row, 1.0, 0.0))
        high = dlog.astype(bf16).astype(f32)
        part = jnp.where(lane < images, high, dlog - high).astype(bf16)
        both = dot(part, head[...], contract_first)
        grad = ((both[:images] + both[images : 2 * images]) * scale).astype(bf16).astype(f32)
        pad = jnp.zeros((8 - images, chans), f32)
        factors[place, pl.ds(0, 8)] = jnp.concatenate([*d2_sums, pad], axis=0)
        factors[place, pl.ds(8, 8)] = jnp.concatenate([grad, pad], axis=0)
        wide = jnp.concatenate([grad, jnp.zeros((16 - images, chans), f32)], axis=0)
        tmp[pl.ds(0, 16)] = dot(wide.astype(bf16), w2[...], contract_last)
        for n in range(images):
            gin[n] = jnp.broadcast_to(grad[n : n + 1], (rows, chans)).astype(bf16)
        for n in range(images):
            back = tmp[pl.ds(n, 1)]
            if n == 0:
                total = back * windows[n]
            else:
                total = total + back * windows[n]
            live = a2[n].astype(f32) > 0
            gp1[n] = jnp.where(live, back * spread5[...], 0.0).astype(bf16)
        for b in range(blocks):
            taps[b, pl.ds(0, 25)] = total[:25, b * LANES : (b + 1) * LANES]

    def hand_over(n):
        return pltpu.make_async_remote_copy(
            src_ref=gout.at[n],
            dst_ref=gin.at[n],
            send_sem=send_sem.at[n],
            recv_sem=recv_sem.at[n],
            device_id={"section": jnp.maximum(section - 1, 0)},
        )

    pl.semaphore_wait(
        barrier,
        jnp.where(section > 0, 1, 0)
        + jnp.where(section < count - 1, 1, 0)
        + (line - 1),
    )

    def give(away):
        other = lax.rem(place + away, line)
        return pltpu.make_async_remote_copy(
            src_ref=factors.at[place],
            dst_ref=factors.at[place],
            send_sem=factor_send.at[away],
            recv_sem=factor_recv.at[away],
            device_id={"dp": other},
        )

    def take(away):
        other = lax.rem(place + line - away, line)
        return pltpu.make_async_remote_copy(
            src_ref=factors.at[other],
            dst_ref=factors.at[other],
            send_sem=factor_send.at[away],
            recv_sem=factor_recv.at[away],
            device_id={"dp": lax.rem(place + away, line)},
        )

    @pl.when(last)
    def _():
        for away in range(1, line):
            give(away).start()

    owner = (line - 1) // 2
    chunk_rows = CHUNK_ROWS
    half = chans // chunk_rows
    main = Line(place, line, owner, [*line_refs[0:3], sums, line_refs[3]],
                lambda k: grads[pl.ds(pl.multiple_of(k * chunk_rows, chunk_rows), chunk_rows)])
    tap_line = Line(place, line, owner, [*line_refs[4:7], tap_sums, line_refs[7]],
                    lambda k: taps[k])
    begin = jnp.where(last, half, 0)

    def weight_grads(n):
        def add(start, left, right):
            part = dot(left[n], right[n], contract_first)
            where = pl.ds(start, chans)

            @pl.when(n == 0)
            def _():
                grads[where] = part

            @pl.when(n > 0)
            def _():
                grads[where] += part

        @pl.when(jnp.logical_not(last))
        def _():
            add(0, d2, gin)

        add(chans, d1, gp1)

    @pl.loop(0, images)
    def _(n):
        @pl.when(jnp.logical_not(last))
        def _():
            hand_over(n).wait_recv()
            tmp[...] = dot(gin[n], w2[...], contract_last)

            @pl.loop(0, blocks)
            def _(b):
                shifts = s5g.at[n, b]
                fill(shifts, tmp[:, cols(b)].reshape(height, width, LANES), 5)
                back = conv(shifts, k5, 5, b, True).reshape(rows, LANES)
                live = a2[n, :, cols(b)].astype(f32) > 0
                gp1[n, :, cols(b)] = jnp.where(live, back, 0.0).astype(bf16)

        @pl.when(n == images - 1)
        def _():
            weight_grads(n)

            @pl.loop(begin, 2 * half)
            def _(k):
                main.leaf(k)

        tmp[...] = dot(gp1[n], w1[...], contract_last)

        @pl.loop(0, blocks)
        def _(b):
            shifts = s3g.at[n, b]
            fill(shifts, tmp[:, cols(b)].reshape(height, width, LANES), 3)

            @pl.when(section > 0)
            def _():
                back = conv(shifts, k3, 3, b, True)
                back = jnp.where(xin(n, b) > 0, back, 0.0).reshape(rows, LANES)
                grad = gin[n, :, cols(b)].astype(f32) + back
                gout[n, :, cols(b)] = grad.astype(bf16)

        @pl.when(section > 0)
        def _():
            hand_over(n).start()

        @pl.when(n < images - 1)
        def _():
            weight_grads(n)

    def kernel_grad(acc, value, ref, size):
        for row_tap in range(size):
            for col_tap in range(size):
                other = ref[size - 1 - col_tap, pl.ds(size - 1 - row_tap, height)]
                part = (value * other).reshape(rows // 8, 8, LANES)
                acc[row_tap * size + col_tap] += jnp.sum(part, axis=0)

    def kernel_grads(unit):
        b, n = unit // images, unit % images

        @pl.when(n == 0)
        def _():
            acc3[...] = jnp.zeros_like(acc3)
            acc5[...] = jnp.zeros_like(acc5)

        @pl.when(jnp.logical_not(last))
        def _():
            value = a2[n, :, cols(b)].astype(f32).reshape(height, width, LANES)
            kernel_grad(acc5, value, s5g.at[n, b], 5)

        kernel_grad(acc3, jnp.maximum(xin(n, b), 0.0), s3g.at[n, b], 3)

        @pl.when(n == images - 1)
        def _():
            @pl.when(jnp.logical_not(last))
            def _():
                taps[b, pl.ds(0, 25)] = jnp.sum(acc5[...], axis=1)

            taps[b, pl.ds(TAP_SMALL, 9)] = jnp.sum(acc3[...], axis=1)

    busy = blocks * images
    taps[:, pl.ds(32, 8)] = jnp.zeros((blocks, 8, LANES), f32)

    @pl.loop(0, max(2 * half, busy + blocks) + LAG * line + SPREAD)
    def _(step):
        for phase in range(3):
            main.advance(phase, step, begin, 2 * half - begin)
            tap_line.advance(phase, step - busy, 0, blocks)
            if phase == 0:

                @pl.when(step < busy)
                def _():
                    kernel_grads(step)

                @pl.when((step >= busy) & (step < busy + blocks))
                def _():
                    tap_line.leaf(step - busy)

    @pl.when(last)
    def _():
        for away in range(1, line):
            take(away).wait_recv()
        left = factors[:, pl.ds(0, 8)].reshape(line * 8, chans)
        right = factors[:, pl.ds(8, 8)].reshape(line * 8, chans)
        left = jnp.concatenate(three_parts(left), axis=0).astype(bf16)
        right = jnp.concatenate([right, right, right], axis=0).astype(bf16)
        value = dot(left, right, contract_first)
        sums[pl.ds(0, half)] = value.reshape(half, chunk_rows, chans).astype(sums.dtype)
        for away in range(1, line):
            give(away).wait_send()

    @pl.loop(0, blocks)
    def _(k):
        tap_line.drain(k)

    @pl.loop(begin, 2 * half)
    def _(k):
        main.drain(k)

    @pl.when(section > 0)
    def _():
        @pl.loop(0, images)
        def _(n):
            hand_over(n).wait_send()


def finish(sums, taps, grad_first, grad_second, grad_small, grad_large):
    chans = sums.shape[1]
    grad_second[...] = sums[pl.ds(0, chans)].astype(f32)
    grad_first[...] = sums[pl.ds(chans, chans)].astype(f32)
    for block in range(chans // LANES):
        where = pl.ds(block * LANES, LANES)
        for tap in range(25):
            grad_large[tap, :, where] = taps[block, pl.ds(tap, 1)]
        for tap in range(9):
            grad_small[tap, :, where] = taps[block, pl.ds(TAP_SMALL + tap, 1)]


def per_device(
    activations, depth_small, point_first, depth_large, point_second, head_weight, offsets, labels
):
    x = activations[0]
    images, height, width, chans = x.shape
    rows = height * width
    blocks = chans // LANES
    vmem = pl.BlockSpec(memory_space=pltpu.VMEM)
    smem = pl.BlockSpec(memory_space=pltpu.SMEM)

    line = lax.axis_size("dp")
    link = bf16 if line <= 4 else f32
    chunks = 2 * chans // CHUNK_ROWS

    def line_scratch(count, length, wide, dtype):
        return [pltpu.VMEM((count, length, wide), dtype)] * 3 + [
            pltpu.SemaphoreType.DMA((6, count))
        ]

    sums, tap_sums = pl.pallas_call(
        kernel,
        out_shape=(
            jax.ShapeDtypeStruct((chunks, CHUNK_ROWS, chans), link),
            jax.ShapeDtypeStruct((blocks, TAP_ROWS, LANES), f32),
        ),
        in_specs=[smem, smem] + [vmem] * 6,
        out_specs=(vmem,) * 2,
        scratch_shapes=[
            pltpu.VMEM((images, rows, chans), bf16),
            pltpu.VMEM((images, rows, chans), bf16),
            pltpu.VMEM((images, rows, chans), bf16),
            pltpu.VMEM((images, rows, chans), bf16),
            pltpu.VMEM((images, rows, chans), bf16),
            pltpu.VMEM((images, rows, chans), bf16),
            pltpu.VMEM((rows, chans), f32),
            pltpu.VMEM((5, height + 4, width, LANES), f32),
            pltpu.VMEM((3, height + 2, width, LANES), f32),
            pltpu.VMEM((images, blocks, 5, height + 4, width, LANES), f32),
            pltpu.VMEM((images, blocks, 3, height + 2, width, LANES), f32),
            pltpu.VMEM((images, 8, chans), f32),
            pltpu.VMEM((9, 8, LANES), f32),
            pltpu.VMEM((25, 8, LANES), f32),
            pltpu.VMEM((blocks, TAP_ROWS, LANES), f32),
            pltpu.VMEM((2 * chans, chans), f32),
            pltpu.VMEM((images, MASK_ROWS, chans), f32),
            pltpu.VMEM((MASK_ROWS, chans), f32),
            pltpu.VMEM((rows, chans), f32),
            pltpu.VMEM((MASK_ROWS, rows), bf16),
            pltpu.VMEM((line, 16, chans), f32),
            pltpu.SemaphoreType.DMA((images,)),
            pltpu.SemaphoreType.DMA((images,)),
            pltpu.SemaphoreType.DMA((line,)),
            pltpu.SemaphoreType.DMA((line,)),
            *line_scratch(chunks, CHUNK_ROWS, chans, link),
            *line_scratch(blocks, TAP_ROWS, LANES, f32),
        ],
        compiler_params=pltpu.CompilerParams(
            collective_id=0, has_side_effects=True, vmem_limit_bytes=56 << 20
        ),
        name="sections",
    )(
        offsets,
        labels,
        x,
        depth_small[0].reshape(9, 1, chans),
        point_first[0],
        depth_large[0].reshape(25, 1, chans),
        point_second[0],
        head_weight,
    )
    sum_first, sum_second, sum_small, sum_large = pl.pallas_call(
        finish,
        out_shape=(
            jax.ShapeDtypeStruct((chans, chans), f32),
            jax.ShapeDtypeStruct((chans, chans), f32),
            jax.ShapeDtypeStruct((9, 1, chans), f32),
            jax.ShapeDtypeStruct((25, 1, chans), f32),
        ),
        in_specs=[vmem] * 2,
        out_specs=(vmem,) * 4,
        compiler_params=pltpu.CompilerParams(vmem_limit_bytes=16 << 20),
        name="finish",
    )(sums.reshape(2 * chans, chans), tap_sums)
    return (
        sum_first[None],
        sum_second[None],
        sum_small.reshape(1, 3, 3, chans),
        sum_large.reshape(1, 5, 5, chans),
    )


def solution(mesh):
    placed = (
        P("section", ("groups", "dp"), None, None, None),
        P("section", None, None, None),
        P("section", None, None),
        P("section", None, None, None),
        P("section", None, None),
        P(),
        P(("groups", "dp")),
        P(("groups", "dp")),
    )
    return jax.shard_map(
        per_device,
        mesh=mesh,
        in_specs=placed,
        out_specs=(
            P("section", "groups", None),
            P("section", "groups", None),
            P("section", "groups", None, None),
            P("section", "groups", None, None),
        ),
        check_vma=False,
    )
```

```python
import jax
import jax.numpy as jnp
from jax import lax
from jax.experimental import pallas as pl
from jax.experimental.pallas import tpu as pltpu
from jax.sharding import PartitionSpec as P

BAND = 4
LOSS_SCALE = 64.0
LANES = 128
CHUNK_ROWS = 32
LAG = 4
TAP_ROWS = 40
TAP_SMALL = 25
MASK_ROWS = 32
PIECES = 4
f32 = jnp.float32
bf16 = jnp.bfloat16
contract_last = (((1,), (1,)), ((), ()))
contract_first = (((0,), (0,)), ((), ()))


def dot(a, b, dims=(((1,), (0,)), ((), ()))):
    return lax.dot_general(a, b, dims, preferred_element_type=f32)


def split_dot(values, matrix, dims):
    rows = values.shape[0]
    high = values.astype(bf16).astype(f32)
    rest = values - high
    mid = rest.astype(bf16).astype(f32)
    low = (rest - mid).astype(bf16).astype(f32)
    parts = jnp.concatenate([high, mid, low, jnp.zeros_like(low)], axis=0).astype(bf16)
    out = dot(parts, matrix, dims)
    return out[:rows] + out[rows : 2 * rows] + out[2 * rows : 3 * rows]


def three_parts(values):
    high = values.astype(bf16).astype(f32)
    rest = values - high
    mid = rest.astype(bf16).astype(f32)
    return high, mid, (rest - mid).astype(bf16).astype(f32)


class Line:
    def __init__(self, place, line, refs, get, done=None):
        self.place, self.line = place, line
        self.out, self.inner, self.across, self.final, self.sems = refs
        self.get, self.done = get, done
        self.left = place < line // 2
        self.outer = jnp.where(self.left, place, line - 1 - place)
        self.deep = line // 2 - 1
        self.middle = self.outer == self.deep

    def copy(self, k, src, dst, lane, step):
        way = jnp.where(self.left, step, -step)
        return pltpu.make_async_remote_copy(
            src_ref=src.at[k],
            dst_ref=dst.at[k],
            send_sem=self.sems.at[lane, k],
            recv_sem=self.sems.at[3 + lane, k],
            device_id={"dp": jnp.clip(self.place + way, 0, self.line - 1)},
        )

    def inward(self, k):
        return self.copy(k, self.out, self.inner, 0, 1)

    def exchange(self, k):
        return self.copy(k, self.out, self.across, 1, 1)

    def outward(self, k):
        return self.copy(k, self.final, self.final, 2, -1)

    def advance(self, phase, step, first, chunks):
        lag, active, act = (
            (LAG * self.outer, True, self.gather),
            (LAG * (self.deep + 1), self.middle, self.total),
            (LAG * (2 * self.deep + 1 - self.outer), jnp.logical_not(self.middle), self.spread),
        )[phase]
        k = step - lag

        @pl.when(active & (k >= 0) & (k < chunks))
        def _():
            act(k + first)

    def gather(self, k):
        dtype = self.out.dtype
        end = self.outer == 0

        @pl.when(end)
        def _():
            self.out[k] = self.get(k).astype(dtype)

        @pl.when(jnp.logical_not(end))
        def _():
            self.inward(k).wait_recv()
            self.out[k] = (self.get(k) + self.inner[k].astype(f32)).astype(dtype)

        @pl.when(self.middle)
        def _():
            self.exchange(k).start()

        @pl.when(jnp.logical_not(self.middle))
        def _():
            self.inward(k).start()

    def total(self, k):
        self.exchange(k).wait_recv()
        value = self.out[k].astype(f32) + self.across[k].astype(f32)
        self.final[k] = value.astype(self.final.dtype)

        @pl.when(self.outer > 0)
        def _():
            self.outward(k).start()

        if self.done is not None:
            self.done(k)

    def spread(self, k):
        self.outward(k).wait_recv()

        @pl.when(self.outer > 0)
        def _():
            self.outward(k).start()

        if self.done is not None:
            self.done(k)

    def drain(self, k):
        @pl.when(self.middle)
        def _():
            self.exchange(k).wait_send()

        @pl.when(jnp.logical_not(self.middle))
        def _():
            self.inward(k).wait_send()

        @pl.when(self.outer > 0)
        def _():
            self.outward(k).wait_send()


def kernel(
    offsets, labels, x, k3, w1, k5, w2, head,
    sums, tap_sums,
    d1, a2, d2, gin, gp1, gout, tmp, s5f, s3f, s5g, s3g, pool, acc3, acc5, taps,
    grads, windows, k5_rows, spread5, push, factors,
    borrowed, send_sem, recv_sem, factor_send, factor_recv, lend_sems, *line_refs,
):
    section = lax.axis_index("section")
    count = lax.axis_size("section")
    images, height, width, chans = x.shape
    rows = height * width
    blocks = chans // LANES
    last = section == count - 1
    scale = 1.0 / rows

    barrier = pltpu.get_barrier_semaphore()

    @pl.when(section > 0)
    def _():
        pl.semaphore_signal(barrier, inc=1, device_id={"section": section - 1})

    @pl.when(section < count - 1)
    def _():
        pl.semaphore_signal(barrier, inc=1, device_id={"section": section + 1})

    place = lax.axis_index("dp")
    line = lax.axis_size("dp")

    for away in range(1, line):
        pl.semaphore_signal(barrier, inc=1, device_id={"dp": lax.rem(place + away, line)})

    lender = section == count - 3

    @pl.when(lender)
    def _():
        pl.semaphore_signal(barrier, inc=1, device_id={"section": jnp.minimum(section + 2, count - 1)})

    @pl.when(last & (count > 2))
    def _():
        pl.semaphore_signal(barrier, inc=1, device_id={"section": jnp.maximum(section - 2, 0)})

    def cols(block):
        return pl.ds(pl.multiple_of(block * LANES, LANES), LANES)

    col_index = lax.broadcasted_iota(jnp.int32, (1, width, LANES), 1)

    def shifted(value, by):
        if by == 0:
            return value
        moved = pltpu.roll(value, (-by) % width, axis=1)
        inside = (col_index + by >= 0) & (col_index + by < width)
        return jnp.where(inside, moved, 0.0)

    def fill(ref, value, size):
        radius = size // 2
        for tap in range(size):
            ref[tap, pl.ds(radius, height)] = shifted(value, tap - radius)

    def clear(ref, size):
        radius = size // 2
        zero = jnp.zeros((radius, width, LANES), f32)
        for tap in range(size):
            ref[tap, pl.ds(0, radius)] = zero
            ref[tap, pl.ds(radius + height, radius)] = zero

    def conv(ref, weights, size, block, flip):
        total = None
        for row_tap in range(size):
            for col_tap in range(size):
                r, c = row_tap, col_tap
                if flip:
                    r, c = size - 1 - r, size - 1 - c
                tap = row_tap * size + col_tap
                part = weights[tap, :, cols(block)] * ref[c, pl.ds(r, height)]
                total = part if total is None else total + part
        return total

    def kept(image):
        away = col_index - offsets[image]
        away = jnp.where(away < 0, away + width, away)
        return jnp.where((away < BAND) | (section > 0), 1.0, 0.0)

    def xin(image, block):
        return x[image, :, :, cols(block)].astype(f32) * kept(image)

    clear(s5f, 5)
    clear(s3f, 3)

    @pl.loop(0, images)
    def _(n):
        @pl.loop(0, blocks)
        def _(b):
            for ref, size in ((s5g, 5), (s3g, 3)):
                clear(ref.at[n, b], size)

    def window_mask():
        tap = lax.broadcasted_iota(jnp.int32, (MASK_ROWS, rows), 0)
        spot = lax.broadcasted_iota(jnp.int32, (MASK_ROWS, rows), 1)
        i, h = jnp.zeros_like(tap), jnp.zeros_like(spot)
        for step in range(1, 5):
            i = i + jnp.where(tap >= 5 * step, 1, 0)
        for step in range(1, height):
            h = h + jnp.where(spot >= width * step, 1, 0)
        down, along = h - i + 2, (spot - width * h) - (tap - 5 * i) + 2
        inside = (down >= 0) & (down < height) & (along >= 0) & (along < width) & (tap < 25)
        return jnp.where(inside, 1.0, 0.0)

    @pl.when(last)
    def _():
        mask = window_mask()
        push[...] = mask.astype(bf16)
        k5_rows[pl.ds(24, 8)] = jnp.zeros((8, chans), f32)
        for tap in range(25):
            k5_rows[pl.ds(tap, 1)] = k5[tap]
        parts = jnp.concatenate(three_parts(k5_rows[...]), axis=0).astype(bf16)
        masks = jnp.concatenate([mask, mask, mask], axis=0).astype(bf16)
        spread5[...] = dot(masks, parts, contract_first)

    @pl.loop(0, images)
    def _(n):
        @pl.loop(0, blocks)
        def _(b):
            value = xin(n, b)
            pool[n, :, cols(b)] = jnp.sum(value.reshape(rows // 8, 8, LANES), axis=0)
            fill(s3f, jnp.maximum(value, 0.0), 3)
            out = conv(s3f, k3, 3, b, False)
            d1[n, :, cols(b)] = out.reshape(rows, LANES).astype(bf16)

        a2[n] = jnp.maximum(dot(d1[n], w1[...]), 0.0).astype(bf16)

        @pl.when(last)
        def _():
            windows[n] = dot(push[...], a2[n])

    def second_depth(start, end):
        @pl.loop(start, end)
        def _(n):
            @pl.loop(0, blocks)
            def _(b):
                value = a2[n, :, cols(b)].astype(f32).reshape(height, width, LANES)
                fill(s5f, value, 5)
                out = conv(s5f, k5, 5, b, False).reshape(rows, LANES).astype(bf16)
                d2[n, :, cols(b)] = out

    late = section == count - 2

    early = jnp.where(late, images // 2, images)

    @pl.when(jnp.logical_not(last))
    def _():
        second_depth(0, early)

    classes = head.shape[0]

    @pl.when(last)
    def _():
        x_sums = [jnp.sum(pool[n], axis=0, keepdims=True) for n in range(images)]
        d2_sums = [
            jnp.sum(k5_rows[...] * windows[n], axis=0, keepdims=True) for n in range(images)
        ]
        twice = -(-2 * images // 8) * 8
        fill_rows = [jnp.zeros((twice - 2 * images, chans), f32)] if twice > 2 * images else []
        x_sum = jnp.concatenate(x_sums + x_sums + fill_rows, axis=0)
        d2_sum = jnp.concatenate(d2_sums + d2_sums + fill_rows, axis=0)
        pooled = (x_sum + split_dot(d2_sum, w2[...], (((1,), (0,)), ((), ())))) * scale
        rest = jnp.zeros((LANES - twice, chans), f32)
        wide = jnp.concatenate([pooled, rest], axis=0)
        high = wide.astype(bf16)
        mid = (wide - high.astype(f32)).astype(bf16)
        logits = dot(head[...], high, contract_last) + dot(head[...], mid, contract_last)
        class_index = lax.broadcasted_iota(jnp.int32, (classes, LANES), 0)
        lane = lax.broadcasted_iota(jnp.int32, (1, LANES), 1)
        label_row = jnp.full((1, LANES), -1, jnp.int32)
        for n in range(images):
            label_row = jnp.where((lane == n) | (lane == n + images), labels[n], label_row)
        dlog = LOSS_SCALE * (logits - jnp.where(class_index == label_row, 1.0, 0.0))
        high = dlog.astype(bf16).astype(f32)
        part = jnp.where(lane < images, high, dlog - high).astype(bf16)
        both = dot(part, head[...], contract_first)
        grad = ((both[:images] + both[images : 2 * images]) * scale).astype(bf16).astype(f32)
        pad = jnp.zeros((8 - images, chans), f32)
        factors[place, pl.ds(0, 8)] = jnp.concatenate([*d2_sums, pad], axis=0)
        factors[place, pl.ds(8, 8)] = jnp.concatenate([grad, pad], axis=0)
        wide = jnp.concatenate([grad, jnp.zeros((16 - images, chans), f32)], axis=0)
        tmp[pl.ds(0, 16)] = dot(wide.astype(bf16), w2[...], contract_last)
        for n in range(images):
            gin[n] = jnp.broadcast_to(grad[n : n + 1], (rows, chans)).astype(bf16)
        for n in range(images):
            back = tmp[pl.ds(n, 1)]
            if n == 0:
                total = back * windows[n]
            else:
                total = total + back * windows[n]
            live = a2[n].astype(f32) > 0
            gp1[n] = jnp.where(live, back * spread5[...], 0.0).astype(bf16)
        for b in range(blocks):
            taps[b, pl.ds(0, 25)] = total[:25, b * LANES : (b + 1) * LANES]

    def hand_over(n):
        return pltpu.make_async_remote_copy(
            src_ref=gout.at[n],
            dst_ref=gin.at[n],
            send_sem=send_sem.at[n],
            recv_sem=recv_sem.at[n],
            device_id={"section": jnp.maximum(section - 1, 0)},
        )

    pl.semaphore_wait(
        barrier,
        jnp.where(section > 0, 1, 0)
        + jnp.where(section < count - 1, 1, 0)
        + jnp.where(lender | (last & (count > 2)), 1, 0)
        + (line - 1),
    )

    def give(away):
        other = lax.rem(place + away, line)
        return pltpu.make_async_remote_copy(
            src_ref=factors.at[place],
            dst_ref=factors.at[place],
            send_sem=factor_send.at[away],
            recv_sem=factor_recv.at[away],
            device_id={"dp": other},
        )

    def take(away):
        other = lax.rem(place + line - away, line)
        return pltpu.make_async_remote_copy(
            src_ref=factors.at[other],
            dst_ref=factors.at[other],
            send_sem=factor_send.at[away],
            recv_sem=factor_recv.at[away],
            device_id={"dp": lax.rem(place + away, line)},
        )

    @pl.when(last)
    def _():
        for away in range(1, line):
            give(away).start()

    chunk_rows = CHUNK_ROWS
    half = chans // chunk_rows

    def rows_of(k):
        return pl.ds(pl.multiple_of(k * chunk_rows, chunk_rows), chunk_rows)

    def lend(k):
        return pltpu.make_async_remote_copy(
            src_ref=line_refs[0].at[k],
            dst_ref=borrowed.at[k],
            send_sem=lend_sems.at[0, k],
            recv_sem=lend_sems.at[1, k],
            device_id={"section": jnp.minimum(section + 2, count - 1)},
        )

    def give_back(k):
        return pltpu.make_async_remote_copy(
            src_ref=sums.at[k + 2 * half],
            dst_ref=sums.at[k],
            send_sem=lend_sems.at[2, k],
            recv_sem=lend_sems.at[3, k],
            device_id={"section": jnp.maximum(section - 2, 0)},
        )

    def own(k):
        @pl.when(k >= 2 * half)
        def _():
            lend(k - 2 * half).wait_recv()
            grads[rows_of(k)] = borrowed[k - 2 * half].astype(f32)

        return grads[rows_of(k)]

    def done(k):
        @pl.when(k >= 2 * half)
        def _():
            give_back(k - 2 * half).start()

    main = Line(place, line, [*line_refs[0:3], sums, line_refs[3]], own, done)
    tap_line = Line(place, line, [*line_refs[4:7], tap_sums, line_refs[7]], lambda k: taps[k])
    begin = jnp.where(last | lender, half, 0)
    finish_at = jnp.where(last & (count > 2), 3 * half, 2 * half)

    flat = (images * rows, chans)

    def weight_grads():
        @pl.when(jnp.logical_not(last))
        def _():
            left, right = d2[...].reshape(flat), gin[...].reshape(flat)
            grads[pl.ds(0, chans)] = dot(left, right, contract_first)

        @pl.when(lender)
        def _():
            @pl.loop(0, half)
            def _(k):
                main.out[k] = grads[rows_of(k)].astype(main.out.dtype)
                lend(k).start()

        left, right = d1[...].reshape(flat), gp1[...].reshape(flat)
        grads[pl.ds(chans, chans)] = dot(left, right, contract_first)

    @pl.loop(0, images)
    def _(n):
        @pl.when(jnp.logical_not(last))
        def _():
            hand_over(n).wait_recv()
            tmp[...] = dot(gin[n], w2[...], contract_last)

            @pl.loop(0, blocks)
            def _(b):
                shifts = s5g.at[n, b]
                fill(shifts, tmp[:, cols(b)].reshape(height, width, LANES), 5)
                back = conv(shifts, k5, 5, b, True).reshape(rows, LANES)
                live = a2[n, :, cols(b)].astype(f32) > 0
                gp1[n, :, cols(b)] = jnp.where(live, back, 0.0).astype(bf16)

        tmp[...] = dot(gp1[n], w1[...], contract_last)

        @pl.loop(0, blocks)
        def _(b):
            shifts = s3g.at[n, b]
            fill(shifts, tmp[:, cols(b)].reshape(height, width, LANES), 3)

            @pl.when(section > 0)
            def _():
                back = conv(shifts, k3, 3, b, True)
                back = jnp.where(xin(n, b) > 0, back, 0.0).reshape(rows, LANES)
                grad = gin[n, :, cols(b)].astype(f32) + back
                gout[n, :, cols(b)] = grad.astype(bf16)

        @pl.when(section > 0)
        def _():
            hand_over(n).start()

    @pl.when(late)
    def _():
        second_depth(images // 2, images)

    weight_grads()

    def kernel_grad(acc, value, ref, size):
        for row_tap in range(size):
            for col_tap in range(size):
                other = ref[size - 1 - col_tap, pl.ds(size - 1 - row_tap, height)]
                part = (value * other).reshape(rows // 8, 8, LANES)
                acc[row_tap * size + col_tap] += jnp.sum(part, axis=0)

    def kernel_grads(unit):
        b, n = unit // images, unit % images

        @pl.when(n == 0)
        def _():
            acc3[...] = jnp.zeros_like(acc3)
            acc5[...] = jnp.zeros_like(acc5)

        @pl.when(jnp.logical_not(last))
        def _():
            value = a2[n, :, cols(b)].astype(f32).reshape(height, width, LANES)
            kernel_grad(acc5, value, s5g.at[n, b], 5)

        kernel_grad(acc3, jnp.maximum(xin(n, b), 0.0), s3g.at[n, b], 3)

        @pl.when(n == images - 1)
        def _():
            @pl.when(jnp.logical_not(last))
            def _():
                taps[b, pl.ds(0, 25)] = jnp.sum(acc5[...], axis=1)

            taps[b, pl.ds(TAP_SMALL, 9)] = jnp.sum(acc3[...], axis=1)

    busy = blocks * images
    taps[:, pl.ds(32, 8)] = jnp.zeros((blocks, 8, LANES), f32)

    behind = LAG * (line - 1)

    @pl.loop(0, jnp.maximum(finish_at - begin, busy + blocks) + behind)
    def _(step):
        for phase in range(3):
            tap_line.advance(phase, step - busy, 0, blocks)
            main.advance(phase, step, begin, finish_at - begin)
            if phase == 0:

                @pl.when(step < busy)
                def _():
                    kernel_grads(step)

    @pl.when(last)
    def _():
        for away in range(1, line):
            take(away).wait_recv()
        left = factors[:, pl.ds(0, 8)].reshape(line * 8, chans)
        right = factors[:, pl.ds(8, 8)].reshape(line * 8, chans)
        left = jnp.concatenate(three_parts(left), axis=0).astype(bf16)
        right = jnp.concatenate([right, right, right], axis=0).astype(bf16)
        value = dot(left, right, contract_first)
        sums[pl.ds(0, half)] = value.reshape(half, chunk_rows, chans).astype(sums.dtype)
        for away in range(1, line):
            give(away).wait_send()

    @pl.loop(0, blocks)
    def _(k):
        tap_line.drain(k)

    @pl.loop(begin, finish_at)
    def _(k):
        main.drain(k)

    @pl.when(lender)
    def _():
        @pl.loop(0, half)
        def _(k):
            give_back(k).wait_recv()
            lend(k).wait_send()

    @pl.when(last & (count > 2))
    def _():
        @pl.loop(0, half)
        def _(k):
            give_back(k).wait_send()

    @pl.when(section > 0)
    def _():
        @pl.loop(0, images)
        def _(n):
            hand_over(n).wait_send()


def finish(
    sums, taps, grad_first, grad_second, grad_small, grad_large,
    narrow, wide, taps_in, small, large, in_sem, out_sem,
):
    pieces, length = narrow.shape[0], narrow.shape[1]
    per_output = pieces // 2
    loads = [
        pltpu.make_async_copy(sums.at[pl.ds(p * length, length)], narrow.at[p], in_sem.at[p])
        for p in range(pieces)
    ]
    stores = [
        pltpu.make_async_copy(
            wide.at[p],
            (grad_second, grad_first)[p // per_output].at[pl.ds(p % per_output * length, length)],
            out_sem.at[p],
        )
        for p in range(pieces)
    ]
    loads.append(pltpu.make_async_copy(taps, taps_in, in_sem.at[pieces]))
    stores.append(pltpu.make_async_copy(small, grad_small, out_sem.at[pieces]))
    stores.append(pltpu.make_async_copy(large, grad_large, out_sem.at[pieces + 1]))
    for load in loads:
        load.start()
    for p in range(pieces):
        loads[p].wait()
        wide[p] = narrow[p].astype(f32)
        stores[p].start()
    loads[pieces].wait()
    for block in range(taps_in.shape[0]):
        where = pl.ds(block * LANES, LANES)
        for tap in range(25):
            large[tap, :, where] = taps_in[block, pl.ds(tap, 1)]
        for tap in range(9):
            small[tap, :, where] = taps_in[block, pl.ds(TAP_SMALL + tap, 1)]
    stores[pieces].start()
    stores[pieces + 1].start()
    for store in stores:
        store.wait()


def per_device(
    activations, depth_small, point_first, depth_large, point_second, head_weight, offsets, labels
):
    x = activations[0]
    images, height, width, chans = x.shape
    rows = height * width
    blocks = chans // LANES
    vmem = pl.BlockSpec(memory_space=pltpu.VMEM)
    smem = pl.BlockSpec(memory_space=pltpu.SMEM)
    anywhere = pl.BlockSpec(memory_space=pl.ANY)

    line = lax.axis_size("dp")
    link = bf16 if line <= 4 else f32
    half = chans // CHUNK_ROWS
    slots = 3 * half

    def line_scratch(count, length, wide, dtype):
        return [pltpu.VMEM((count, length, wide), dtype)] * 3 + [
            pltpu.SemaphoreType.DMA((6, count))
        ]

    sums, tap_sums = pl.pallas_call(
        kernel,
        out_shape=(
            jax.ShapeDtypeStruct((slots, CHUNK_ROWS, chans), link),
            jax.ShapeDtypeStruct((blocks, TAP_ROWS, LANES), f32),
        ),
        in_specs=[smem, smem] + [vmem] * 6,
        out_specs=(vmem,) * 2,
        scratch_shapes=[
            pltpu.VMEM((images, rows, chans), bf16),
            pltpu.VMEM((images, rows, chans), bf16),
            pltpu.VMEM((images, rows, chans), bf16),
            pltpu.VMEM((images, rows, chans), bf16),
            pltpu.VMEM((images, rows, chans), bf16),
            pltpu.VMEM((images, rows, chans), bf16),
            pltpu.VMEM((rows, chans), f32),
            pltpu.VMEM((5, height + 4, width, LANES), f32),
            pltpu.VMEM((3, height + 2, width, LANES), f32),
            pltpu.VMEM((images, blocks, 5, height + 4, width, LANES), f32),
            pltpu.VMEM((images, blocks, 3, height + 2, width, LANES), f32),
            pltpu.VMEM((images, 8, chans), f32),
            pltpu.VMEM((9, 8, LANES), f32),
            pltpu.VMEM((25, 8, LANES), f32),
            pltpu.VMEM((blocks, TAP_ROWS, LANES), f32),
            pltpu.VMEM((3 * chans, chans), f32),
            pltpu.VMEM((images, MASK_ROWS, chans), f32),
            pltpu.VMEM((MASK_ROWS, chans), f32),
            pltpu.VMEM((rows, chans), f32),
            pltpu.VMEM((MASK_ROWS, rows), bf16),
            pltpu.VMEM((line, 16, chans), f32),
            pltpu.VMEM((half, CHUNK_ROWS, chans), link),
            pltpu.SemaphoreType.DMA((images,)),
            pltpu.SemaphoreType.DMA((images,)),
            pltpu.SemaphoreType.DMA((line,)),
            pltpu.SemaphoreType.DMA((line,)),
            pltpu.SemaphoreType.DMA((4, half)),
            *line_scratch(slots, CHUNK_ROWS, chans, link),
            *line_scratch(blocks, TAP_ROWS, LANES, f32),
        ],
        compiler_params=pltpu.CompilerParams(
            collective_id=0, has_side_effects=True, vmem_limit_bytes=56 << 20
        ),
        name="sections",
    )(
        offsets,
        labels,
        x,
        depth_small[0].reshape(9, 1, chans),
        point_first[0],
        depth_large[0].reshape(25, 1, chans),
        point_second[0],
        head_weight,
    )
    sum_first, sum_second, sum_small, sum_large = pl.pallas_call(
        finish,
        out_shape=(
            jax.ShapeDtypeStruct((chans, chans), f32),
            jax.ShapeDtypeStruct((chans, chans), f32),
            jax.ShapeDtypeStruct((9, 1, chans), f32),
            jax.ShapeDtypeStruct((25, 1, chans), f32),
        ),
        in_specs=[anywhere] * 2,
        out_specs=(anywhere,) * 4,
        scratch_shapes=[
            pltpu.VMEM((PIECES, 2 * chans // PIECES, chans), link),
            pltpu.VMEM((PIECES, 2 * chans // PIECES, chans), f32),
            pltpu.VMEM((blocks, TAP_ROWS, LANES), f32),
            pltpu.VMEM((9, 1, chans), f32),
            pltpu.VMEM((25, 1, chans), f32),
            pltpu.SemaphoreType.DMA((PIECES + 1,)),
            pltpu.SemaphoreType.DMA((PIECES + 2,)),
        ],
        compiler_params=pltpu.CompilerParams(vmem_limit_bytes=60 << 20),
        name="finish",
    )(sums.reshape(3 * chans, chans), tap_sums)
    return (
        sum_first[None],
        sum_second[None],
        sum_small.reshape(1, 3, 3, chans),
        sum_large.reshape(1, 5, 5, chans),
    )


def solution(mesh):
    placed = (
        P("section", ("groups", "dp"), None, None, None),
        P("section", None, None, None),
        P("section", None, None),
        P("section", None, None, None),
        P("section", None, None),
        P(),
        P(("groups", "dp")),
        P(("groups", "dp")),
    )
    return jax.shard_map(
        per_device,
        mesh=mesh,
        in_specs=placed,
        out_specs=(
            P("section", "groups", None),
            P("section", "groups", None),
            P("section", "groups", None, None),
            P("section", "groups", None, None),
        ),
        check_vma=False,
    )
```

```python
import jax
import jax.numpy as jnp
from jax import lax
from jax.experimental import pallas as pl
from jax.experimental.pallas import tpu as pltpu
from jax.sharding import PartitionSpec as P

BAND = 4
LOSS_SCALE = 64.0
LANES = 128
CHUNK_ROWS = 64
LAG = 4
AHEAD = 4
TAP_ROWS = 40
TAP_SMALL = 25
MASK_ROWS = 32
PIECES = 4
GROUP = 4
EDGE = 8
f32 = jnp.float32
bf16 = jnp.bfloat16
contract_last = (((1,), (1,)), ((), ()))
contract_first = (((0,), (0,)), ((), ()))


def dot(a, b, dims=(((1,), (0,)), ((), ()))):
    return lax.dot_general(a, b, dims, preferred_element_type=f32)


def split_dot(values, matrix, dims):
    rows = values.shape[0]
    high = values.astype(bf16).astype(f32)
    rest = values - high
    mid = rest.astype(bf16).astype(f32)
    low = (rest - mid).astype(bf16).astype(f32)
    parts = jnp.concatenate([high, mid, low, jnp.zeros_like(low)], axis=0).astype(bf16)
    out = dot(parts, matrix, dims)
    return out[:rows] + out[rows : 2 * rows] + out[2 * rows : 3 * rows]


def three_parts(values):
    high = values.astype(bf16).astype(f32)
    rest = values - high
    mid = rest.astype(bf16).astype(f32)
    return high, mid, (rest - mid).astype(bf16).astype(f32)


class Line:
    def __init__(self, place, line, refs, get, done=None):
        self.place, self.line = place, line
        self.out, self.inner, self.across, self.final, self.sems = refs
        self.get, self.done = get, done
        self.left = place < line // 2
        self.outer = jnp.where(self.left, place, line - 1 - place)
        self.deep = line // 2 - 1
        self.middle = self.outer == self.deep

    def copy(self, k, src, dst, lane, step):
        way = jnp.where(self.left, step, -step)
        return pltpu.make_async_remote_copy(
            src_ref=src.at[k],
            dst_ref=dst.at[k],
            send_sem=self.sems.at[lane, k],
            recv_sem=self.sems.at[3 + lane, k],
            device_id={"dp": jnp.clip(self.place + way, 0, self.line - 1)},
        )

    def inward(self, k):
        return self.copy(k, self.out, self.inner, 0, 1)

    def exchange(self, k):
        return self.copy(k, self.out, self.across, 1, 1)

    def outward(self, k):
        return self.copy(k, self.final, self.final, 2, -1)

    def advance(self, phase, step, first, chunks, sent=0):
        lag, active, act = (
            (LAG * self.outer, True, self.gather),
            (LAG * (self.deep + 1), self.middle, self.total),
            (LAG * (2 * self.deep + 1 - self.outer), jnp.logical_not(self.middle), self.spread),
        )[phase]
        k = step - lag

        if phase == 0:
            active = (self.outer > 0) | (k + first >= sent)

        @pl.when(active & (k >= 0) & (k < chunks))
        def _():
            act(k + first)

    def gather(self, k):
        dtype = self.out.dtype
        end = self.outer == 0

        @pl.when(end)
        def _():
            self.out[k] = self.get(k).astype(dtype)

        @pl.when(jnp.logical_not(end))
        def _():
            self.inward(k).wait_recv()
            self.out[k] = (self.get(k) + self.inner[k].astype(f32)).astype(dtype)

        @pl.when(self.middle)
        def _():
            self.exchange(k).start()

        @pl.when(jnp.logical_not(self.middle))
        def _():
            self.inward(k).start()

    def total(self, k):
        self.exchange(k).wait_recv()
        value = self.out[k].astype(f32) + self.across[k].astype(f32)
        self.final[k] = value.astype(self.final.dtype)

        @pl.when(self.outer > 0)
        def _():
            self.outward(k).start()

        if self.done is not None:
            self.done(k)

    def spread(self, k):
        self.outward(k).wait_recv()

        @pl.when(self.outer > 0)
        def _():
            self.outward(k).start()

        if self.done is not None:
            self.done(k)

    def drain(self, k):
        @pl.when(self.middle)
        def _():
            self.exchange(k).wait_send()

        @pl.when(jnp.logical_not(self.middle))
        def _():
            self.inward(k).wait_send()

        @pl.when(self.outer > 0)
        def _():
            self.outward(k).wait_send()


def kernel(
    offsets, labels, x, k3, w1, k5, w2, head,
    sums, tap_sums,
    d1, a2, d2, gin, gp1, gout, tmp, s5f, s3f, s5g, s3g, pool, acc3, acc5, taps,
    grads, windows, k5_rows, spread5, push, factors,
    borrowed, send_sem, recv_sem, factor_send, factor_recv, lend_sems, *line_refs,
):
    section = lax.axis_index("section")
    count = lax.axis_size("section")
    images, height, width, chans = x.shape
    rows = height * width
    blocks = chans // LANES
    last = section == count - 1
    scale = 1.0 / rows

    barrier = pltpu.get_barrier_semaphore()

    @pl.when(section > 0)
    def _():
        pl.semaphore_signal(barrier, inc=1, device_id={"section": section - 1})

    @pl.when(section < count - 1)
    def _():
        pl.semaphore_signal(barrier, inc=1, device_id={"section": section + 1})

    place = lax.axis_index("dp")
    line = lax.axis_size("dp")

    for away in range(1, line):
        pl.semaphore_signal(barrier, inc=1, device_id={"dp": lax.rem(place + away, line)})

    lender = section == count - 3

    @pl.when(lender)
    def _():
        pl.semaphore_signal(barrier, inc=1, device_id={"section": jnp.minimum(section + 2, count - 1)})

    @pl.when(last & (count > 2))
    def _():
        pl.semaphore_signal(barrier, inc=1, device_id={"section": jnp.maximum(section - 2, 0)})

    def cols(block):
        return pl.ds(pl.multiple_of(block * LANES, LANES), LANES)

    col_index = lax.broadcasted_iota(jnp.int32, (1, width, LANES), 1)

    def fill(ref, value, size):
        ref[pl.ds(size // 2, height), pl.ds(EDGE, width)] = value

    def clear(ref, size):
        radius = size // 2
        side = jnp.zeros((height + 2 * radius, EDGE, LANES), f32)
        ref[:, pl.ds(0, EDGE)] = side
        ref[:, pl.ds(EDGE + width, EDGE)] = side
        zero = jnp.zeros((radius, width, LANES), f32)
        ref[pl.ds(0, radius), pl.ds(EDGE, width)] = zero
        ref[pl.ds(radius + height, radius), pl.ds(EDGE, width)] = zero

    flat_group = GROUP * width

    def conv(ref, weights, size, block, flip, put):
        for start in range(0, height, GROUP):
            total = None
            for c in range(size):
                moved = ref[pl.ds(start, GROUP + size - 1), pl.ds(EDGE + c - size // 2, width)]
                for r in range(size):
                    tap = r * size + c
                    tap = size * size - 1 - tap if flip else tap
                    part = weights[tap, :, cols(block)] * moved[r : r + GROUP]
                    total = part if total is None else total + part
            put(pl.ds(start, GROUP), pl.ds(start * width, flat_group), total.reshape(flat_group, LANES))

    def kept(image):
        away = col_index - offsets[image]
        away = jnp.where(away < 0, away + width, away)
        return jnp.where((away < BAND) | (section > 0), 1.0, 0.0)

    def xin(image, block, some=slice(None)):
        return x[image, some, :, cols(block)].astype(f32) * kept(image)

    clear(s5f, 5)
    clear(s3f, 3)

    acc5[...] = jnp.zeros_like(acc5)
    acc3[...] = jnp.zeros_like(acc3)

    @pl.loop(0, images)
    def _(n):
        @pl.loop(0, blocks)
        def _(b):
            clear(s3g.at[n, b], 3)

            @pl.when(jnp.logical_not(last))
            def _():
                clear(s5g.at[n, b], 5)

    def window_mask():
        tap = lax.broadcasted_iota(jnp.int32, (MASK_ROWS, rows), 0)
        spot = lax.broadcasted_iota(jnp.int32, (MASK_ROWS, rows), 1)
        i, h = jnp.zeros_like(tap), jnp.zeros_like(spot)
        for step in range(1, 5):
            i = i + jnp.where(tap >= 5 * step, 1, 0)
        for step in range(1, height):
            h = h + jnp.where(spot >= width * step, 1, 0)
        down, along = h - i + 2, (spot - width * h) - (tap - 5 * i) + 2
        inside = (down >= 0) & (down < height) & (along >= 0) & (along < width) & (tap < 25)
        return jnp.where(inside, 1.0, 0.0)

    @pl.when(last)
    def _():
        mask = window_mask()
        push[...] = mask.astype(bf16)
        k5_rows[pl.ds(24, 8)] = jnp.zeros((8, chans), f32)
        for tap in range(25):
            k5_rows[pl.ds(tap, 1)] = k5[tap]
        parts = jnp.concatenate(three_parts(k5_rows[...]), axis=0).astype(bf16)
        masks = jnp.concatenate([mask, mask, mask], axis=0).astype(bf16)
        spread5[...] = dot(masks, parts, contract_first)

    @pl.loop(0, images)
    def _(n):
        @pl.loop(0, blocks)
        def _(b):
            value = xin(n, b)
            pool[n, :, cols(b)] = jnp.sum(value.reshape(rows // 8, 8, LANES), axis=0)
            fill(s3f, jnp.maximum(value, 0.0), 3)

            def put(_, where, out):
                d1[n, where, cols(b)] = out.astype(bf16)

            conv(s3f, k3, 3, b, False, put)

    flat = (images * rows, chans)
    a2[...] = jnp.maximum(dot(d1[...].reshape(flat), w1[...]), 0.0).astype(bf16).reshape(a2.shape)

    @pl.when(last)
    def _():
        for n in range(images):
            windows[n] = dot(push[...], a2[n])

    def second_depth(start, end):
        @pl.loop(start, end)
        def _(n):
            @pl.loop(0, blocks)
            def _(b):
                value = a2[n, :, cols(b)].astype(f32).reshape(height, width, LANES)
                fill(s5f, value, 5)

                def put(_, where, out):
                    d2[n, where, cols(b)] = out.astype(bf16)

                conv(s5f, k5, 5, b, False, put)

    late = section == count - 2

    early = jnp.where(late, images // 2, images)

    @pl.when(jnp.logical_not(last))
    def _():
        second_depth(0, early)

    classes = head.shape[0]

    @pl.when(last)
    def _():
        x_sums = [jnp.sum(pool[n], axis=0, keepdims=True) for n in range(images)]
        d2_sums = [
            jnp.sum(k5_rows[...] * windows[n], axis=0, keepdims=True) for n in range(images)
        ]
        twice = -(-2 * images // 8) * 8
        fill_rows = [jnp.zeros((twice - 2 * images, chans), f32)] if twice > 2 * images else []
        x_sum = jnp.concatenate(x_sums + x_sums + fill_rows, axis=0)
        d2_sum = jnp.concatenate(d2_sums + d2_sums + fill_rows, axis=0)
        pooled = (x_sum + split_dot(d2_sum, w2[...], (((1,), (0,)), ((), ())))) * scale
        rest = jnp.zeros((LANES - twice, chans), f32)
        wide = jnp.concatenate([pooled, rest], axis=0)
        high = wide.astype(bf16)
        mid = (wide - high.astype(f32)).astype(bf16)
        logits = dot(head[...], high, contract_last) + dot(head[...], mid, contract_last)
        class_index = lax.broadcasted_iota(jnp.int32, (classes, LANES), 0)
        lane = lax.broadcasted_iota(jnp.int32, (1, LANES), 1)
        label_row = jnp.full((1, LANES), -1, jnp.int32)
        for n in range(images):
            label_row = jnp.where((lane == n) | (lane == n + images), labels[n], label_row)
        dlog = LOSS_SCALE * (logits - jnp.where(class_index == label_row, 1.0, 0.0))
        high = dlog.astype(bf16).astype(f32)
        part = jnp.where(lane < images, high, dlog - high).astype(bf16)
        both = dot(part, head[...], contract_first)
        grad = ((both[:images] + both[images : 2 * images]) * scale).astype(bf16).astype(f32)
        pad = jnp.zeros((8 - images, chans), f32)
        factors[place, pl.ds(0, 8)] = jnp.concatenate([*d2_sums, pad], axis=0)
        factors[place, pl.ds(8, 8)] = jnp.concatenate([grad, pad], axis=0)
        wide = jnp.concatenate([grad, jnp.zeros((16 - images, chans), f32)], axis=0)
        tmp[pl.ds(0, 16)] = dot(wide.astype(bf16), w2[...], contract_last)
        for n in range(images):
            gin[n] = jnp.broadcast_to(grad[n : n + 1], (rows, chans)).astype(bf16)
        for n in range(images):
            back = tmp[pl.ds(n, 1)]
            if n == 0:
                total = back * windows[n]
            else:
                total = total + back * windows[n]
            live = a2[n].astype(f32) > 0
            gp1[n] = jnp.where(live, back * spread5[...], 0.0).astype(bf16)
        for b in range(blocks):
            taps[b, pl.ds(0, 25)] = total[:25, b * LANES : (b + 1) * LANES]

    def hand_over(n):
        return pltpu.make_async_remote_copy(
            src_ref=gout.at[n],
            dst_ref=gin.at[n],
            send_sem=send_sem.at[n],
            recv_sem=recv_sem.at[n],
            device_id={"section": jnp.maximum(section - 1, 0)},
        )

    pl.semaphore_wait(
        barrier,
        jnp.where(section > 0, 1, 0)
        + jnp.where(section < count - 1, 1, 0)
        + jnp.where(lender | (last & (count > 2)), 1, 0)
        + (line - 1),
    )

    def give(away):
        other = lax.rem(place + away, line)
        return pltpu.make_async_remote_copy(
            src_ref=factors.at[place],
            dst_ref=factors.at[place],
            send_sem=factor_send.at[away],
            recv_sem=factor_recv.at[away],
            device_id={"dp": other},
        )

    def take(away):
        other = lax.rem(place + line - away, line)
        return pltpu.make_async_remote_copy(
            src_ref=factors.at[other],
            dst_ref=factors.at[other],
            send_sem=factor_send.at[away],
            recv_sem=factor_recv.at[away],
            device_id={"dp": lax.rem(place + away, line)},
        )

    @pl.when(last)
    def _():
        for away in range(1, line):
            give(away).start()

    chunk_rows = CHUNK_ROWS
    half = chans // chunk_rows

    def rows_of(k):
        return pl.ds(pl.multiple_of(k * chunk_rows, chunk_rows), chunk_rows)

    def lend(k):
        return pltpu.make_async_remote_copy(
            src_ref=line_refs[0].at[k],
            dst_ref=borrowed.at[k],
            send_sem=lend_sems.at[0, k],
            recv_sem=lend_sems.at[1, k],
            device_id={"section": jnp.minimum(section + 2, count - 1)},
        )

    def give_back(k):
        return pltpu.make_async_remote_copy(
            src_ref=sums.at[k + 2 * half],
            dst_ref=sums.at[k],
            send_sem=lend_sems.at[2, k],
            recv_sem=lend_sems.at[3, k],
            device_id={"section": jnp.maximum(section - 2, 0)},
        )

    def own(k):
        @pl.when(k >= 2 * half)
        def _():
            lend(k - 2 * half).wait_recv()
            grads[rows_of(k)] = borrowed[k - 2 * half].astype(f32)

        return grads[rows_of(k)]

    def done(k):
        @pl.when(k >= 2 * half)
        def _():
            give_back(k - 2 * half).start()

    main = Line(place, line, [*line_refs[0:3], sums, line_refs[3]], own, done)
    tap_line = Line(place, line, [*line_refs[4:7], tap_sums, line_refs[7]], lambda k: taps[k])
    begin = jnp.where(last | lender, half, 0)
    finish_at = jnp.where(last & (count > 2), 3 * half, 2 * half)

    def kernel_grad(acc, value, ref, size):
        for c in range(size):
            sums_of = [None] * size
            for start in range(0, height, GROUP):
                left = value(pl.ds(start, GROUP), pl.ds(start * width, flat_group))
                moved = ref[
                    pl.ds(start, GROUP + size - 1), pl.ds(EDGE + size - 1 - c - size // 2, width)
                ]
                for r in range(size):
                    part = left * moved[size - 1 - r : size - 1 - r + GROUP]
                    part = jnp.sum(part.reshape(flat_group // 8, 8, LANES), axis=0)
                    sums_of[r] = part if sums_of[r] is None else sums_of[r] + part
            for r in range(size):
                acc[r * size + c] += sums_of[r]

    def kernel_grads(n, b):
        def second_value(_, where):
            return a2[n, where, cols(b)].astype(f32).reshape(GROUP, width, LANES)

        def first_value(some, _):
            return jnp.maximum(xin(n, b, some), 0.0)

        @pl.when(jnp.logical_not(last))
        def _():
            kernel_grad(acc5.at[b], second_value, s5g.at[n, b], 5)

        kernel_grad(acc3.at[b], first_value, s3g.at[n, b], 3)

        @pl.when(n == images - 1)
        def _():
            @pl.when(jnp.logical_not(last))
            def _():
                taps[b, pl.ds(0, 25)] = jnp.sum(acc5[b], axis=1)

            taps[b, pl.ds(TAP_SMALL, 9)] = jnp.sum(acc3[b], axis=1)

    waits = section < count - 2

    def product(at, left, right, start, end):
        shape = ((end - start) * rows, chans)
        left = left[pl.ds(start, end - start)].reshape(shape)
        right = right[pl.ds(start, end - start)].reshape(shape)
        part = dot(left, right, contract_first)
        if start == 0:
            grads[pl.ds(at, chans)] = part
        else:
            grads[pl.ds(at, chans)] += part

    def closing(at, left, right):
        @pl.when(waits)
        def _():
            product(at, left, right, images - 1, images)

        @pl.when(jnp.logical_not(waits))
        def _():
            product(at, left, right, 0, images)

    def weight_grads():
        @pl.when(jnp.logical_not(last))
        def _():
            closing(0, d2, gin)

            @pl.when((main.outer == 0) & jnp.logical_not(lender))
            def _():
                @pl.loop(0, AHEAD)
                def _(k):
                    main.gather(k)

        @pl.when(lender)
        def _():
            @pl.loop(0, half)
            def _(k):
                main.out[k] = grads[rows_of(k)].astype(main.out.dtype)
                lend(k).start()

        closing(chans, d1, gp1)

    @pl.loop(0, images)
    def _(n):
        @pl.when(jnp.logical_not(last))
        def _():
            hand_over(n).wait_recv()
            tmp[...] = dot(gin[n], w2[...], contract_last)

            @pl.loop(0, blocks)
            def _(b):
                shifts = s5g.at[n, b]
                fill(shifts, tmp[:, cols(b)].reshape(height, width, LANES), 5)

                def put(_, where, back):
                    live = a2[n, where, cols(b)].astype(f32) > 0
                    gp1[n, where, cols(b)] = jnp.where(live, back, 0.0).astype(bf16)

                conv(shifts, k5, 5, b, True, put)

        tmp[...] = dot(gp1[n], w1[...], contract_last)

        @pl.loop(0, blocks)
        def _(b):
            shifts = s3g.at[n, b]
            fill(shifts, tmp[:, cols(b)].reshape(height, width, LANES), 3)

            @pl.when(section > 0)
            def _():
                def put(some, where, back):
                    live = xin(n, b, some).reshape(flat_group, LANES) > 0
                    grad = gin[n, where, cols(b)].astype(f32) + jnp.where(live, back, 0.0)
                    gout[n, where, cols(b)] = grad.astype(bf16)

                conv(shifts, k3, 3, b, True, put)

        @pl.when(section > 0)
        def _():
            hand_over(n).start()

        @pl.when(waits & (n == images - 2))
        def _():
            product(0, d2, gin, 0, images - 1)
            product(chans, d1, gp1, 0, images - 1)

    @pl.when(late)
    def _():
        second_depth(images // 2, images)

    weight_grads()

    busy = blocks * images
    taps[:, pl.ds(32, 8)] = jnp.zeros((blocks, 8, LANES), f32)

    behind = LAG * (line - 1)
    sent = jnp.where(last | lender, 0, AHEAD)

    @pl.loop(0, jnp.maximum(finish_at - begin, busy + blocks) + behind)
    def _(step):
        for phase in range(3):
            tap_line.advance(phase, step - (busy - blocks + 1), 0, blocks)
            main.advance(phase, step, begin, finish_at - begin, sent)
            if phase == 0:

                @pl.when(step < busy)
                def _():
                    kernel_grads(step // blocks, step % blocks)

    @pl.when(last)
    def _():
        for away in range(1, line):
            take(away).wait_recv()
        left = factors[:, pl.ds(0, 8)].reshape(line * 8, chans)
        right = factors[:, pl.ds(8, 8)].reshape(line * 8, chans)
        left = jnp.concatenate(three_parts(left), axis=0).astype(bf16)
        right = jnp.concatenate([right, right, right], axis=0).astype(bf16)
        value = dot(left, right, contract_first)
        sums[pl.ds(0, half)] = value.reshape(half, chunk_rows, chans).astype(sums.dtype)
        for away in range(1, line):
            give(away).wait_send()

    @pl.loop(0, blocks)
    def _(k):
        tap_line.drain(k)

    @pl.loop(begin, finish_at)
    def _(k):
        main.drain(k)

    @pl.when(lender)
    def _():
        @pl.loop(0, half)
        def _(k):
            give_back(k).wait_recv()
            lend(k).wait_send()

    @pl.when(last & (count > 2))
    def _():
        @pl.loop(0, half)
        def _(k):
            give_back(k).wait_send()

    @pl.when(section > 0)
    def _():
        @pl.loop(0, images)
        def _(n):
            hand_over(n).wait_send()


def finish(
    sums, taps, grad_first, grad_second, grad_small, grad_large,
    narrow, wide, taps_in, small, large, in_sem, out_sem,
):
    pieces, length = narrow.shape[0], narrow.shape[1]
    per_output = pieces // 2
    loads = [
        pltpu.make_async_copy(sums.at[pl.ds(p * length, length)], narrow.at[p], in_sem.at[p])
        for p in range(pieces)
    ]
    stores = [
        pltpu.make_async_copy(
            wide.at[p],
            (grad_second, grad_first)[p // per_output].at[pl.ds(p % per_output * length, length)],
            out_sem.at[p],
        )
        for p in range(pieces)
    ]
    loads.append(pltpu.make_async_copy(taps, taps_in, in_sem.at[pieces]))
    stores.append(pltpu.make_async_copy(small, grad_small, out_sem.at[pieces]))
    stores.append(pltpu.make_async_copy(large, grad_large, out_sem.at[pieces + 1]))
    for load in loads:
        load.start()
    for p in range(pieces):
        loads[p].wait()
        wide[p] = narrow[p].astype(f32)
        stores[p].start()
    loads[pieces].wait()
    for block in range(taps_in.shape[0]):
        where = pl.ds(block * LANES, LANES)
        for tap in range(25):
            large[tap, :, where] = taps_in[block, pl.ds(tap, 1)]
        for tap in range(9):
            small[tap, :, where] = taps_in[block, pl.ds(TAP_SMALL + tap, 1)]
    stores[pieces].start()
    stores[pieces + 1].start()
    for store in stores:
        store.wait()


def per_device(
    activations, depth_small, point_first, depth_large, point_second, head_weight, offsets, labels
):
    x = activations[0]
    images, height, width, chans = x.shape
    rows = height * width
    blocks = chans // LANES
    vmem = pl.BlockSpec(memory_space=pltpu.VMEM)
    smem = pl.BlockSpec(memory_space=pltpu.SMEM)
    anywhere = pl.BlockSpec(memory_space=pl.ANY)

    padded = width + 2 * EDGE
    line = lax.axis_size("dp")
    link = bf16 if line <= 4 else f32
    half = chans // CHUNK_ROWS
    slots = 3 * half

    def line_scratch(count, length, wide, dtype):
        return [pltpu.VMEM((count, length, wide), dtype)] * 3 + [
            pltpu.SemaphoreType.DMA((6, count))
        ]

    sums, tap_sums = pl.pallas_call(
        kernel,
        out_shape=(
            jax.ShapeDtypeStruct((slots, CHUNK_ROWS, chans), link),
            jax.ShapeDtypeStruct((blocks, TAP_ROWS, LANES), f32),
        ),
        in_specs=[smem, smem] + [vmem] * 6,
        out_specs=(vmem,) * 2,
        scratch_shapes=[
            pltpu.VMEM((images, rows, chans), bf16),
            pltpu.VMEM((images, rows, chans), bf16),
            pltpu.VMEM((images, rows, chans), bf16),
            pltpu.VMEM((images, rows, chans), bf16),
            pltpu.VMEM((images, rows, chans), bf16),
            pltpu.VMEM((images, rows, chans), bf16),
            pltpu.VMEM((rows, chans), f32),
            pltpu.VMEM((height + 4, padded, LANES), f32),
            pltpu.VMEM((height + 2, padded, LANES), f32),
            pltpu.VMEM((images, blocks, height + 4, padded, LANES), f32),
            pltpu.VMEM((images, blocks, height + 2, padded, LANES), f32),
            pltpu.VMEM((images, 8, chans), f32),
            pltpu.VMEM((blocks, 9, 8, LANES), f32),
            pltpu.VMEM((blocks, 25, 8, LANES), f32),
            pltpu.VMEM((blocks, TAP_ROWS, LANES), f32),
            pltpu.VMEM((3 * chans, chans), f32),
            pltpu.VMEM((images, MASK_ROWS, chans), f32),
            pltpu.VMEM((MASK_ROWS, chans), f32),
            pltpu.VMEM((rows, chans), f32),
            pltpu.VMEM((MASK_ROWS, rows), bf16),
            pltpu.VMEM((line, 16, chans), f32),
            pltpu.VMEM((half, CHUNK_ROWS, chans), link),
            pltpu.SemaphoreType.DMA((images,)),
            pltpu.SemaphoreType.DMA((images,)),
            pltpu.SemaphoreType.DMA((line,)),
            pltpu.SemaphoreType.DMA((line,)),
            pltpu.SemaphoreType.DMA((4, half)),
            *line_scratch(slots, CHUNK_ROWS, chans, link),
            *line_scratch(blocks, TAP_ROWS, LANES, f32),
        ],
        compiler_params=pltpu.CompilerParams(
            collective_id=0, has_side_effects=True, vmem_limit_bytes=56 << 20
        ),
        name="sections",
    )(
        offsets,
        labels,
        x,
        depth_small[0].reshape(9, 1, chans),
        point_first[0],
        depth_large[0].reshape(25, 1, chans),
        point_second[0],
        head_weight,
    )
    sum_first, sum_second, sum_small, sum_large = pl.pallas_call(
        finish,
        out_shape=(
            jax.ShapeDtypeStruct((chans, chans), f32),
            jax.ShapeDtypeStruct((chans, chans), f32),
            jax.ShapeDtypeStruct((9, 1, chans), f32),
            jax.ShapeDtypeStruct((25, 1, chans), f32),
        ),
        in_specs=[anywhere] * 2,
        out_specs=(anywhere,) * 4,
        scratch_shapes=[
            pltpu.VMEM((PIECES, 2 * chans // PIECES, chans), link),
            pltpu.VMEM((PIECES, 2 * chans // PIECES, chans), f32),
            pltpu.VMEM((blocks, TAP_ROWS, LANES), f32),
            pltpu.VMEM((9, 1, chans), f32),
            pltpu.VMEM((25, 1, chans), f32),
            pltpu.SemaphoreType.DMA((PIECES + 1,)),
            pltpu.SemaphoreType.DMA((PIECES + 2,)),
        ],
        compiler_params=pltpu.CompilerParams(vmem_limit_bytes=60 << 20),
        name="finish",
    )(sums.reshape(3 * chans, chans), tap_sums)
    return (
        sum_first[None],
        sum_second[None],
        sum_small.reshape(1, 3, 3, chans),
        sum_large.reshape(1, 5, 5, chans),
    )


def solution(mesh):
    placed = (
        P("section", ("groups", "dp"), None, None, None),
        P("section", None, None, None),
        P("section", None, None),
        P("section", None, None, None),
        P("section", None, None),
        P(),
        P(("groups", "dp")),
        P(("groups", "dp")),
    )
    return jax.shard_map(
        per_device,
        mesh=mesh,
        in_specs=placed,
        out_specs=(
            P("section", "groups", None),
            P("section", "groups", None),
            P("section", "groups", None, None),
            P("section", "groups", None, None),
        ),
        check_vma=False,
    )
```

```python
import jax
import jax.numpy as jnp
from jax import lax
from jax.experimental import pallas as pl
from jax.experimental.pallas import tpu as pltpu
from jax.sharding import PartitionSpec as P

BAND = 4
LOSS_SCALE = 64.0
LANES = 128
CHUNK_ROWS = 64
LAG = 4
AHEAD = 4
LENT = 10
TAP_ROWS = 40
TAP_SMALL = 25
MASK_ROWS = 32
PIECES = 4
GROUP = 4
EDGE = 8
f32 = jnp.float32
bf16 = jnp.bfloat16
contract_last = (((1,), (1,)), ((), ()))
contract_first = (((0,), (0,)), ((), ()))


def dot(a, b, dims=(((1,), (0,)), ((), ()))):
    return lax.dot_general(a, b, dims, preferred_element_type=f32)


def split_dot(values, matrix, dims):
    rows = values.shape[0]
    high = values.astype(bf16).astype(f32)
    rest = values - high
    mid = rest.astype(bf16).astype(f32)
    low = (rest - mid).astype(bf16).astype(f32)
    parts = jnp.concatenate([high, mid, low, jnp.zeros_like(low)], axis=0).astype(bf16)
    out = dot(parts, matrix, dims)
    return out[:rows] + out[rows : 2 * rows] + out[2 * rows : 3 * rows]


def three_parts(values):
    high = values.astype(bf16).astype(f32)
    rest = values - high
    mid = rest.astype(bf16).astype(f32)
    return high, mid, (rest - mid).astype(bf16).astype(f32)


class Line:
    def __init__(self, place, line, refs, get, done=None):
        self.place, self.line = place, line
        self.out, self.inner, self.across, self.final, self.sems = refs
        self.get, self.done = get, done
        self.left = place < line // 2
        self.outer = jnp.where(self.left, place, line - 1 - place)
        self.deep = line // 2 - 1
        self.middle = self.outer == self.deep

    def copy(self, k, src, dst, lane, step):
        way = jnp.where(self.left, step, -step)
        return pltpu.make_async_remote_copy(
            src_ref=src.at[k],
            dst_ref=dst.at[k],
            send_sem=self.sems.at[lane, k],
            recv_sem=self.sems.at[3 + lane, k],
            device_id={"dp": jnp.clip(self.place + way, 0, self.line - 1)},
        )

    def inward(self, k):
        return self.copy(k, self.out, self.inner, 0, 1)

    def exchange(self, k):
        return self.copy(k, self.out, self.across, 1, 1)

    def outward(self, k):
        return self.copy(k, self.final, self.final, 2, -1)

    def advance(self, phase, step, first, chunks, sent=0):
        lag, active, act = (
            (LAG * self.outer, True, self.gather),
            (LAG * (self.deep + 1), self.middle, self.total),
            (LAG * (2 * self.deep + 1 - self.outer), jnp.logical_not(self.middle), self.spread),
        )[phase]
        k = step - lag

        if phase == 0:
            active = (self.outer > 0) | (k + first >= sent)

        @pl.when(active & (k >= 0) & (k < chunks))
        def _():
            act(k + first)

    def gather(self, k):
        dtype = self.out.dtype
        end = self.outer == 0

        @pl.when(end)
        def _():
            self.out[k] = self.get(k).astype(dtype)

        @pl.when(jnp.logical_not(end))
        def _():
            self.inward(k).wait_recv()
            self.out[k] = (self.get(k) + self.inner[k].astype(f32)).astype(dtype)

        @pl.when(self.middle)
        def _():
            self.exchange(k).start()

        @pl.when(jnp.logical_not(self.middle))
        def _():
            self.inward(k).start()

    def total(self, k):
        self.exchange(k).wait_recv()
        value = self.out[k].astype(f32) + self.across[k].astype(f32)
        self.final[k] = value.astype(self.final.dtype)

        @pl.when(self.outer > 0)
        def _():
            self.outward(k).start()

        if self.done is not None:
            self.done(k)

    def spread(self, k):
        self.outward(k).wait_recv()

        @pl.when(self.outer > 0)
        def _():
            self.outward(k).start()

        if self.done is not None:
            self.done(k)

    def drain(self, k):
        @pl.when(self.middle)
        def _():
            self.exchange(k).wait_send()

        @pl.when(jnp.logical_not(self.middle))
        def _():
            self.inward(k).wait_send()

        @pl.when(self.outer > 0)
        def _():
            self.outward(k).wait_send()


def kernel(
    offsets, labels, x_in, k3, w1_in, k5, w2_in, head_in,
    sums, tap_sums,
    d1, a2, d2, gin, gp1, gout, tmp, s5f, s3f, s5g, s3g, pool, acc3, acc5, taps,
    grads, windows, k5_rows, spread5, push, factors,
    borrowed, x, w1, w2, head, load_sems, send_sem, recv_sem, factor_send, factor_recv, lend_sems, *line_refs,
):
    section = lax.axis_index("section")
    count = lax.axis_size("section")
    images, height, width, chans = x.shape
    rows = height * width
    blocks = chans // LANES
    last = section == count - 1
    scale = 1.0 / rows

    def load(source, target, index):
        return pltpu.make_async_copy(source, target, load_sems.at[index])

    def load_x(n):
        return load(x_in.at[n], x.at[n], n)

    load_w1, load_w2 = load(w1_in, w1, images), load(w2_in, w2, images + 1)
    load_head = load(head_in, head, images + 2)

    for n in range(images):
        load_x(n).start()
    load_w1.start()
    load_w2.start()

    @pl.when(last)
    def _():
        load_head.start()

    barrier = pltpu.get_barrier_semaphore()

    @pl.when(section > 0)
    def _():
        pl.semaphore_signal(barrier, inc=1, device_id={"section": section - 1})

    @pl.when(section < count - 1)
    def _():
        pl.semaphore_signal(barrier, inc=1, device_id={"section": section + 1})

    place = lax.axis_index("dp")
    line = lax.axis_size("dp")

    for away in range(1, line):
        pl.semaphore_signal(barrier, inc=1, device_id={"dp": lax.rem(place + away, line)})

    lender = section == count - 3

    @pl.when(lender)
    def _():
        pl.semaphore_signal(barrier, inc=1, device_id={"section": jnp.minimum(section + 2, count - 1)})

    @pl.when(last & (count > 2))
    def _():
        pl.semaphore_signal(barrier, inc=1, device_id={"section": jnp.maximum(section - 2, 0)})

    def cols(block):
        return pl.ds(pl.multiple_of(block * LANES, LANES), LANES)

    col_index = lax.broadcasted_iota(jnp.int32, (1, width, LANES), 1)

    def fill(ref, value, size):
        ref[pl.ds(size // 2, height), pl.ds(EDGE, width)] = value

    def clear(ref, size):
        radius = size // 2
        side = jnp.zeros((height + 2 * radius, EDGE, LANES), f32)
        ref[:, pl.ds(0, EDGE)] = side
        ref[:, pl.ds(EDGE + width, EDGE)] = side
        zero = jnp.zeros((radius, width, LANES), f32)
        ref[pl.ds(0, radius), pl.ds(EDGE, width)] = zero
        ref[pl.ds(radius + height, radius), pl.ds(EDGE, width)] = zero

    flat_group = GROUP * width

    def conv(ref, weights, size, block, flip, put):
        for start in range(0, height, GROUP):
            total = None
            for c in range(size):
                moved = ref[pl.ds(start, GROUP + size - 1), pl.ds(EDGE + c - size // 2, width)]
                for r in range(size):
                    tap = r * size + c
                    tap = size * size - 1 - tap if flip else tap
                    part = weights[tap, :, cols(block)] * moved[r : r + GROUP]
                    total = part if total is None else total + part
            put(pl.ds(start, GROUP), pl.ds(start * width, flat_group), total.reshape(flat_group, LANES))

    def kept(image):
        away = col_index - offsets[image]
        away = jnp.where(away < 0, away + width, away)
        return jnp.where((away < BAND) | (section > 0), 1.0, 0.0)

    def xin(image, block, some=slice(None)):
        return x[image, some, :, cols(block)].astype(f32) * kept(image)

    clear(s5f, 5)
    clear(s3f, 3)

    acc5[...] = jnp.zeros_like(acc5)
    acc3[...] = jnp.zeros_like(acc3)

    @pl.loop(0, images)
    def _(n):
        @pl.loop(0, blocks)
        def _(b):
            clear(s3g.at[n, b], 3)

            @pl.when(jnp.logical_not(last))
            def _():
                clear(s5g.at[n, b], 5)

    def window_mask():
        tap = lax.broadcasted_iota(jnp.int32, (MASK_ROWS, rows), 0)
        spot = lax.broadcasted_iota(jnp.int32, (MASK_ROWS, rows), 1)
        i, h = jnp.zeros_like(tap), jnp.zeros_like(spot)
        for step in range(1, 5):
            i = i + jnp.where(tap >= 5 * step, 1, 0)
        for step in range(1, height):
            h = h + jnp.where(spot >= width * step, 1, 0)
        down, along = h - i + 2, (spot - width * h) - (tap - 5 * i) + 2
        inside = (down >= 0) & (down < height) & (along >= 0) & (along < width) & (tap < 25)
        return jnp.where(inside, 1.0, 0.0)

    @pl.when(last)
    def _():
        mask = window_mask()
        push[...] = mask.astype(bf16)
        k5_rows[pl.ds(24, 8)] = jnp.zeros((8, chans), f32)
        for tap in range(25):
            k5_rows[pl.ds(tap, 1)] = k5[tap]
        parts = jnp.concatenate(three_parts(k5_rows[...]), axis=0).astype(bf16)
        masks = jnp.concatenate([mask, mask, mask], axis=0).astype(bf16)
        spread5[...] = dot(masks, parts, contract_first)

    @pl.loop(0, images)
    def _(n):
        load_x(n).wait()

        @pl.loop(0, blocks)
        def _(b):
            value = xin(n, b)
            pool[n, :, cols(b)] = jnp.sum(value.reshape(rows // 8, 8, LANES), axis=0)
            fill(s3f, jnp.maximum(value, 0.0), 3)

            def put(_, where, out):
                d1[n, where, cols(b)] = out.astype(bf16)

            conv(s3f, k3, 3, b, False, put)

    flat = (images * rows, chans)
    load_w1.wait()
    a2[...] = jnp.maximum(dot(d1[...].reshape(flat), w1[...]), 0.0).astype(bf16).reshape(a2.shape)

    @pl.when(last)
    def _():
        for n in range(images):
            windows[n] = dot(push[...], a2[n])

    def second_depth(start, end):
        @pl.loop(start, end)
        def _(n):
            @pl.loop(0, blocks)
            def _(b):
                value = a2[n, :, cols(b)].astype(f32).reshape(height, width, LANES)
                fill(s5f, value, 5)

                def put(_, where, out):
                    d2[n, where, cols(b)] = out.astype(bf16)

                conv(s5f, k5, 5, b, False, put)

    late = section == count - 2

    early = jnp.where(late, images // 2, images)

    @pl.when(jnp.logical_not(last))
    def _():
        second_depth(0, early)

    classes = head.shape[0]
    load_w2.wait()

    @pl.when(last)
    def _():
        load_head.wait()
        x_sums = [jnp.sum(pool[n], axis=0, keepdims=True) for n in range(images)]
        d2_sums = [
            jnp.sum(k5_rows[...] * windows[n], axis=0, keepdims=True) for n in range(images)
        ]
        twice = -(-2 * images // 8) * 8
        fill_rows = [jnp.zeros((twice - 2 * images, chans), f32)] if twice > 2 * images else []
        x_sum = jnp.concatenate(x_sums + x_sums + fill_rows, axis=0)
        d2_sum = jnp.concatenate(d2_sums + d2_sums + fill_rows, axis=0)
        pooled = (x_sum + split_dot(d2_sum, w2[...], (((1,), (0,)), ((), ())))) * scale
        rest = jnp.zeros((LANES - twice, chans), f32)
        wide = jnp.concatenate([pooled, rest], axis=0)
        high = wide.astype(bf16)
        mid = (wide - high.astype(f32)).astype(bf16)
        logits = dot(head[...], high, contract_last) + dot(head[...], mid, contract_last)
        class_index = lax.broadcasted_iota(jnp.int32, (classes, LANES), 0)
        lane = lax.broadcasted_iota(jnp.int32, (1, LANES), 1)
        label_row = jnp.full((1, LANES), -1, jnp.int32)
        for n in range(images):
            label_row = jnp.where((lane == n) | (lane == n + images), labels[n], label_row)
        dlog = LOSS_SCALE * (logits - jnp.where(class_index == label_row, 1.0, 0.0))
        high = dlog.astype(bf16).astype(f32)
        part = jnp.where(lane < images, high, dlog - high).astype(bf16)
        both = dot(part, head[...], contract_first)
        grad = ((both[:images] + both[images : 2 * images]) * scale).astype(bf16).astype(f32)
        pad = jnp.zeros((8 - images, chans), f32)
        factors[place, pl.ds(0, 8)] = jnp.concatenate([*d2_sums, pad], axis=0)
        factors[place, pl.ds(8, 8)] = jnp.concatenate([grad, pad], axis=0)
        wide = jnp.concatenate([grad, jnp.zeros((16 - images, chans), f32)], axis=0)
        tmp[pl.ds(0, 16)] = dot(wide.astype(bf16), w2[...], contract_last)
        for n in range(images):
            gin[n] = jnp.broadcast_to(grad[n : n + 1], (rows, chans)).astype(bf16)
        for n in range(images):
            back = tmp[pl.ds(n, 1)]
            if n == 0:
                total = back * windows[n]
            else:
                total = total + back * windows[n]
            live = a2[n].astype(f32) > 0
            gp1[n] = jnp.where(live, back * spread5[...], 0.0).astype(bf16)
        for b in range(blocks):
            taps[b, pl.ds(0, 25)] = total[:25, b * LANES : (b + 1) * LANES]

    def hand_over(n):
        return pltpu.make_async_remote_copy(
            src_ref=gout.at[n],
            dst_ref=gin.at[n],
            send_sem=send_sem.at[n],
            recv_sem=recv_sem.at[n],
            device_id={"section": jnp.maximum(section - 1, 0)},
        )

    pl.semaphore_wait(
        barrier,
        jnp.where(section > 0, 1, 0)
        + jnp.where(section < count - 1, 1, 0)
        + jnp.where(lender | (last & (count > 2)), 1, 0)
        + (line - 1),
    )

    def give(away):
        other = lax.rem(place + away, line)
        return pltpu.make_async_remote_copy(
            src_ref=factors.at[place],
            dst_ref=factors.at[place],
            send_sem=factor_send.at[away],
            recv_sem=factor_recv.at[away],
            device_id={"dp": other},
        )

    def take(away):
        other = lax.rem(place + line - away, line)
        return pltpu.make_async_remote_copy(
            src_ref=factors.at[other],
            dst_ref=factors.at[other],
            send_sem=factor_send.at[away],
            recv_sem=factor_recv.at[away],
            device_id={"dp": lax.rem(place + away, line)},
        )

    @pl.when(last)
    def _():
        for away in range(1, line):
            give(away).start()

    chunk_rows = CHUNK_ROWS
    half = chans // chunk_rows

    def rows_of(k):
        return pl.ds(pl.multiple_of(k * chunk_rows, chunk_rows), chunk_rows)

    def lend(k):
        return pltpu.make_async_remote_copy(
            src_ref=line_refs[0].at[k],
            dst_ref=borrowed.at[k],
            send_sem=lend_sems.at[0, k],
            recv_sem=lend_sems.at[1, k],
            device_id={"section": jnp.minimum(section + 2, count - 1)},
        )

    def give_back(k):
        return pltpu.make_async_remote_copy(
            src_ref=sums.at[k + 2 * half],
            dst_ref=sums.at[k],
            send_sem=lend_sems.at[2, k],
            recv_sem=lend_sems.at[3, k],
            device_id={"section": jnp.maximum(section - 2, 0)},
        )

    def own(k):
        @pl.when(k >= 2 * half)
        def _():
            lend(k - 2 * half).wait_recv()
            grads[rows_of(k)] = borrowed[k - 2 * half].astype(f32)

        return grads[rows_of(k)]

    def done(k):
        @pl.when(k >= 2 * half)
        def _():
            give_back(k - 2 * half).start()

    main = Line(place, line, [*line_refs[0:3], sums, line_refs[3]], own, done)
    tap_line = Line(place, line, [*line_refs[4:7], tap_sums, line_refs[7]], lambda k: taps[k])
    lent = borrowed.shape[0]
    begin = jnp.where(lender, lent, jnp.where(last, half, 0))
    finish_at = jnp.where(last & (count > 2), 2 * half + lent, 2 * half)

    def kernel_grad(acc, value, ref, size):
        for c in range(size):
            sums_of = [None] * size
            for start in range(0, height, GROUP):
                left = value(pl.ds(start, GROUP), pl.ds(start * width, flat_group))
                moved = ref[
                    pl.ds(start, GROUP + size - 1), pl.ds(EDGE + size - 1 - c - size // 2, width)
                ]
                for r in range(size):
                    part = left * moved[size - 1 - r : size - 1 - r + GROUP]
                    part = jnp.sum(part.reshape(flat_group // 8, 8, LANES), axis=0)
                    sums_of[r] = part if sums_of[r] is None else sums_of[r] + part
            for r in range(size):
                acc[r * size + c] += sums_of[r]

    def kernel_grads(n, b):
        def second_value(_, where):
            return a2[n, where, cols(b)].astype(f32).reshape(GROUP, width, LANES)

        def first_value(some, _):
            return jnp.maximum(xin(n, b, some), 0.0)

        @pl.when(jnp.logical_not(last))
        def _():
            kernel_grad(acc5.at[b], second_value, s5g.at[n, b], 5)

        kernel_grad(acc3.at[b], first_value, s3g.at[n, b], 3)

        @pl.when(n == images - 1)
        def _():
            @pl.when(jnp.logical_not(last))
            def _():
                taps[b, pl.ds(0, 25)] = jnp.sum(acc5[b], axis=1)

            taps[b, pl.ds(TAP_SMALL, 9)] = jnp.sum(acc3[b], axis=1)

    waits = section < count - 2

    def product(at, left, right, start, end):
        shape = ((end - start) * rows, chans)
        left = left[pl.ds(start, end - start)].reshape(shape)
        right = right[pl.ds(start, end - start)].reshape(shape)
        part = dot(left, right, contract_first)
        if start == 0:
            grads[pl.ds(at, chans)] = part
        else:
            grads[pl.ds(at, chans)] += part

    def closing(at, left, right):
        @pl.when(waits)
        def _():
            product(at, left, right, images - 1, images)

        @pl.when(jnp.logical_not(waits))
        def _():
            product(at, left, right, 0, images)

    def weight_grads():
        @pl.when(jnp.logical_not(last))
        def _():
            closing(0, d2, gin)

            @pl.when((main.outer == 0) & jnp.logical_not(lender))
            def _():
                @pl.loop(0, AHEAD)
                def _(k):
                    main.gather(k)

        def hand_out(start, end):
            @pl.when(lender)
            def _():
                @pl.loop(start, end)
                def _(k):
                    main.out[k] = grads[rows_of(k)].astype(main.out.dtype)
                    lend(k).start()

        hand_out(0, min(half, lent))
        closing(chans, d1, gp1)
        hand_out(min(half, lent), lent)

    @pl.loop(0, images)
    def _(n):
        @pl.when(jnp.logical_not(last))
        def _():
            hand_over(n).wait_recv()
            tmp[...] = dot(gin[n], w2[...], contract_last)

            @pl.loop(0, blocks)
            def _(b):
                shifts = s5g.at[n, b]
                fill(shifts, tmp[:, cols(b)].reshape(height, width, LANES), 5)

                def put(_, where, back):
                    live = a2[n, where, cols(b)].astype(f32) > 0
                    gp1[n, where, cols(b)] = jnp.where(live, back, 0.0).astype(bf16)

                conv(shifts, k5, 5, b, True, put)

        @pl.when((section == 0) & (n == images - 1))
        def _():
            weight_grads()

        tmp[...] = dot(gp1[n], w1[...], contract_last)

        @pl.loop(0, blocks)
        def _(b):
            shifts = s3g.at[n, b]
            fill(shifts, tmp[:, cols(b)].reshape(height, width, LANES), 3)

            @pl.when(section > 0)
            def _():
                def put(some, where, back):
                    live = xin(n, b, some).reshape(flat_group, LANES) > 0
                    grad = gin[n, where, cols(b)].astype(f32) + jnp.where(live, back, 0.0)
                    gout[n, where, cols(b)] = grad.astype(bf16)

                conv(shifts, k3, 3, b, True, put)

        @pl.when(section > 0)
        def _():
            hand_over(n).start()

        @pl.when(waits & (n == images - 2))
        def _():
            product(0, d2, gin, 0, images - 1)
            product(chans, d1, gp1, 0, images - 1)

    @pl.when(late)
    def _():
        second_depth(images // 2, images)

    @pl.when(section > 0)
    def _():
        weight_grads()

    busy = blocks * images
    taps[:, pl.ds(32, 8)] = jnp.zeros((blocks, 8, LANES), f32)

    behind = LAG * (line - 1)
    sent = jnp.where(last | lender, 0, AHEAD)

    @pl.loop(0, jnp.maximum(finish_at - begin, busy + blocks) + behind)
    def _(step):
        for phase in range(3):
            tap_line.advance(phase, step - (busy - blocks + 1), 0, blocks)
            main.advance(phase, step, begin, finish_at - begin, sent)
            if phase == 0:

                @pl.when(step < busy)
                def _():
                    kernel_grads(step // blocks, step % blocks)

    @pl.when(last)
    def _():
        for away in range(1, line):
            take(away).wait_recv()
        left = factors[:, pl.ds(0, 8)].reshape(line * 8, chans)
        right = factors[:, pl.ds(8, 8)].reshape(line * 8, chans)
        left = jnp.concatenate(three_parts(left), axis=0).astype(bf16)
        right = jnp.concatenate([right, right, right], axis=0).astype(bf16)
        value = dot(left, right, contract_first)
        sums[pl.ds(0, half)] = value.reshape(half, chunk_rows, chans).astype(sums.dtype)
        for away in range(1, line):
            give(away).wait_send()

    @pl.loop(0, blocks)
    def _(k):
        tap_line.drain(k)

    @pl.loop(begin, finish_at)
    def _(k):
        main.drain(k)

    @pl.when(lender)
    def _():
        @pl.loop(0, lent)
        def _(k):
            give_back(k).wait_recv()
            lend(k).wait_send()

    @pl.when(last & (count > 2))
    def _():
        @pl.loop(0, lent)
        def _(k):
            give_back(k).wait_send()

    @pl.when(section > 0)
    def _():
        @pl.loop(0, images)
        def _(n):
            hand_over(n).wait_send()


def finish(
    sums, taps, grad_first, grad_second, grad_small, grad_large,
    narrow, wide, taps_in, small, large, in_sem, out_sem,
):
    pieces, length = narrow.shape[0], narrow.shape[1]
    per_output = pieces // 2
    loads = [
        pltpu.make_async_copy(sums.at[pl.ds(p * length, length)], narrow.at[p], in_sem.at[p])
        for p in range(pieces)
    ]
    stores = [
        pltpu.make_async_copy(
            wide.at[p],
            (grad_second, grad_first)[p // per_output].at[pl.ds(p % per_output * length, length)],
            out_sem.at[p],
        )
        for p in range(pieces)
    ]
    loads.append(pltpu.make_async_copy(taps, taps_in, in_sem.at[pieces]))
    stores.append(pltpu.make_async_copy(small, grad_small, out_sem.at[pieces]))
    stores.append(pltpu.make_async_copy(large, grad_large, out_sem.at[pieces + 1]))
    for load in loads:
        load.start()
    for p in range(pieces):
        loads[p].wait()
        wide[p] = narrow[p].astype(f32)
        stores[p].start()
    loads[pieces].wait()
    for block in range(taps_in.shape[0]):
        where = pl.ds(block * LANES, LANES)
        for tap in range(25):
            large[tap, :, where] = taps_in[block, pl.ds(tap, 1)]
        for tap in range(9):
            small[tap, :, where] = taps_in[block, pl.ds(TAP_SMALL + tap, 1)]
    stores[pieces].start()
    stores[pieces + 1].start()
    for store in stores:
        store.wait()


def per_device(
    activations, depth_small, point_first, depth_large, point_second, head_weight, offsets, labels
):
    x = activations[0]
    images, height, width, chans = x.shape
    rows = height * width
    blocks = chans // LANES
    vmem = pl.BlockSpec(memory_space=pltpu.VMEM)
    smem = pl.BlockSpec(memory_space=pltpu.SMEM)
    anywhere = pl.BlockSpec(memory_space=pl.ANY)

    padded = width + 2 * EDGE
    line = lax.axis_size("dp")
    link = bf16 if line <= 4 else f32
    half = chans // CHUNK_ROWS
    lent = half * LENT // 8
    slots = 2 * half + lent

    def line_scratch(count, length, wide, dtype):
        return [pltpu.VMEM((count, length, wide), dtype)] * 3 + [
            pltpu.SemaphoreType.DMA((6, count))
        ]

    sums, tap_sums = pl.pallas_call(
        kernel,
        out_shape=(
            jax.ShapeDtypeStruct((slots, CHUNK_ROWS, chans), link),
            jax.ShapeDtypeStruct((blocks, TAP_ROWS, LANES), f32),
        ),
        in_specs=[smem, smem, anywhere, vmem, anywhere, vmem, anywhere, anywhere],
        out_specs=(vmem,) * 2,
        scratch_shapes=[
            pltpu.VMEM((images, rows, chans), bf16),
            pltpu.VMEM((images, rows, chans), bf16),
            pltpu.VMEM((images, rows, chans), bf16),
            pltpu.VMEM((images, rows, chans), bf16),
            pltpu.VMEM((images, rows, chans), bf16),
            pltpu.VMEM((images, rows, chans), bf16),
            pltpu.VMEM((rows, chans), f32),
            pltpu.VMEM((height + 4, padded, LANES), f32),
            pltpu.VMEM((height + 2, padded, LANES), f32),
            pltpu.VMEM((images, blocks, height + 4, padded, LANES), f32),
            pltpu.VMEM((images, blocks, height + 2, padded, LANES), f32),
            pltpu.VMEM((images, 8, chans), f32),
            pltpu.VMEM((blocks, 9, 8, LANES), f32),
            pltpu.VMEM((blocks, 25, 8, LANES), f32),
            pltpu.VMEM((blocks, TAP_ROWS, LANES), f32),
            pltpu.VMEM((slots * CHUNK_ROWS, chans), f32),
            pltpu.VMEM((images, MASK_ROWS, chans), f32),
            pltpu.VMEM((MASK_ROWS, chans), f32),
            pltpu.VMEM((rows, chans), f32),
            pltpu.VMEM((MASK_ROWS, rows), bf16),
            pltpu.VMEM((line, 16, chans), f32),
            pltpu.VMEM((lent, CHUNK_ROWS, chans), link),
            pltpu.VMEM(x.shape, bf16),
            pltpu.VMEM((chans, chans), bf16),
            pltpu.VMEM((chans, chans), bf16),
            pltpu.VMEM(head_weight.shape, bf16),
            pltpu.SemaphoreType.DMA((images + 3,)),
            pltpu.SemaphoreType.DMA((images,)),
            pltpu.SemaphoreType.DMA((images,)),
            pltpu.SemaphoreType.DMA((line,)),
            pltpu.SemaphoreType.DMA((line,)),
            pltpu.SemaphoreType.DMA((4, lent)),
            *line_scratch(slots, CHUNK_ROWS, chans, link),
            *line_scratch(blocks, TAP_ROWS, LANES, f32),
        ],
        compiler_params=pltpu.CompilerParams(
            collective_id=0, has_side_effects=True, vmem_limit_bytes=56 << 20
        ),
        name="sections",
    )(
        offsets,
        labels,
        x,
        depth_small[0].reshape(9, 1, chans),
        point_first[0],
        depth_large[0].reshape(25, 1, chans),
        point_second[0],
        head_weight,
    )
    sum_first, sum_second, sum_small, sum_large = pl.pallas_call(
        finish,
        out_shape=(
            jax.ShapeDtypeStruct((chans, chans), f32),
            jax.ShapeDtypeStruct((chans, chans), f32),
            jax.ShapeDtypeStruct((9, 1, chans), f32),
            jax.ShapeDtypeStruct((25, 1, chans), f32),
        ),
        in_specs=[anywhere] * 2,
        out_specs=(anywhere,) * 4,
        scratch_shapes=[
            pltpu.VMEM((PIECES, 2 * chans // PIECES, chans), link),
            pltpu.VMEM((PIECES, 2 * chans // PIECES, chans), f32),
            pltpu.VMEM((blocks, TAP_ROWS, LANES), f32),
            pltpu.VMEM((9, 1, chans), f32),
            pltpu.VMEM((25, 1, chans), f32),
            pltpu.SemaphoreType.DMA((PIECES + 1,)),
            pltpu.SemaphoreType.DMA((PIECES + 2,)),
        ],
        compiler_params=pltpu.CompilerParams(vmem_limit_bytes=60 << 20),
        name="finish",
    )(sums.reshape(slots * CHUNK_ROWS, chans), tap_sums)
    return (
        sum_first[None],
        sum_second[None],
        sum_small.reshape(1, 3, 3, chans),
        sum_large.reshape(1, 5, 5, chans),
    )


def solution(mesh):
    placed = (
        P("section", ("groups", "dp"), None, None, None),
        P("section", None, None, None),
        P("section", None, None),
        P("section", None, None, None),
        P("section", None, None),
        P(),
        P(("groups", "dp")),
        P(("groups", "dp")),
    )
    return jax.shard_map(
        per_device,
        mesh=mesh,
        in_specs=placed,
        out_specs=(
            P("section", "groups", None),
            P("section", "groups", None),
            P("section", "groups", None, None),
            P("section", "groups", None, None),
        ),
        check_vma=False,
    )
```

```python
import jax
import jax.numpy as jnp
from jax import lax
from jax.experimental import pallas as pl
from jax.experimental.pallas import tpu as pltpu
from jax.sharding import PartitionSpec as P

BAND = 4
LOSS_SCALE = 64.0
LANES = 128
CHUNK_ROWS = 64
LAG = 4
AHEAD = 4
LENT = 11
FAR_LEND = False
FAR_BACK = True
TAP_ROWS = 40
TAP_SMALL = 25
MASK_ROWS = 32
PIECES = 4
GROUP = 4
EDGE = 8
f32 = jnp.float32
bf16 = jnp.bfloat16
contract_last = (((1,), (1,)), ((), ()))
contract_first = (((0,), (0,)), ((), ()))


def dot(a, b, dims=(((1,), (0,)), ((), ()))):
    return lax.dot_general(a, b, dims, preferred_element_type=f32)


def split_dot(values, matrix, dims):
    rows = values.shape[0]
    high = values.astype(bf16).astype(f32)
    rest = values - high
    mid = rest.astype(bf16).astype(f32)
    low = (rest - mid).astype(bf16).astype(f32)
    parts = jnp.concatenate([high, mid, low, jnp.zeros_like(low)], axis=0).astype(bf16)
    out = dot(parts, matrix, dims)
    return out[:rows] + out[rows : 2 * rows] + out[2 * rows : 3 * rows]


def three_parts(values):
    high = values.astype(bf16).astype(f32)
    rest = values - high
    mid = rest.astype(bf16).astype(f32)
    return high, mid, (rest - mid).astype(bf16).astype(f32)


class Line:
    def __init__(self, place, line, refs, get, done=None, pass_on=None, skips=(None, None)):
        self.place, self.line = place, line
        self.out, self.inner, self.across, self.final, self.sems = refs
        self.get, self.done, self.skips = get, done, skips
        self.pass_on = pass_on or (lambda k: self.outward(k).start())
        self.left = place < line // 2
        self.outer = jnp.where(self.left, place, line - 1 - place)
        self.deep = line // 2 - 1
        self.middle = self.outer == self.deep

    def copy(self, k, src, dst, lane, step):
        way = jnp.where(self.left, step, -step)
        return pltpu.make_async_remote_copy(
            src_ref=src.at[k],
            dst_ref=dst.at[k],
            send_sem=self.sems.at[lane, k],
            recv_sem=self.sems.at[3 + lane, k],
            device_id={"dp": jnp.clip(self.place + way, 0, self.line - 1)},
        )

    def inward(self, k):
        return self.copy(k, self.out, self.inner, 0, 1)

    def exchange(self, k):
        return self.copy(k, self.out, self.across, 1, 1)

    def outward(self, k):
        return self.copy(k, self.final, self.final, 2, -1)

    def advance(self, phase, step, first, chunks, sent=0):
        lag, active, act = (
            (LAG * self.outer, True, self.gather),
            (LAG * (self.deep + 1), self.middle, self.total),
            (LAG * (2 * self.deep + 1 - self.outer), jnp.logical_not(self.middle), self.spread),
        )[phase]
        k = step - lag

        if phase == 0:
            active = (self.outer > 0) | (k + first >= sent)
        skip = self.skips[phase // 2]
        if phase != 1 and skip is not None:
            active = active & jnp.logical_not(skip(k + first))

        @pl.when(active & (k >= 0) & (k < chunks))
        def _():
            act(k + first)

    def gather(self, k):
        dtype = self.out.dtype
        end = self.outer == 0

        @pl.when(end)
        def _():
            self.out[k] = self.get(k).astype(dtype)

        @pl.when(jnp.logical_not(end))
        def _():
            self.inward(k).wait_recv()
            self.out[k] = (self.get(k) + self.inner[k].astype(f32)).astype(dtype)

        @pl.when(self.middle)
        def _():
            self.exchange(k).start()

        @pl.when(jnp.logical_not(self.middle))
        def _():
            self.inward(k).start()

    def total(self, k):
        self.exchange(k).wait_recv()
        value = self.out[k].astype(f32) + self.across[k].astype(f32)
        self.final[k] = value.astype(self.final.dtype)

        @pl.when(self.outer > 0)
        def _():
            self.pass_on(k)

        if self.done is not None:
            self.done(k)

    def spread(self, k):
        self.outward(k).wait_recv()

        @pl.when(self.outer > 0)
        def _():
            self.pass_on(k)

        if self.done is not None:
            self.done(k)

    def drain(self, k):
        @pl.when(self.middle)
        def _():
            self.exchange(k).wait_send()

        sends = jnp.logical_not(self.middle)
        if self.skips[0] is not None:
            sends = sends & jnp.logical_not(self.skips[0](k))

        @pl.when(sends)
        def _():
            self.inward(k).wait_send()

        @pl.when(self.outer > 0)
        def _():
            self.outward(k).wait_send()


def kernel(
    offsets, labels, x_in, k3, w1_in, k5, w2_in, head_in,
    sums, tap_sums,
    d1, a2, d2, gin, gp1, gout, tmp, s5f, s3f, s5g, s3g, pool, acc3, acc5, taps,
    grads, windows, k5_rows, spread5, push, factors,
    back_rows, borrowed, x, w1, w2, head, load_sems, send_sem, recv_sem, factor_send, factor_recv, lend_sems, *line_refs,
):
    section = lax.axis_index("section")
    count = lax.axis_size("section")
    images, height, width, chans = x.shape
    rows = height * width
    blocks = chans // LANES
    last = section == count - 1
    scale = 1.0 / rows

    def load(source, target, index):
        return pltpu.make_async_copy(source, target, load_sems.at[index])

    def load_x(n):
        return load(x_in.at[n], x.at[n], n)

    load_w1, load_w2 = load(w1_in, w1, images), load(w2_in, w2, images + 1)
    load_head = load(head_in, head, images + 2)

    for n in range(images):
        load_x(n).start()
    load_w1.start()
    load_w2.start()

    @pl.when(last)
    def _():
        load_head.start()

    barrier = pltpu.get_barrier_semaphore()

    @pl.when(section > 0)
    def _():
        pl.semaphore_signal(barrier, inc=1, device_id={"section": section - 1})

    @pl.when(section < count - 1)
    def _():
        pl.semaphore_signal(barrier, inc=1, device_id={"section": section + 1})

    place = lax.axis_index("dp")
    line = lax.axis_size("dp")

    for away in range(1, line):
        pl.semaphore_signal(barrier, inc=1, device_id={"dp": lax.rem(place + away, line)})

    lender = section == count - 3

    @pl.when(lender)
    def _():
        pl.semaphore_signal(barrier, inc=1, device_id={"section": jnp.minimum(section + 2, count - 1)})

    @pl.when(last & (count > 2))
    def _():
        pl.semaphore_signal(barrier, inc=1, device_id={"section": jnp.maximum(section - 2, 0)})

    on_left = place < line // 2
    outer = jnp.where(on_left, place, line - 1 - place)
    inner_place = jnp.clip(jnp.where(on_left, place + 1, place - 1), 0, line - 1)
    outer_place = jnp.clip(jnp.where(on_left, place - 1, place + 1), 0, line - 1)
    end = (outer == 0) & (line > 2)
    lends_far = lender & end
    backs_far = last & (count > 2) & (outer == 1)

    @pl.when(lends_far)
    def _():
        pl.semaphore_signal(
            barrier,
            inc=1,
            device_id={"dp": inner_place, "section": jnp.minimum(section + 2, count - 1)},
        )

    @pl.when(backs_far)
    def _():
        pl.semaphore_signal(
            barrier, inc=1, device_id={"dp": outer_place, "section": jnp.maximum(section - 2, 0)}
        )

    def cols(block):
        return pl.ds(pl.multiple_of(block * LANES, LANES), LANES)

    col_index = lax.broadcasted_iota(jnp.int32, (1, width, LANES), 1)

    def fill(ref, value, size):
        ref[pl.ds(size // 2, height), pl.ds(EDGE, width)] = value

    def clear(ref, size):
        radius = size // 2
        side = jnp.zeros((height + 2 * radius, EDGE, LANES), f32)
        ref[:, pl.ds(0, EDGE)] = side
        ref[:, pl.ds(EDGE + width, EDGE)] = side
        zero = jnp.zeros((radius, width, LANES), f32)
        ref[pl.ds(0, radius), pl.ds(EDGE, width)] = zero
        ref[pl.ds(radius + height, radius), pl.ds(EDGE, width)] = zero

    flat_group = GROUP * width

    def conv(ref, weights, size, block, flip, put):
        for start in range(0, height, GROUP):
            total = None
            for c in range(size):
                moved = ref[pl.ds(start, GROUP + size - 1), pl.ds(EDGE + c - size // 2, width)]
                for r in range(size):
                    tap = r * size + c
                    tap = size * size - 1 - tap if flip else tap
                    part = weights[tap, :, cols(block)] * moved[r : r + GROUP]
                    total = part if total is None else total + part
            put(pl.ds(start, GROUP), pl.ds(start * width, flat_group), total.reshape(flat_group, LANES))

    def kept(image):
        away = col_index - offsets[image]
        away = jnp.where(away < 0, away + width, away)
        return jnp.where((away < BAND) | (section > 0), 1.0, 0.0)

    def xin(image, block, some=slice(None)):
        return x[image, some, :, cols(block)].astype(f32) * kept(image)

    clear(s5f, 5)
    clear(s3f, 3)

    acc5[...] = jnp.zeros_like(acc5)
    acc3[...] = jnp.zeros_like(acc3)

    @pl.loop(0, images)
    def _(n):
        @pl.loop(0, blocks)
        def _(b):
            clear(s3g.at[n, b], 3)

            @pl.when(jnp.logical_not(last))
            def _():
                clear(s5g.at[n, b], 5)

    def window_mask():
        tap = lax.broadcasted_iota(jnp.int32, (MASK_ROWS, rows), 0)
        spot = lax.broadcasted_iota(jnp.int32, (MASK_ROWS, rows), 1)
        i, h = jnp.zeros_like(tap), jnp.zeros_like(spot)
        for step in range(1, 5):
            i = i + jnp.where(tap >= 5 * step, 1, 0)
        for step in range(1, height):
            h = h + jnp.where(spot >= width * step, 1, 0)
        down, along = h - i + 2, (spot - width * h) - (tap - 5 * i) + 2
        inside = (down >= 0) & (down < height) & (along >= 0) & (along < width) & (tap < 25)
        return jnp.where(inside, 1.0, 0.0)

    @pl.when(last)
    def _():
        mask = window_mask()
        push[...] = mask.astype(bf16)
        k5_rows[pl.ds(24, 8)] = jnp.zeros((8, chans), f32)
        for tap in range(25):
            k5_rows[pl.ds(tap, 1)] = k5[tap]
        parts = jnp.concatenate(three_parts(k5_rows[...]), axis=0).astype(bf16)
        masks = jnp.concatenate([mask, mask, mask], axis=0).astype(bf16)
        spread5[...] = dot(masks, parts, contract_first)

    @pl.loop(0, images)
    def _(n):
        load_x(n).wait()

        @pl.loop(0, blocks)
        def _(b):
            value = xin(n, b)
            pool[n, :, cols(b)] = jnp.sum(value.reshape(rows // 8, 8, LANES), axis=0)
            fill(s3f, jnp.maximum(value, 0.0), 3)

            def put(_, where, out):
                d1[n, where, cols(b)] = out.astype(bf16)

            conv(s3f, k3, 3, b, False, put)

    flat = (images * rows, chans)
    load_w1.wait()
    a2[...] = jnp.maximum(dot(d1[...].reshape(flat), w1[...]), 0.0).astype(bf16).reshape(a2.shape)

    @pl.when(last)
    def _():
        for n in range(images):
            windows[n] = dot(push[...], a2[n])

    def second_depth(start, end):
        @pl.loop(start, end)
        def _(n):
            @pl.loop(0, blocks)
            def _(b):
                value = a2[n, :, cols(b)].astype(f32).reshape(height, width, LANES)
                fill(s5f, value, 5)

                def put(_, where, out):
                    d2[n, where, cols(b)] = out.astype(bf16)

                conv(s5f, k5, 5, b, False, put)

    late = section == count - 2

    early = jnp.where(late, images // 2, images)

    @pl.when(jnp.logical_not(last))
    def _():
        second_depth(0, early)

    classes = head.shape[0]
    load_w2.wait()

    @pl.when(last)
    def _():
        load_head.wait()
        x_sums = [jnp.sum(pool[n], axis=0, keepdims=True) for n in range(images)]
        d2_sums = [
            jnp.sum(k5_rows[...] * windows[n], axis=0, keepdims=True) for n in range(images)
        ]
        twice = -(-2 * images // 8) * 8
        fill_rows = [jnp.zeros((twice - 2 * images, chans), f32)] if twice > 2 * images else []
        x_sum = jnp.concatenate(x_sums + x_sums + fill_rows, axis=0)
        d2_sum = jnp.concatenate(d2_sums + d2_sums + fill_rows, axis=0)
        pooled = (x_sum + split_dot(d2_sum, w2[...], (((1,), (0,)), ((), ())))) * scale
        rest = jnp.zeros((LANES - twice, chans), f32)
        wide = jnp.concatenate([pooled, rest], axis=0)
        high = wide.astype(bf16)
        mid = (wide - high.astype(f32)).astype(bf16)
        logits = dot(head[...], high, contract_last) + dot(head[...], mid, contract_last)
        class_index = lax.broadcasted_iota(jnp.int32, (classes, LANES), 0)
        lane = lax.broadcasted_iota(jnp.int32, (1, LANES), 1)
        label_row = jnp.full((1, LANES), -1, jnp.int32)
        for n in range(images):
            label_row = jnp.where((lane == n) | (lane == n + images), labels[n], label_row)
        dlog = LOSS_SCALE * (logits - jnp.where(class_index == label_row, 1.0, 0.0))
        high = dlog.astype(bf16).astype(f32)
        part = jnp.where(lane < images, high, dlog - high).astype(bf16)
        both = dot(part, head[...], contract_first)
        grad = ((both[:images] + both[images : 2 * images]) * scale).astype(bf16).astype(f32)
        pad = jnp.zeros((8 - images, chans), f32)
        factors[place, pl.ds(0, 8)] = jnp.concatenate([*d2_sums, pad], axis=0)
        factors[place, pl.ds(8, 8)] = jnp.concatenate([grad, pad], axis=0)
        wide = jnp.concatenate([grad, jnp.zeros((16 - images, chans), f32)], axis=0)
        back_rows[...] = dot(wide.astype(bf16), w2[...], contract_last)

    def hand_over(n):
        return pltpu.make_async_remote_copy(
            src_ref=gout.at[n],
            dst_ref=gin.at[n],
            send_sem=send_sem.at[n],
            recv_sem=recv_sem.at[n],
            device_id={"section": jnp.maximum(section - 1, 0)},
        )

    pl.semaphore_wait(
        barrier,
        jnp.where(section > 0, 1, 0)
        + jnp.where(section < count - 1, 1, 0)
        + jnp.where(lender | (last & (count > 2)), 1, 0)
        + jnp.where(lends_far | backs_far, 1, 0)
        + (line - 1),
    )

    def give(away):
        other = lax.rem(place + away, line)
        return pltpu.make_async_remote_copy(
            src_ref=factors.at[place],
            dst_ref=factors.at[place],
            send_sem=factor_send.at[away],
            recv_sem=factor_recv.at[away],
            device_id={"dp": other},
        )

    def take(away):
        other = lax.rem(place + line - away, line)
        return pltpu.make_async_remote_copy(
            src_ref=factors.at[other],
            dst_ref=factors.at[other],
            send_sem=factor_send.at[away],
            recv_sem=factor_recv.at[away],
            device_id={"dp": lax.rem(place + away, line)},
        )

    @pl.when(last)
    def _():
        for away in range(1, line):
            give(away).start()

    chunk_rows = CHUNK_ROWS
    half = chans // chunk_rows

    def rows_of(k):
        return pl.ds(pl.multiple_of(k * chunk_rows, chunk_rows), chunk_rows)

    def lend(k):
        return pltpu.make_async_remote_copy(
            src_ref=line_refs[0].at[k],
            dst_ref=borrowed.at[k],
            send_sem=lend_sems.at[0, k],
            recv_sem=lend_sems.at[1, k],
            device_id={"section": jnp.minimum(section + 2, count - 1)},
        )

    def lend_far(k):
        return pltpu.make_async_remote_copy(
            src_ref=line_refs[0].at[k],
            dst_ref=line_refs[1].at[k + 2 * half],
            send_sem=lend_sems.at[0, k],
            recv_sem=line_refs[3].at[3, k + 2 * half],
            device_id={"dp": inner_place, "section": jnp.minimum(section + 2, count - 1)},
        )

    def back_far(k):
        return pltpu.make_async_remote_copy(
            src_ref=sums.at[k],
            dst_ref=sums.at[k - 2 * half],
            send_sem=line_refs[3].at[2, k],
            recv_sem=lend_sems.at[3, k - 2 * half],
            device_id={"dp": outer_place, "section": jnp.maximum(section - 2, 0)},
        )

    def pass_on(k):
        far = (k >= 2 * half) & (outer == 1) & FAR_BACK

        @pl.when(far)
        def _():
            back_far(k).start()

        @pl.when(jnp.logical_not(far))
        def _():
            main.outward(k).start()

    def give_back(k):
        return pltpu.make_async_remote_copy(
            src_ref=sums.at[k + 2 * half],
            dst_ref=sums.at[k],
            send_sem=lend_sems.at[2, k],
            recv_sem=lend_sems.at[3, k],
            device_id={"section": jnp.maximum(section - 2, 0)},
        )

    def own(k):
        @pl.when(k >= 2 * half)
        def _():
            lend(k - 2 * half).wait_recv()
            grads[rows_of(k)] = borrowed[k - 2 * half].astype(f32)

        return grads[rows_of(k)]

    def done(k):
        @pl.when(k >= 2 * half)
        def _():
            give_back(k - 2 * half).start()

    skips = (
        (lambda k: (k >= 2 * half) & end) if FAR_LEND else None,
        (lambda k: (k >= 2 * half) & end) if FAR_BACK else None,
    )
    main = Line(place, line, [*line_refs[0:3], sums, line_refs[3]], own, done, pass_on, skips)
    tap_line = Line(place, line, [*line_refs[4:7], tap_sums, line_refs[7]], lambda k: taps[k])
    lent = borrowed.shape[0]
    begin = jnp.where(lender, lent, jnp.where(last, half, 0))
    borrows = last & (count > 2)
    returns = borrows & jnp.logical_not(end) if FAR_BACK else borrows
    finish_at = jnp.where(borrows, 2 * half + lent, 2 * half)

    def kernel_grad(acc, value, ref, size):
        for c in range(size):
            sums_of = [None] * size
            for start in range(0, height, GROUP):
                left = value(pl.ds(start, GROUP), pl.ds(start * width, flat_group))
                moved = ref[
                    pl.ds(start, GROUP + size - 1), pl.ds(EDGE + size - 1 - c - size // 2, width)
                ]
                for r in range(size):
                    part = left * moved[size - 1 - r : size - 1 - r + GROUP]
                    part = jnp.sum(part.reshape(flat_group // 8, 8, LANES), axis=0)
                    sums_of[r] = part if sums_of[r] is None else sums_of[r] + part
            for r in range(size):
                acc[r * size + c] += sums_of[r]

    def kernel_grads(n, b):
        def second_value(_, where):
            return a2[n, where, cols(b)].astype(f32).reshape(GROUP, width, LANES)

        def first_value(some, _):
            return jnp.maximum(xin(n, b, some), 0.0)

        @pl.when(jnp.logical_not(last))
        def _():
            kernel_grad(acc5.at[b], second_value, s5g.at[n, b], 5)

        kernel_grad(acc3.at[b], first_value, s3g.at[n, b], 3)

        @pl.when(n == images - 1)
        def _():
            @pl.when(jnp.logical_not(last))
            def _():
                taps[b, pl.ds(0, 25)] = jnp.sum(acc5[b], axis=1)

            taps[b, pl.ds(TAP_SMALL, 9)] = jnp.sum(acc3[b], axis=1)

    waits = section < count - 2

    def product(at, left, right, start, end):
        shape = ((end - start) * rows, chans)
        left = left[pl.ds(start, end - start)].reshape(shape)
        right = right[pl.ds(start, end - start)].reshape(shape)
        part = dot(left, right, contract_first)
        if start == 0:
            grads[pl.ds(at, chans)] = part
        else:
            grads[pl.ds(at, chans)] += part

    def closing(at, left, right):
        @pl.when(waits)
        def _():
            product(at, left, right, images - 1, images)

        @pl.when(jnp.logical_not(waits))
        def _():
            product(at, left, right, 0, images)

    def weight_grads():
        @pl.when(jnp.logical_not(last))
        def _():
            closing(0, d2, gin)

            @pl.when((main.outer == 0) & jnp.logical_not(lender))
            def _():
                @pl.loop(0, AHEAD)
                def _(k):
                    main.gather(k)

        def hand_out(start, stop):
            @pl.when(lender)
            def _():
                @pl.loop(start, stop)
                def _(k):
                    main.out[k] = grads[rows_of(k)].astype(main.out.dtype)

                    @pl.when(end & FAR_LEND)
                    def _():
                        lend_far(k).start()

                    @pl.when(jnp.logical_not(end & FAR_LEND))
                    def _():
                        lend(k).start()

        hand_out(0, min(half, lent))
        closing(chans, d1, gp1)
        hand_out(min(half, lent), lent)

    @pl.loop(0, images)
    def _(n):
        @pl.when(jnp.logical_not(last))
        def _():
            hand_over(n).wait_recv()
            tmp[...] = dot(gin[n], w2[...], contract_last)

            @pl.loop(0, blocks)
            def _(b):
                shifts = s5g.at[n, b]
                fill(shifts, tmp[:, cols(b)].reshape(height, width, LANES), 5)

                def put(_, where, back):
                    live = a2[n, where, cols(b)].astype(f32) > 0
                    gp1[n, where, cols(b)] = jnp.where(live, back, 0.0).astype(bf16)

                conv(shifts, k5, 5, b, True, put)

        @pl.when(last)
        def _():
            grad = factors[place, pl.ds(8 + n, 1)]
            gin[n] = jnp.broadcast_to(grad, (rows, chans)).astype(bf16)
            back = back_rows[pl.ds(n, 1)]
            live = a2[n].astype(f32) > 0
            gp1[n] = jnp.where(live, back * spread5[...], 0.0).astype(bf16)

        @pl.when((section == 0) & (n == images - 1))
        def _():
            weight_grads()

        tmp[...] = dot(gp1[n], w1[...], contract_last)

        @pl.loop(0, blocks)
        def _(b):
            shifts = s3g.at[n, b]
            fill(shifts, tmp[:, cols(b)].reshape(height, width, LANES), 3)

            @pl.when(section > 0)
            def _():
                def put(some, where, back):
                    live = xin(n, b, some).reshape(flat_group, LANES) > 0
                    grad = gin[n, where, cols(b)].astype(f32) + jnp.where(live, back, 0.0)
                    gout[n, where, cols(b)] = grad.astype(bf16)

                conv(shifts, k3, 3, b, True, put)

        @pl.when(section > 0)
        def _():
            hand_over(n).start()

        @pl.when(waits & (n == images - 2))
        def _():
            product(0, d2, gin, 0, images - 1)
            product(chans, d1, gp1, 0, images - 1)

    @pl.when(late)
    def _():
        second_depth(images // 2, images)

    @pl.when(section > 0)
    def _():
        weight_grads()

    busy = blocks * images
    taps[:, pl.ds(32, 8)] = jnp.zeros((blocks, 8, LANES), f32)

    @pl.when(last)
    def _():
        total = back_rows[pl.ds(0, 1)] * windows[0]
        for n in range(1, images):
            total = total + back_rows[pl.ds(n, 1)] * windows[n]
        for b in range(blocks):
            taps[b, pl.ds(0, 25)] = total[:25, b * LANES : (b + 1) * LANES]


    behind = LAG * (line - 1)
    sent = jnp.where(last | lender, 0, AHEAD)

    @pl.loop(0, jnp.maximum(finish_at - begin, busy + blocks) + behind)
    def _(step):
        for phase in range(3):
            tap_line.advance(phase, step - (busy - blocks + 1), 0, blocks)
            main.advance(phase, step, begin, finish_at - begin, sent)
            if phase == 0:

                @pl.when(step < busy)
                def _():
                    kernel_grads(step // blocks, step % blocks)

    @pl.when(last)
    def _():
        for away in range(1, line):
            take(away).wait_recv()
        left = factors[:, pl.ds(0, 8)].reshape(line * 8, chans)
        right = factors[:, pl.ds(8, 8)].reshape(line * 8, chans)
        left = jnp.concatenate(three_parts(left), axis=0).astype(bf16)
        right = jnp.concatenate([right, right, right], axis=0).astype(bf16)
        value = dot(left, right, contract_first)
        sums[pl.ds(0, half)] = value.reshape(half, chunk_rows, chans).astype(sums.dtype)
        for away in range(1, line):
            give(away).wait_send()

    @pl.loop(0, blocks)
    def _(k):
        tap_line.drain(k)

    @pl.loop(begin, finish_at)
    def _(k):
        main.drain(k)

    @pl.when(lender)
    def _():
        @pl.loop(0, lent)
        def _(k):
            give_back(k).wait_recv()
            lend(k).wait_send()

    @pl.when(returns)
    def _():
        @pl.loop(0, lent)
        def _(k):
            give_back(k).wait_send()

    @pl.when(section > 0)
    def _():
        @pl.loop(0, images)
        def _(n):
            hand_over(n).wait_send()


def finish(
    sums, taps, grad_first, grad_second, grad_small, grad_large,
    narrow, wide, taps_in, small, large, in_sem, out_sem,
):
    pieces, length = narrow.shape[0], narrow.shape[1]
    per_output = pieces // 2
    loads = [
        pltpu.make_async_copy(sums.at[pl.ds(p * length, length)], narrow.at[p], in_sem.at[p])
        for p in range(pieces)
    ]
    stores = [
        pltpu.make_async_copy(
            wide.at[p],
            (grad_second, grad_first)[p // per_output].at[pl.ds(p % per_output * length, length)],
            out_sem.at[p],
        )
        for p in range(pieces)
    ]
    loads.append(pltpu.make_async_copy(taps, taps_in, in_sem.at[pieces]))
    stores.append(pltpu.make_async_copy(small, grad_small, out_sem.at[pieces]))
    stores.append(pltpu.make_async_copy(large, grad_large, out_sem.at[pieces + 1]))
    for load in loads:
        load.start()
    for p in range(pieces):
        loads[p].wait()
        wide[p] = narrow[p].astype(f32)
        stores[p].start()
    loads[pieces].wait()
    for block in range(taps_in.shape[0]):
        where = pl.ds(block * LANES, LANES)
        for tap in range(25):
            large[tap, :, where] = taps_in[block, pl.ds(tap, 1)]
        for tap in range(9):
            small[tap, :, where] = taps_in[block, pl.ds(TAP_SMALL + tap, 1)]
    stores[pieces].start()
    stores[pieces + 1].start()
    for store in stores:
        store.wait()


def per_device(
    activations, depth_small, point_first, depth_large, point_second, head_weight, offsets, labels
):
    x = activations[0]
    images, height, width, chans = x.shape
    rows = height * width
    blocks = chans // LANES
    vmem = pl.BlockSpec(memory_space=pltpu.VMEM)
    smem = pl.BlockSpec(memory_space=pltpu.SMEM)
    anywhere = pl.BlockSpec(memory_space=pl.ANY)

    padded = width + 2 * EDGE
    line = lax.axis_size("dp")
    link = bf16 if line <= 4 else f32
    half = chans // CHUNK_ROWS
    lent = half * LENT // 8
    slots = 2 * half + lent

    def line_scratch(count, length, wide, dtype):
        return [pltpu.VMEM((count, length, wide), dtype)] * 3 + [
            pltpu.SemaphoreType.DMA((6, count))
        ]

    sums, tap_sums = pl.pallas_call(
        kernel,
        out_shape=(
            jax.ShapeDtypeStruct((slots, CHUNK_ROWS, chans), link),
            jax.ShapeDtypeStruct((blocks, TAP_ROWS, LANES), f32),
        ),
        in_specs=[smem, smem, anywhere, vmem, anywhere, vmem, anywhere, anywhere],
        out_specs=(vmem,) * 2,
        scratch_shapes=[
            pltpu.VMEM((images, rows, chans), bf16),
            pltpu.VMEM((images, rows, chans), bf16),
            pltpu.VMEM((images, rows, chans), bf16),
            pltpu.VMEM((images, rows, chans), bf16),
            pltpu.VMEM((images, rows, chans), bf16),
            pltpu.VMEM((images, rows, chans), bf16),
            pltpu.VMEM((rows, chans), f32),
            pltpu.VMEM((height + 4, padded, LANES), f32),
            pltpu.VMEM((height + 2, padded, LANES), f32),
            pltpu.VMEM((images, blocks, height + 4, padded, LANES), f32),
            pltpu.VMEM((images, blocks, height + 2, padded, LANES), f32),
            pltpu.VMEM((images, 8, chans), f32),
            pltpu.VMEM((blocks, 9, 8, LANES), f32),
            pltpu.VMEM((blocks, 25, 8, LANES), f32),
            pltpu.VMEM((blocks, TAP_ROWS, LANES), f32),
            pltpu.VMEM((slots * CHUNK_ROWS, chans), f32),
            pltpu.VMEM((images, MASK_ROWS, chans), f32),
            pltpu.VMEM((MASK_ROWS, chans), f32),
            pltpu.VMEM((rows, chans), f32),
            pltpu.VMEM((MASK_ROWS, rows), bf16),
            pltpu.VMEM((line, 16, chans), f32),
            pltpu.VMEM((16, chans), f32),
            pltpu.VMEM((lent, CHUNK_ROWS, chans), link),
            pltpu.VMEM(x.shape, bf16),
            pltpu.VMEM((chans, chans), bf16),
            pltpu.VMEM((chans, chans), bf16),
            pltpu.VMEM(head_weight.shape, bf16),
            pltpu.SemaphoreType.DMA((images + 3,)),
            pltpu.SemaphoreType.DMA((images,)),
            pltpu.SemaphoreType.DMA((images,)),
            pltpu.SemaphoreType.DMA((line,)),
            pltpu.SemaphoreType.DMA((line,)),
            pltpu.SemaphoreType.DMA((4, lent)),
            *line_scratch(slots, CHUNK_ROWS, chans, link),
            *line_scratch(blocks, TAP_ROWS, LANES, f32),
        ],
        compiler_params=pltpu.CompilerParams(
            collective_id=0, has_side_effects=True, vmem_limit_bytes=56 << 20
        ),
        name="sections",
    )(
        offsets,
        labels,
        x,
        depth_small[0].reshape(9, 1, chans),
        point_first[0],
        depth_large[0].reshape(25, 1, chans),
        point_second[0],
        head_weight,
    )
    sum_first, sum_second, sum_small, sum_large = pl.pallas_call(
        finish,
        out_shape=(
            jax.ShapeDtypeStruct((chans, chans), f32),
            jax.ShapeDtypeStruct((chans, chans), f32),
            jax.ShapeDtypeStruct((9, 1, chans), f32),
            jax.ShapeDtypeStruct((25, 1, chans), f32),
        ),
        in_specs=[anywhere] * 2,
        out_specs=(anywhere,) * 4,
        scratch_shapes=[
            pltpu.VMEM((PIECES, 2 * chans // PIECES, chans), link),
            pltpu.VMEM((PIECES, 2 * chans // PIECES, chans), f32),
            pltpu.VMEM((blocks, TAP_ROWS, LANES), f32),
            pltpu.VMEM((9, 1, chans), f32),
            pltpu.VMEM((25, 1, chans), f32),
            pltpu.SemaphoreType.DMA((PIECES + 1,)),
            pltpu.SemaphoreType.DMA((PIECES + 2,)),
        ],
        compiler_params=pltpu.CompilerParams(vmem_limit_bytes=60 << 20),
        name="finish",
    )(sums.reshape(slots * CHUNK_ROWS, chans), tap_sums)
    return (
        sum_first[None],
        sum_second[None],
        sum_small.reshape(1, 3, 3, chans),
        sum_large.reshape(1, 5, 5, chans),
    )


def solution(mesh):
    placed = (
        P("section", ("groups", "dp"), None, None, None),
        P("section", None, None, None),
        P("section", None, None),
        P("section", None, None, None),
        P("section", None, None),
        P(),
        P(("groups", "dp")),
        P(("groups", "dp")),
    )
    return jax.shard_map(
        per_device,
        mesh=mesh,
        in_specs=placed,
        out_specs=(
            P("section", "groups", None),
            P("section", "groups", None),
            P("section", "groups", None, None),
            P("section", "groups", None, None),
        ),
        check_vma=False,
    )
```

```python
import jax
import jax.numpy as jnp
from jax import lax
from jax.experimental import pallas as pl
from jax.experimental.pallas import tpu as pltpu
from jax.sharding import PartitionSpec as P

BAND = 4
LOSS_SCALE = 64.0
LANES = 128
CHUNK_ROWS = 64
LAG = 4
AHEAD = 4
LENT = 11
FAR_LEND = False
FAR_BACK = True
TAP_ROWS = 40
TAP_SMALL = 25
MASK_ROWS = 32
PIECES = 4
GROUP = 4
EDGE = 8
f32 = jnp.float32
bf16 = jnp.bfloat16
contract_last = (((1,), (1,)), ((), ()))
contract_first = (((0,), (0,)), ((), ()))


def dot(a, b, dims=(((1,), (0,)), ((), ()))):
    return lax.dot_general(a, b, dims, preferred_element_type=f32)


def split_dot(values, matrix, dims):
    rows = values.shape[0]
    high = values.astype(bf16).astype(f32)
    rest = values - high
    mid = rest.astype(bf16).astype(f32)
    low = (rest - mid).astype(bf16).astype(f32)
    parts = jnp.concatenate([high, mid, low, jnp.zeros_like(low)], axis=0).astype(bf16)
    out = dot(parts, matrix, dims)
    return out[:rows] + out[rows : 2 * rows] + out[2 * rows : 3 * rows]


def three_parts(values):
    high = values.astype(bf16).astype(f32)
    rest = values - high
    mid = rest.astype(bf16).astype(f32)
    return high, mid, (rest - mid).astype(bf16).astype(f32)


class Line:
    def __init__(self, place, line, refs, get, done=None, pass_on=None, skips=(None, None)):
        self.place, self.line = place, line
        self.out, self.inner, self.across, self.final, self.sems = refs
        self.get, self.done, self.skips = get, done, skips
        self.pass_on = pass_on or (lambda k: self.outward(k).start())
        self.left = place < line // 2
        self.outer = jnp.where(self.left, place, line - 1 - place)
        self.deep = line // 2 - 1
        self.middle = self.outer == self.deep

    def copy(self, k, src, dst, lane, step):
        way = jnp.where(self.left, step, -step)
        return pltpu.make_async_remote_copy(
            src_ref=src.at[k],
            dst_ref=dst.at[k],
            send_sem=self.sems.at[lane, k],
            recv_sem=self.sems.at[3 + lane, k],
            device_id={"dp": jnp.clip(self.place + way, 0, self.line - 1)},
        )

    def inward(self, k):
        return self.copy(k, self.out, self.inner, 0, 1)

    def exchange(self, k):
        return self.copy(k, self.out, self.across, 1, 1)

    def outward(self, k):
        return self.copy(k, self.final, self.final, 2, -1)

    def advance(self, phase, step, first, chunks, sent=0):
        lag, active, act = (
            (LAG * self.outer, True, self.gather),
            (LAG * (self.deep + 1), self.middle, self.total),
            (LAG * (2 * self.deep + 1 - self.outer), jnp.logical_not(self.middle), self.spread),
        )[phase]
        k = step - lag

        if phase == 0:
            active = (self.outer > 0) | (k + first >= sent)
        skip = self.skips[phase // 2]
        if phase != 1 and skip is not None:
            active = active & jnp.logical_not(skip(k + first))

        @pl.when(active & (k >= 0) & (k < chunks))
        def _():
            act(k + first)

    def gather(self, k):
        dtype = self.out.dtype
        end = self.outer == 0

        @pl.when(end)
        def _():
            self.out[k] = self.get(k).astype(dtype)

        @pl.when(jnp.logical_not(end))
        def _():
            self.inward(k).wait_recv()
            self.out[k] = (self.get(k) + self.inner[k].astype(f32)).astype(dtype)

        @pl.when(self.middle)
        def _():
            self.exchange(k).start()

        @pl.when(jnp.logical_not(self.middle))
        def _():
            self.inward(k).start()

    def total(self, k):
        self.exchange(k).wait_recv()
        value = self.out[k].astype(f32) + self.across[k].astype(f32)
        self.final[k] = value.astype(self.final.dtype)

        @pl.when(self.outer > 0)
        def _():
            self.pass_on(k)

        if self.done is not None:
            self.done(k)

    def spread(self, k):
        self.outward(k).wait_recv()

        @pl.when(self.outer > 0)
        def _():
            self.pass_on(k)

        if self.done is not None:
            self.done(k)

    def drain(self, k):
        @pl.when(self.middle)
        def _():
            self.exchange(k).wait_send()

        sends = jnp.logical_not(self.middle)
        if self.skips[0] is not None:
            sends = sends & jnp.logical_not(self.skips[0](k))

        @pl.when(sends)
        def _():
            self.inward(k).wait_send()

        @pl.when(self.outer > 0)
        def _():
            self.outward(k).wait_send()


def kernel(
    offsets, labels, x_in, k3, w1_in, k5, w2_in, head_in,
    sums_out, tap_sums,
    sums, out_sems, d1, a2, d2, gin, gp1, gout, tmp, s5f, s3f, s5g, s3g, pool, acc3, acc5, taps,
    grads, windows, k5_rows, spread5, push, factors,
    w1t, w2t, back_rows, borrowed, x, w1, w2, head, load_sems, send_sem, recv_sem, factor_send, factor_recv, lend_sems, *line_refs,
):
    section = lax.axis_index("section")
    count = lax.axis_size("section")
    images, height, width, chans = x.shape
    rows = height * width
    blocks = chans // LANES
    last = section == count - 1
    scale = 1.0 / rows

    def load(source, target, index):
        return pltpu.make_async_copy(source, target, load_sems.at[index])

    def load_x(n):
        return load(x_in.at[n], x.at[n], n)

    load_w1, load_w2 = load(w1_in, w1, images), load(w2_in, w2, images + 1)
    load_head = load(head_in, head, images + 2)

    for n in range(images):
        load_x(n).start()
    load_w1.start()
    load_w2.start()

    @pl.when(last)
    def _():
        load_head.start()

    barrier = pltpu.get_barrier_semaphore()

    @pl.when(section > 0)
    def _():
        pl.semaphore_signal(barrier, inc=1, device_id={"section": section - 1})

    @pl.when(section < count - 1)
    def _():
        pl.semaphore_signal(barrier, inc=1, device_id={"section": section + 1})

    place = lax.axis_index("dp")
    line = lax.axis_size("dp")

    for away in range(1, line):
        pl.semaphore_signal(barrier, inc=1, device_id={"dp": lax.rem(place + away, line)})

    lender = section == count - 3

    @pl.when(lender)
    def _():
        pl.semaphore_signal(barrier, inc=1, device_id={"section": jnp.minimum(section + 2, count - 1)})

    @pl.when(last & (count > 2))
    def _():
        pl.semaphore_signal(barrier, inc=1, device_id={"section": jnp.maximum(section - 2, 0)})

    on_left = place < line // 2
    outer = jnp.where(on_left, place, line - 1 - place)
    inner_place = jnp.clip(jnp.where(on_left, place + 1, place - 1), 0, line - 1)
    outer_place = jnp.clip(jnp.where(on_left, place - 1, place + 1), 0, line - 1)
    end = (outer == 0) & (line > 2)
    lends_far = lender & end
    backs_far = last & (count > 2) & (outer == 1)

    @pl.when(lends_far)
    def _():
        pl.semaphore_signal(
            barrier,
            inc=1,
            device_id={"dp": inner_place, "section": jnp.minimum(section + 2, count - 1)},
        )

    @pl.when(backs_far)
    def _():
        pl.semaphore_signal(
            barrier, inc=1, device_id={"dp": outer_place, "section": jnp.maximum(section - 2, 0)}
        )

    def cols(block):
        return pl.ds(pl.multiple_of(block * LANES, LANES), LANES)

    col_index = lax.broadcasted_iota(jnp.int32, (1, width, LANES), 1)

    def fill(ref, value, size):
        ref[pl.ds(size // 2, height), pl.ds(EDGE, width)] = value

    def clear(ref, size):
        radius = size // 2
        side = jnp.zeros((height + 2 * radius, EDGE, LANES), f32)
        ref[:, pl.ds(0, EDGE)] = side
        ref[:, pl.ds(EDGE + width, EDGE)] = side
        zero = jnp.zeros((radius, width, LANES), f32)
        ref[pl.ds(0, radius), pl.ds(EDGE, width)] = zero
        ref[pl.ds(radius + height, radius), pl.ds(EDGE, width)] = zero

    flat_group = GROUP * width

    def conv(ref, weights, size, block, flip, put):
        for start in range(0, height, GROUP):
            total = None
            for c in range(size):
                moved = ref[pl.ds(start, GROUP + size - 1), pl.ds(EDGE + c - size // 2, width)]
                for r in range(size):
                    tap = r * size + c
                    tap = size * size - 1 - tap if flip else tap
                    part = weights[tap, :, cols(block)] * moved[r : r + GROUP]
                    total = part if total is None else total + part
            put(pl.ds(start, GROUP), pl.ds(start * width, flat_group), total.reshape(flat_group, LANES))

    def kept(image):
        away = col_index - offsets[image]
        away = jnp.where(away < 0, away + width, away)
        return jnp.where((away < BAND) | (section > 0), 1.0, 0.0)

    def xin(image, block, some=slice(None)):
        return x[image, some, :, cols(block)].astype(f32) * kept(image)

    clear(s5f, 5)
    clear(s3f, 3)

    acc5[...] = jnp.zeros_like(acc5)
    acc3[...] = jnp.zeros_like(acc3)

    @pl.loop(0, images)
    def _(n):
        @pl.loop(0, blocks)
        def _(b):
            clear(s3g.at[n, b], 3)

            @pl.when(jnp.logical_not(last))
            def _():
                clear(s5g.at[n, b], 5)

    def window_mask():
        tap = lax.broadcasted_iota(jnp.int32, (MASK_ROWS, rows), 0)
        spot = lax.broadcasted_iota(jnp.int32, (MASK_ROWS, rows), 1)
        i, h = jnp.zeros_like(tap), jnp.zeros_like(spot)
        for step in range(1, 5):
            i = i + jnp.where(tap >= 5 * step, 1, 0)
        for step in range(1, height):
            h = h + jnp.where(spot >= width * step, 1, 0)
        down, along = h - i + 2, (spot - width * h) - (tap - 5 * i) + 2
        inside = (down >= 0) & (down < height) & (along >= 0) & (along < width) & (tap < 25)
        return jnp.where(inside, 1.0, 0.0)

    @pl.when(last)
    def _():
        mask = window_mask()
        push[...] = mask.astype(bf16)
        k5_rows[pl.ds(24, 8)] = jnp.zeros((8, chans), f32)
        for tap in range(25):
            k5_rows[pl.ds(tap, 1)] = k5[tap]
        parts = jnp.concatenate(three_parts(k5_rows[...]), axis=0).astype(bf16)
        masks = jnp.concatenate([mask, mask, mask], axis=0).astype(bf16)
        spread5[...] = dot(masks, parts, contract_first)

    @pl.loop(0, images)
    def _(n):
        load_x(n).wait()

        @pl.loop(0, blocks)
        def _(b):
            value = xin(n, b)
            pool[n, :, cols(b)] = jnp.sum(value.reshape(rows // 8, 8, LANES), axis=0)
            fill(s3f, jnp.maximum(value, 0.0), 3)

            def put(_, where, out):
                d1[n, where, cols(b)] = out.astype(bf16)

            conv(s3f, k3, 3, b, False, put)

    flat = (images * rows, chans)
    load_w1.wait()
    a2[...] = jnp.maximum(dot(d1[...].reshape(flat), w1[...]), 0.0).astype(bf16).reshape(a2.shape)

    @pl.when(last)
    def _():
        for n in range(images):
            windows[n] = dot(push[...], a2[n])

    def second_depth(start, end):
        @pl.loop(start, end)
        def _(n):
            @pl.loop(0, blocks)
            def _(b):
                value = a2[n, :, cols(b)].astype(f32).reshape(height, width, LANES)
                fill(s5f, value, 5)

                def put(_, where, out):
                    d2[n, where, cols(b)] = out.astype(bf16)

                conv(s5f, k5, 5, b, False, put)

    late = section == count - 2

    load_w2.wait()
    early = jnp.where(late, images // 2, images)

    @pl.when(jnp.logical_not(last))
    def _():
        second_depth(0, early)
        w1t[...] = w1[...].T
        w2t[...] = w2[...].T

    classes = head.shape[0]

    @pl.when(last)
    def _():
        load_head.wait()
        x_sums = [jnp.sum(pool[n], axis=0, keepdims=True) for n in range(images)]
        d2_sums = [
            jnp.sum(k5_rows[...] * windows[n], axis=0, keepdims=True) for n in range(images)
        ]
        twice = -(-2 * images // 8) * 8
        fill_rows = [jnp.zeros((twice - 2 * images, chans), f32)] if twice > 2 * images else []
        x_sum = jnp.concatenate(x_sums + x_sums + fill_rows, axis=0)
        d2_sum = jnp.concatenate(d2_sums + d2_sums + fill_rows, axis=0)
        pooled = (x_sum + split_dot(d2_sum, w2[...], (((1,), (0,)), ((), ())))) * scale
        rest = jnp.zeros((LANES - twice, chans), f32)
        wide = jnp.concatenate([pooled, rest], axis=0)
        high = wide.astype(bf16)
        mid = (wide - high.astype(f32)).astype(bf16)
        logits = dot(head[...], high, contract_last) + dot(head[...], mid, contract_last)
        class_index = lax.broadcasted_iota(jnp.int32, (classes, LANES), 0)
        lane = lax.broadcasted_iota(jnp.int32, (1, LANES), 1)
        label_row = jnp.full((1, LANES), -1, jnp.int32)
        for n in range(images):
            label_row = jnp.where((lane == n) | (lane == n + images), labels[n], label_row)
        dlog = LOSS_SCALE * (logits - jnp.where(class_index == label_row, 1.0, 0.0))
        high = dlog.astype(bf16).astype(f32)
        part = jnp.where(lane < images, high, dlog - high).astype(bf16)
        both = dot(part, head[...], contract_first)
        grad = ((both[:images] + both[images : 2 * images]) * scale).astype(bf16).astype(f32)
        pad = jnp.zeros((8 - images, chans), f32)
        factors[place, pl.ds(0, 8)] = jnp.concatenate([*d2_sums, pad], axis=0)
        factors[place, pl.ds(8, 8)] = jnp.concatenate([grad, pad], axis=0)
        wide = jnp.concatenate([grad, jnp.zeros((16 - images, chans), f32)], axis=0)
        back_rows[...] = dot(wide.astype(bf16), w2[...], contract_last)

    def hand_over(n):
        return pltpu.make_async_remote_copy(
            src_ref=gout.at[n],
            dst_ref=gin.at[n],
            send_sem=send_sem.at[n],
            recv_sem=recv_sem.at[n],
            device_id={"section": jnp.maximum(section - 1, 0)},
        )

    pl.semaphore_wait(
        barrier,
        jnp.where(section > 0, 1, 0)
        + jnp.where(section < count - 1, 1, 0)
        + jnp.where(lender | (last & (count > 2)), 1, 0)
        + jnp.where(lends_far | backs_far, 1, 0)
        + (line - 1),
    )

    def give(away):
        other = lax.rem(place + away, line)
        return pltpu.make_async_remote_copy(
            src_ref=factors.at[place],
            dst_ref=factors.at[place],
            send_sem=factor_send.at[away],
            recv_sem=factor_recv.at[away],
            device_id={"dp": other},
        )

    def take(away):
        other = lax.rem(place + line - away, line)
        return pltpu.make_async_remote_copy(
            src_ref=factors.at[other],
            dst_ref=factors.at[other],
            send_sem=factor_send.at[away],
            recv_sem=factor_recv.at[away],
            device_id={"dp": lax.rem(place + away, line)},
        )

    @pl.when(last)
    def _():
        for away in range(1, line):
            give(away).start()

    chunk_rows = CHUNK_ROWS
    half = chans // chunk_rows

    def rows_of(k):
        return pl.ds(pl.multiple_of(k * chunk_rows, chunk_rows), chunk_rows)

    def lend(k):
        return pltpu.make_async_remote_copy(
            src_ref=line_refs[0].at[k],
            dst_ref=borrowed.at[k],
            send_sem=lend_sems.at[0, k],
            recv_sem=lend_sems.at[1, k],
            device_id={"section": jnp.minimum(section + 2, count - 1)},
        )

    def lend_far(k):
        return pltpu.make_async_remote_copy(
            src_ref=line_refs[0].at[k],
            dst_ref=line_refs[1].at[k + 2 * half],
            send_sem=lend_sems.at[0, k],
            recv_sem=line_refs[3].at[3, k + 2 * half],
            device_id={"dp": inner_place, "section": jnp.minimum(section + 2, count - 1)},
        )

    def back_far(k):
        return pltpu.make_async_remote_copy(
            src_ref=sums.at[k],
            dst_ref=sums.at[k - 2 * half],
            send_sem=line_refs[3].at[2, k],
            recv_sem=lend_sems.at[3, k - 2 * half],
            device_id={"dp": outer_place, "section": jnp.maximum(section - 2, 0)},
        )

    def pass_on(k):
        far = (k >= 2 * half) & (outer == 1) & FAR_BACK

        @pl.when(far)
        def _():
            back_far(k).start()

        @pl.when(jnp.logical_not(far))
        def _():
            main.outward(k).start()

    def give_back(k):
        return pltpu.make_async_remote_copy(
            src_ref=sums.at[k + 2 * half],
            dst_ref=sums.at[k],
            send_sem=lend_sems.at[2, k],
            recv_sem=lend_sems.at[3, k],
            device_id={"section": jnp.maximum(section - 2, 0)},
        )

    def own(k):
        @pl.when(k >= 2 * half)
        def _():
            lend(k - 2 * half).wait_recv()
            grads[rows_of(k)] = borrowed[k - 2 * half].astype(f32)

        return grads[rows_of(k)]

    def write_out(k):
        return pltpu.make_async_copy(sums.at[k], sums_out.at[k], out_sems.at[k])

    def done(k):
        @pl.when(k >= 2 * half)
        def _():
            give_back(k - 2 * half).start()

        @pl.when(k < 2 * half)
        def _():
            write_out(k).start()

    skips = (
        (lambda k: (k >= 2 * half) & end) if FAR_LEND else None,
        (lambda k: (k >= 2 * half) & end) if FAR_BACK else None,
    )
    main = Line(place, line, [*line_refs[0:3], sums, line_refs[3]], own, done, pass_on, skips)
    tap_line = Line(place, line, [*line_refs[4:7], tap_sums, line_refs[7]], lambda k: taps[k])
    lent = borrowed.shape[0]
    begin = jnp.where(lender, lent, jnp.where(last, half, 0))
    borrows = last & (count > 2)
    returns = borrows & jnp.logical_not(end) if FAR_BACK else borrows
    finish_at = jnp.where(borrows, 2 * half + lent, 2 * half)

    def kernel_grad(acc, value, ref, size):
        for c in range(size):
            sums_of = [None] * size
            for start in range(0, height, GROUP):
                left = value(pl.ds(start, GROUP), pl.ds(start * width, flat_group))
                moved = ref[
                    pl.ds(start, GROUP + size - 1), pl.ds(EDGE + size - 1 - c - size // 2, width)
                ]
                for r in range(size):
                    part = left * moved[size - 1 - r : size - 1 - r + GROUP]
                    part = jnp.sum(part.reshape(flat_group // 8, 8, LANES), axis=0)
                    sums_of[r] = part if sums_of[r] is None else sums_of[r] + part
            for r in range(size):
                acc[r * size + c] += sums_of[r]

    def kernel_grads(n, b):
        def second_value(_, where):
            return a2[n, where, cols(b)].astype(f32).reshape(GROUP, width, LANES)

        def first_value(some, _):
            return jnp.maximum(xin(n, b, some), 0.0)

        @pl.when(jnp.logical_not(last))
        def _():
            kernel_grad(acc5.at[b], second_value, s5g.at[n, b], 5)

        kernel_grad(acc3.at[b], first_value, s3g.at[n, b], 3)

        @pl.when(n == images - 1)
        def _():
            @pl.when(jnp.logical_not(last))
            def _():
                taps[b, pl.ds(0, 25)] = jnp.sum(acc5[b], axis=1)

            taps[b, pl.ds(TAP_SMALL, 9)] = jnp.sum(acc3[b], axis=1)

    waits = section < count - 2

    def product(at, left, right, start, end):
        shape = ((end - start) * rows, chans)
        left = left[pl.ds(start, end - start)].reshape(shape)
        right = right[pl.ds(start, end - start)].reshape(shape)
        part = dot(left, right, contract_first)
        if start == 0:
            grads[pl.ds(at, chans)] = part
        else:
            grads[pl.ds(at, chans)] += part

    def closing(at, left, right):
        @pl.when(waits)
        def _():
            product(at, left, right, images - 1, images)

        @pl.when(jnp.logical_not(waits))
        def _():
            product(at, left, right, 0, images)

    def weight_grads():
        @pl.when(jnp.logical_not(last))
        def _():
            closing(0, d2, gin)

            @pl.when((main.outer == 0) & jnp.logical_not(lender))
            def _():
                @pl.loop(0, AHEAD)
                def _(k):
                    main.gather(k)

        def hand_out(start, stop):
            @pl.when(lender)
            def _():
                @pl.loop(start, stop)
                def _(k):
                    main.out[k] = grads[rows_of(k)].astype(main.out.dtype)

                    @pl.when(end & FAR_LEND)
                    def _():
                        lend_far(k).start()

                    @pl.when(jnp.logical_not(end & FAR_LEND))
                    def _():
                        lend(k).start()

        hand_out(0, min(half, lent))
        closing(chans, d1, gp1)
        hand_out(min(half, lent), lent)

    @pl.loop(0, images)
    def _(n):
        @pl.when(jnp.logical_not(last))
        def _():
            hand_over(n).wait_recv()
            tmp[...] = dot(gin[n], w2t[...])

            @pl.loop(0, blocks)
            def _(b):
                shifts = s5g.at[n, b]
                fill(shifts, tmp[:, cols(b)].reshape(height, width, LANES), 5)

                def put(_, where, back):
                    live = a2[n, where, cols(b)].astype(f32) > 0
                    gp1[n, where, cols(b)] = jnp.where(live, back, 0.0).astype(bf16)

                conv(shifts, k5, 5, b, True, put)

        @pl.when(last)
        def _():
            grad = factors[place, pl.ds(8 + n, 1)]
            gin[n] = jnp.broadcast_to(grad, (rows, chans)).astype(bf16)
            back = back_rows[pl.ds(n, 1)]
            live = a2[n].astype(f32) > 0
            gp1[n] = jnp.where(live, back * spread5[...], 0.0).astype(bf16)

        @pl.when((section == 0) & (n == images - 1))
        def _():
            weight_grads()

        @pl.when(last)
        def _():
            tmp[...] = dot(gp1[n], w1[...], contract_last)

        @pl.when(jnp.logical_not(last))
        def _():
            tmp[...] = dot(gp1[n], w1t[...])

        @pl.loop(0, blocks)
        def _(b):
            shifts = s3g.at[n, b]
            fill(shifts, tmp[:, cols(b)].reshape(height, width, LANES), 3)

            @pl.when(section > 0)
            def _():
                def put(some, where, back):
                    live = xin(n, b, some).reshape(flat_group, LANES) > 0
                    grad = gin[n, where, cols(b)].astype(f32) + jnp.where(live, back, 0.0)
                    gout[n, where, cols(b)] = grad.astype(bf16)

                conv(shifts, k3, 3, b, True, put)

        @pl.when(section > 0)
        def _():
            hand_over(n).start()

        @pl.when(waits & (n == images - 2))
        def _():
            product(0, d2, gin, 0, images - 1)
            product(chans, d1, gp1, 0, images - 1)

    @pl.when(late)
    def _():
        second_depth(images // 2, images)

    @pl.when(section > 0)
    def _():
        weight_grads()

    busy = blocks * images
    taps[:, pl.ds(32, 8)] = jnp.zeros((blocks, 8, LANES), f32)

    @pl.when(last)
    def _():
        total = back_rows[pl.ds(0, 1)] * windows[0]
        for n in range(1, images):
            total = total + back_rows[pl.ds(n, 1)] * windows[n]
        for b in range(blocks):
            taps[b, pl.ds(0, 25)] = total[:25, b * LANES : (b + 1) * LANES]


    behind = LAG * (line - 1)
    sent = jnp.where(last | lender, 0, AHEAD)

    @pl.loop(0, jnp.maximum(finish_at - begin, busy + blocks) + behind)
    def _(step):
        for phase in range(3):
            tap_line.advance(phase, step - (busy - blocks + 1), 0, blocks)
            main.advance(phase, step, begin, finish_at - begin, sent)
            if phase == 0:

                @pl.when(step < busy)
                def _():
                    kernel_grads(step // blocks, step % blocks)

    @pl.when(last)
    def _():
        for away in range(1, line):
            take(away).wait_recv()
        left = factors[:, pl.ds(0, 8)].reshape(line * 8, chans)
        right = factors[:, pl.ds(8, 8)].reshape(line * 8, chans)
        left = jnp.concatenate(three_parts(left), axis=0).astype(bf16)
        right = jnp.concatenate([right, right, right], axis=0).astype(bf16)
        value = dot(left, right, contract_first)
        sums[pl.ds(0, half)] = value.reshape(half, chunk_rows, chans).astype(sums.dtype)

        @pl.loop(0, half)
        def _(k):
            write_out(k).start()

        for away in range(1, line):
            give(away).wait_send()

    @pl.loop(0, blocks)
    def _(k):
        tap_line.drain(k)

    @pl.loop(begin, finish_at)
    def _(k):
        main.drain(k)

    @pl.when(lender)
    def _():
        @pl.loop(0, lent)
        def _(k):
            give_back(k).wait_recv()
            write_out(k).start()
            lend(k).wait_send()

    @pl.when(returns)
    def _():
        @pl.loop(0, lent)
        def _(k):
            give_back(k).wait_send()

    @pl.when(section > 0)
    def _():
        @pl.loop(0, images)
        def _(n):
            hand_over(n).wait_send()

    @pl.loop(0, 2 * half)
    def _(k):
        write_out(k).wait()


def finish(
    sums, taps, grad_first, grad_second, grad_small, grad_large,
    narrow, wide, taps_in, small, large, in_sem, out_sem,
):
    pieces, length = narrow.shape[0], narrow.shape[1]
    per_output = pieces // 2
    loads = [
        pltpu.make_async_copy(sums.at[pl.ds(p * length, length)], narrow.at[p], in_sem.at[p])
        for p in range(pieces)
    ]
    stores = [
        pltpu.make_async_copy(
            wide.at[p],
            (grad_second, grad_first)[p // per_output].at[pl.ds(p % per_output * length, length)],
            out_sem.at[p],
        )
        for p in range(pieces)
    ]
    loads.append(pltpu.make_async_copy(taps, taps_in, in_sem.at[pieces]))
    stores.append(pltpu.make_async_copy(small, grad_small, out_sem.at[pieces]))
    stores.append(pltpu.make_async_copy(large, grad_large, out_sem.at[pieces + 1]))
    for load in loads:
        load.start()
    for p in range(pieces):
        loads[p].wait()
        wide[p] = narrow[p].astype(f32)
        stores[p].start()
    loads[pieces].wait()
    for block in range(taps_in.shape[0]):
        where = pl.ds(block * LANES, LANES)
        for tap in range(25):
            large[tap, :, where] = taps_in[block, pl.ds(tap, 1)]
        for tap in range(9):
            small[tap, :, where] = taps_in[block, pl.ds(TAP_SMALL + tap, 1)]
    stores[pieces].start()
    stores[pieces + 1].start()
    for store in stores:
        store.wait()


def per_device(
    activations, depth_small, point_first, depth_large, point_second, head_weight, offsets, labels
):
    x = activations[0]
    images, height, width, chans = x.shape
    rows = height * width
    blocks = chans // LANES
    vmem = pl.BlockSpec(memory_space=pltpu.VMEM)
    smem = pl.BlockSpec(memory_space=pltpu.SMEM)
    anywhere = pl.BlockSpec(memory_space=pl.ANY)

    padded = width + 2 * EDGE
    line = lax.axis_size("dp")
    link = bf16 if line <= 4 else f32
    half = chans // CHUNK_ROWS
    lent = half * LENT // 8
    slots = 2 * half + lent

    def line_scratch(count, length, wide, dtype):
        return [pltpu.VMEM((count, length, wide), dtype)] * 3 + [
            pltpu.SemaphoreType.DMA((6, count))
        ]

    sums, tap_sums = pl.pallas_call(
        kernel,
        out_shape=(
            jax.ShapeDtypeStruct((2 * half, CHUNK_ROWS, chans), link),
            jax.ShapeDtypeStruct((blocks, TAP_ROWS, LANES), f32),
        ),
        in_specs=[smem, smem, anywhere, vmem, anywhere, vmem, anywhere, anywhere],
        out_specs=(anywhere, vmem),
        scratch_shapes=[
            pltpu.VMEM((slots, CHUNK_ROWS, chans), link),
            pltpu.SemaphoreType.DMA((2 * half,)),
            pltpu.VMEM((images, rows, chans), bf16),
            pltpu.VMEM((images, rows, chans), bf16),
            pltpu.VMEM((images, rows, chans), bf16),
            pltpu.VMEM((images, rows, chans), bf16),
            pltpu.VMEM((images, rows, chans), bf16),
            pltpu.VMEM((images, rows, chans), bf16),
            pltpu.VMEM((rows, chans), f32),
            pltpu.VMEM((height + 4, padded, LANES), f32),
            pltpu.VMEM((height + 2, padded, LANES), f32),
            pltpu.VMEM((images, blocks, height + 4, padded, LANES), f32),
            pltpu.VMEM((images, blocks, height + 2, padded, LANES), f32),
            pltpu.VMEM((images, 8, chans), f32),
            pltpu.VMEM((blocks, 9, 8, LANES), f32),
            pltpu.VMEM((blocks, 25, 8, LANES), f32),
            pltpu.VMEM((blocks, TAP_ROWS, LANES), f32),
            pltpu.VMEM((slots * CHUNK_ROWS, chans), f32),
            pltpu.VMEM((images, MASK_ROWS, chans), f32),
            pltpu.VMEM((MASK_ROWS, chans), f32),
            pltpu.VMEM((rows, chans), f32),
            pltpu.VMEM((MASK_ROWS, rows), bf16),
            pltpu.VMEM((line, 16, chans), f32),
            pltpu.VMEM((chans, chans), bf16),
            pltpu.VMEM((chans, chans), bf16),
            pltpu.VMEM((16, chans), f32),
            pltpu.VMEM((lent, CHUNK_ROWS, chans), link),
            pltpu.VMEM(x.shape, bf16),
            pltpu.VMEM((chans, chans), bf16),
            pltpu.VMEM((chans, chans), bf16),
            pltpu.VMEM(head_weight.shape, bf16),
            pltpu.SemaphoreType.DMA((images + 3,)),
            pltpu.SemaphoreType.DMA((images,)),
            pltpu.SemaphoreType.DMA((images,)),
            pltpu.SemaphoreType.DMA((line,)),
            pltpu.SemaphoreType.DMA((line,)),
            pltpu.SemaphoreType.DMA((4, lent)),
            *line_scratch(slots, CHUNK_ROWS, chans, link),
            *line_scratch(blocks, TAP_ROWS, LANES, f32),
        ],
        compiler_params=pltpu.CompilerParams(
            collective_id=0, has_side_effects=True, vmem_limit_bytes=56 << 20
        ),
        name="sections",
    )(
        offsets,
        labels,
        x,
        depth_small[0].reshape(9, 1, chans),
        point_first[0],
        depth_large[0].reshape(25, 1, chans),
        point_second[0],
        head_weight,
    )
    sum_first, sum_second, sum_small, sum_large = pl.pallas_call(
        finish,
        out_shape=(
            jax.ShapeDtypeStruct((chans, chans), f32),
            jax.ShapeDtypeStruct((chans, chans), f32),
            jax.ShapeDtypeStruct((9, 1, chans), f32),
            jax.ShapeDtypeStruct((25, 1, chans), f32),
        ),
        in_specs=[anywhere] * 2,
        out_specs=(anywhere,) * 4,
        scratch_shapes=[
            pltpu.VMEM((PIECES, 2 * chans // PIECES, chans), link),
            pltpu.VMEM((PIECES, 2 * chans // PIECES, chans), f32),
            pltpu.VMEM((blocks, TAP_ROWS, LANES), f32),
            pltpu.VMEM((9, 1, chans), f32),
            pltpu.VMEM((25, 1, chans), f32),
            pltpu.SemaphoreType.DMA((PIECES + 1,)),
            pltpu.SemaphoreType.DMA((PIECES + 2,)),
        ],
        compiler_params=pltpu.CompilerParams(vmem_limit_bytes=60 << 20),
        name="finish",
    )(sums.reshape(2 * chans, chans), tap_sums)
    return (
        sum_first[None],
        sum_second[None],
        sum_small.reshape(1, 3, 3, chans),
        sum_large.reshape(1, 5, 5, chans),
    )


def solution(mesh):
    placed = (
        P("section", ("groups", "dp"), None, None, None),
        P("section", None, None, None),
        P("section", None, None),
        P("section", None, None, None),
        P("section", None, None),
        P(),
        P(("groups", "dp")),
        P(("groups", "dp")),
    )
    return jax.shard_map(
        per_device,
        mesh=mesh,
        in_specs=placed,
        out_specs=(
            P("section", "groups", None),
            P("section", "groups", None),
            P("section", "groups", None, None),
            P("section", "groups", None, None),
        ),
        check_vma=False,
    )
```

```python
import jax
import jax.numpy as jnp
from jax import lax
from jax.experimental import pallas as pl
from jax.experimental.pallas import tpu as pltpu
from jax.sharding import PartitionSpec as P

BAND = 4
LOSS_SCALE = 64.0
LANES = 128
CHUNK_ROWS = 64
LAG = 4
AHEAD = 4
LENT = 11
FAR_LEND = False
FAR_BACK = True
TAP_ROWS = 40
TAP_SMALL = 25
MASK_ROWS = 32
PIECES = 4
GROUP = 4
EDGE = 8
f32 = jnp.float32
bf16 = jnp.bfloat16
contract_last = (((1,), (1,)), ((), ()))
contract_first = (((0,), (0,)), ((), ()))


def dot(a, b, dims=(((1,), (0,)), ((), ()))):
    return lax.dot_general(a, b, dims, preferred_element_type=f32)


def split_dot(values, matrix, dims):
    rows = values.shape[0]
    high = values.astype(bf16).astype(f32)
    rest = values - high
    mid = rest.astype(bf16).astype(f32)
    low = (rest - mid).astype(bf16).astype(f32)
    parts = jnp.concatenate([high, mid, low, jnp.zeros_like(low)], axis=0).astype(bf16)
    out = dot(parts, matrix, dims)
    return out[:rows] + out[rows : 2 * rows] + out[2 * rows : 3 * rows]


def three_parts(values):
    high = values.astype(bf16).astype(f32)
    rest = values - high
    mid = rest.astype(bf16).astype(f32)
    return high, mid, (rest - mid).astype(bf16).astype(f32)


class Line:
    def __init__(self, place, line, refs, get, done=None, pass_on=None, skips=(None, None)):
        self.place, self.line = place, line
        self.out, self.inner, self.across, self.final, self.sems = refs
        self.get, self.done, self.skips = get, done, skips
        self.pass_on = pass_on or (lambda k: self.outward(k).start())
        self.left = place < line // 2
        self.outer = jnp.where(self.left, place, line - 1 - place)
        self.deep = line // 2 - 1
        self.middle = self.outer == self.deep

    def copy(self, k, src, dst, lane, step):
        way = jnp.where(self.left, step, -step)
        return pltpu.make_async_remote_copy(
            src_ref=src.at[k],
            dst_ref=dst.at[k],
            send_sem=self.sems.at[lane, k],
            recv_sem=self.sems.at[3 + lane, k],
            device_id={"dp": jnp.clip(self.place + way, 0, self.line - 1)},
        )

    def inward(self, k):
        return self.copy(k, self.out, self.inner, 0, 1)

    def exchange(self, k):
        return self.copy(k, self.out, self.across, 1, 1)

    def outward(self, k):
        return self.copy(k, self.final, self.final, 2, -1)

    def advance(self, phase, step, first, chunks, sent=0):
        lag, active, act = (
            (LAG * self.outer, True, self.gather),
            (LAG * (self.deep + 1), self.middle, self.total),
            (LAG * (2 * self.deep + 1 - self.outer), jnp.logical_not(self.middle), self.spread),
        )[phase]
        k = step - lag

        if phase == 0:
            active = (self.outer > 0) | (k + first >= sent)
        skip = self.skips[phase // 2]
        if phase != 1 and skip is not None:
            active = active & jnp.logical_not(skip(k + first))

        @pl.when(active & (k >= 0) & (k < chunks))
        def _():
            act(k + first)

    def gather(self, k):
        dtype = self.out.dtype
        end = self.outer == 0

        @pl.when(end)
        def _():
            self.out[k] = self.get(k).astype(dtype)

        @pl.when(jnp.logical_not(end))
        def _():
            self.inward(k).wait_recv()
            self.out[k] = (self.get(k) + self.inner[k].astype(f32)).astype(dtype)

        @pl.when(self.middle)
        def _():
            self.exchange(k).start()

        @pl.when(jnp.logical_not(self.middle))
        def _():
            self.inward(k).start()

    def total(self, k):
        self.exchange(k).wait_recv()
        value = self.out[k].astype(f32) + self.across[k].astype(f32)
        self.final[k] = value.astype(self.final.dtype)

        @pl.when(self.outer > 0)
        def _():
            self.pass_on(k)

        if self.done is not None:
            self.done(k)

    def spread(self, k):
        self.outward(k).wait_recv()

        @pl.when(self.outer > 0)
        def _():
            self.pass_on(k)

        if self.done is not None:
            self.done(k)

    def drain(self, k):
        @pl.when(self.middle)
        def _():
            self.exchange(k).wait_send()

        sends = jnp.logical_not(self.middle)
        if self.skips[0] is not None:
            sends = sends & jnp.logical_not(self.skips[0](k))

        @pl.when(sends)
        def _():
            self.inward(k).wait_send()

        @pl.when(self.outer > 0)
        def _():
            self.outward(k).wait_send()


def kernel(
    offsets, labels, x_in, k3, w1_in, k5, w2_in, head_in,
    sums_out, tap_sums,
    sums, out_sems, d1, a2, d2, gin, gp1, gout, tmp, s5f, s3f, s5g, s3g, pool, acc3, acc5, taps,
    grads, windows, k5_rows, spread5, push, factors,
    w1t, w2t, back_rows, borrowed, x, w1, w2, head, load_sems, send_sem, recv_sem, factor_send, factor_recv, lend_sems, *line_refs,
):
    section = lax.axis_index("section")
    count = lax.axis_size("section")
    images, height, width, chans = x.shape
    rows = height * width
    blocks = chans // LANES
    last = section == count - 1
    scale = 1.0 / rows

    def load(source, target, index):
        return pltpu.make_async_copy(source, target, load_sems.at[index])

    def load_x(n):
        return load(x_in.at[n], x.at[n], n)

    load_w1, load_w2 = load(w1_in, w1, images), load(w2_in, w2, images + 1)
    load_head = load(head_in, head, images + 2)

    for n in range(images):
        load_x(n).start()
    load_w1.start()
    load_w2.start()

    @pl.when(last)
    def _():
        load_head.start()

    barrier = pltpu.get_barrier_semaphore()

    @pl.when(section > 0)
    def _():
        pl.semaphore_signal(barrier, inc=1, device_id={"section": section - 1})

    @pl.when(section < count - 1)
    def _():
        pl.semaphore_signal(barrier, inc=1, device_id={"section": section + 1})

    place = lax.axis_index("dp")
    line = lax.axis_size("dp")

    for away in range(1, line):
        pl.semaphore_signal(barrier, inc=1, device_id={"dp": lax.rem(place + away, line)})

    lender = section == count - 3

    @pl.when(lender)
    def _():
        pl.semaphore_signal(barrier, inc=1, device_id={"section": jnp.minimum(section + 2, count - 1)})

    @pl.when(last & (count > 2))
    def _():
        pl.semaphore_signal(barrier, inc=1, device_id={"section": jnp.maximum(section - 2, 0)})

    on_left = place < line // 2
    outer = jnp.where(on_left, place, line - 1 - place)
    inner_place = jnp.clip(jnp.where(on_left, place + 1, place - 1), 0, line - 1)
    outer_place = jnp.clip(jnp.where(on_left, place - 1, place + 1), 0, line - 1)
    end = (outer == 0) & (line > 2)
    lends_far = lender & end
    backs_far = last & (count > 2) & (outer == 1)

    @pl.when(lends_far)
    def _():
        pl.semaphore_signal(
            barrier,
            inc=1,
            device_id={"dp": inner_place, "section": jnp.minimum(section + 2, count - 1)},
        )

    @pl.when(backs_far)
    def _():
        pl.semaphore_signal(
            barrier, inc=1, device_id={"dp": outer_place, "section": jnp.maximum(section - 2, 0)}
        )

    def cols(block):
        return pl.ds(pl.multiple_of(block * LANES, LANES), LANES)

    col_index = lax.broadcasted_iota(jnp.int32, (1, width, LANES), 1)

    def fill(ref, value, size):
        ref[pl.ds(size // 2, height), pl.ds(EDGE, width)] = value

    def clear(ref, size):
        radius = size // 2
        side = jnp.zeros((height + 2 * radius, EDGE, LANES), f32)
        ref[:, pl.ds(0, EDGE)] = side
        ref[:, pl.ds(EDGE + width, EDGE)] = side
        zero = jnp.zeros((radius, width, LANES), f32)
        ref[pl.ds(0, radius), pl.ds(EDGE, width)] = zero
        ref[pl.ds(radius + height, radius), pl.ds(EDGE, width)] = zero

    flat_group = GROUP * width

    def conv(ref, weights, size, block, flip, put, starts=None):
        for start in starts or range(0, height, GROUP):
            total = None
            for c in range(size):
                moved = ref[pl.ds(start, GROUP + size - 1), pl.ds(EDGE + c - size // 2, width)]
                for r in range(size):
                    tap = r * size + c
                    tap = size * size - 1 - tap if flip else tap
                    part = weights[tap, :, cols(block)] * moved[r : r + GROUP]
                    total = part if total is None else total + part
            put(pl.ds(start, GROUP), pl.ds(start * width, flat_group), total.reshape(flat_group, LANES))

    def kept(image):
        away = col_index - offsets[image]
        away = jnp.where(away < 0, away + width, away)
        return jnp.where((away < BAND) | (section > 0), 1.0, 0.0)

    def xin(image, block, some=slice(None)):
        return x[image, some, :, cols(block)].astype(f32) * kept(image)

    clear(s5f, 5)
    clear(s3f, 3)

    acc5[...] = jnp.zeros_like(acc5)
    acc3[...] = jnp.zeros_like(acc3)

    @pl.loop(0, images)
    def _(n):
        @pl.loop(0, blocks)
        def _(b):
            clear(s3g.at[n, b], 3)

            @pl.when(jnp.logical_not(last))
            def _():
                clear(s5g.at[n, b], 5)

    def window_mask():
        tap = lax.broadcasted_iota(jnp.int32, (MASK_ROWS, rows), 0)
        spot = lax.broadcasted_iota(jnp.int32, (MASK_ROWS, rows), 1)
        i, h = jnp.zeros_like(tap), jnp.zeros_like(spot)
        for step in range(1, 5):
            i = i + jnp.where(tap >= 5 * step, 1, 0)
        for step in range(1, height):
            h = h + jnp.where(spot >= width * step, 1, 0)
        down, along = h - i + 2, (spot - width * h) - (tap - 5 * i) + 2
        inside = (down >= 0) & (down < height) & (along >= 0) & (along < width) & (tap < 25)
        return jnp.where(inside, 1.0, 0.0)

    @pl.when(last)
    def _():
        mask = window_mask()
        push[...] = mask.astype(bf16)
        k5_rows[pl.ds(24, 8)] = jnp.zeros((8, chans), f32)
        for tap in range(25):
            k5_rows[pl.ds(tap, 1)] = k5[tap]
        parts = jnp.concatenate(three_parts(k5_rows[...]), axis=0).astype(bf16)
        masks = jnp.concatenate([mask, mask, mask], axis=0).astype(bf16)
        spread5[...] = dot(masks, parts, contract_first)

    @pl.loop(0, images)
    def _(n):
        load_x(n).wait()

        @pl.loop(0, blocks)
        def _(b):
            value = xin(n, b)
            pool[n, :, cols(b)] = jnp.sum(value.reshape(rows // 8, 8, LANES), axis=0)
            fill(s3f, jnp.maximum(value, 0.0), 3)

            def put(_, where, out):
                d1[n, where, cols(b)] = out.astype(bf16)

            conv(s3f, k3, 3, b, False, put)

    flat = (images * rows, chans)
    load_w1.wait()
    a2[...] = jnp.maximum(dot(d1[...].reshape(flat), w1[...]), 0.0).astype(bf16).reshape(a2.shape)

    @pl.when(last)
    def _():
        for n in range(images):
            windows[n] = dot(push[...], a2[n])

    def second_depth(start, end):
        @pl.loop(start, end)
        def _(n):
            @pl.loop(0, blocks)
            def _(b):
                value = a2[n, :, cols(b)].astype(f32).reshape(height, width, LANES)
                fill(s5f, value, 5)

                def put(_, where, out):
                    d2[n, where, cols(b)] = out.astype(bf16)

                conv(s5f, k5, 5, b, False, put)

    late = section == count - 2

    load_w2.wait()
    early = jnp.where(late, images // 2, images)

    @pl.when(jnp.logical_not(last))
    def _():
        second_depth(0, early)
        w1t[...] = w1[...].T
        w2t[...] = w2[...].T

    classes = head.shape[0]

    @pl.when(last)
    def _():
        load_head.wait()
        x_sums = [jnp.sum(pool[n], axis=0, keepdims=True) for n in range(images)]
        d2_sums = [
            jnp.sum(k5_rows[...] * windows[n], axis=0, keepdims=True) for n in range(images)
        ]
        twice = -(-2 * images // 8) * 8
        fill_rows = [jnp.zeros((twice - 2 * images, chans), f32)] if twice > 2 * images else []
        x_sum = jnp.concatenate(x_sums + x_sums + fill_rows, axis=0)
        d2_sum = jnp.concatenate(d2_sums + d2_sums + fill_rows, axis=0)
        pooled = (x_sum + split_dot(d2_sum, w2[...], (((1,), (0,)), ((), ())))) * scale
        rest = jnp.zeros((LANES - twice, chans), f32)
        wide = jnp.concatenate([pooled, rest], axis=0)
        high = wide.astype(bf16)
        mid = (wide - high.astype(f32)).astype(bf16)
        logits = dot(head[...], high, contract_last) + dot(head[...], mid, contract_last)
        class_index = lax.broadcasted_iota(jnp.int32, (classes, LANES), 0)
        lane = lax.broadcasted_iota(jnp.int32, (1, LANES), 1)
        label_row = jnp.full((1, LANES), -1, jnp.int32)
        for n in range(images):
            label_row = jnp.where((lane == n) | (lane == n + images), labels[n], label_row)
        dlog = LOSS_SCALE * (logits - jnp.where(class_index == label_row, 1.0, 0.0))
        high = dlog.astype(bf16).astype(f32)
        part = jnp.where(lane < images, high, dlog - high).astype(bf16)
        both = dot(part, head[...], contract_first)
        grad = ((both[:images] + both[images : 2 * images]) * scale).astype(bf16).astype(f32)
        pad = jnp.zeros((8 - images, chans), f32)
        factors[place, pl.ds(0, 8)] = jnp.concatenate([*d2_sums, pad], axis=0)
        factors[place, pl.ds(8, 8)] = jnp.concatenate([grad, pad], axis=0)
        wide = jnp.concatenate([grad, jnp.zeros((16 - images, chans), f32)], axis=0)
        back_rows[...] = dot(wide.astype(bf16), w2[...], contract_last)

    half_height = height // 2

    def hand_over(n, part):
        where = pl.ds(part * half_height * width, half_height * width)
        return pltpu.make_async_remote_copy(
            src_ref=gout.at[n, where],
            dst_ref=gin.at[n, where],
            send_sem=send_sem.at[n, part],
            recv_sem=recv_sem.at[n, part],
            device_id={"section": jnp.maximum(section - 1, 0)},
        )

    pl.semaphore_wait(
        barrier,
        jnp.where(section > 0, 1, 0)
        + jnp.where(section < count - 1, 1, 0)
        + jnp.where(lender | (last & (count > 2)), 1, 0)
        + jnp.where(lends_far | backs_far, 1, 0)
        + (line - 1),
    )

    def give(away):
        other = lax.rem(place + away, line)
        return pltpu.make_async_remote_copy(
            src_ref=factors.at[place],
            dst_ref=factors.at[place],
            send_sem=factor_send.at[away],
            recv_sem=factor_recv.at[away],
            device_id={"dp": other},
        )

    def take(away):
        other = lax.rem(place + line - away, line)
        return pltpu.make_async_remote_copy(
            src_ref=factors.at[other],
            dst_ref=factors.at[other],
            send_sem=factor_send.at[away],
            recv_sem=factor_recv.at[away],
            device_id={"dp": lax.rem(place + away, line)},
        )

    @pl.when(last)
    def _():
        for away in range(1, line):
            give(away).start()

    chunk_rows = CHUNK_ROWS
    half = chans // chunk_rows

    def rows_of(k):
        return pl.ds(pl.multiple_of(k * chunk_rows, chunk_rows), chunk_rows)

    def lend(k):
        return pltpu.make_async_remote_copy(
            src_ref=line_refs[0].at[k],
            dst_ref=borrowed.at[k],
            send_sem=lend_sems.at[0, k],
            recv_sem=lend_sems.at[1, k],
            device_id={"section": jnp.minimum(section + 2, count - 1)},
        )

    def lend_far(k):
        return pltpu.make_async_remote_copy(
            src_ref=line_refs[0].at[k],
            dst_ref=line_refs[1].at[k + 2 * half],
            send_sem=lend_sems.at[0, k],
            recv_sem=line_refs[3].at[3, k + 2 * half],
            device_id={"dp": inner_place, "section": jnp.minimum(section + 2, count - 1)},
        )

    def back_far(k):
        return pltpu.make_async_remote_copy(
            src_ref=sums.at[k],
            dst_ref=sums.at[k - 2 * half],
            send_sem=line_refs[3].at[2, k],
            recv_sem=lend_sems.at[3, k - 2 * half],
            device_id={"dp": outer_place, "section": jnp.maximum(section - 2, 0)},
        )

    def pass_on(k):
        far = (k >= 2 * half) & (outer == 1) & FAR_BACK

        @pl.when(far)
        def _():
            back_far(k).start()

        @pl.when(jnp.logical_not(far))
        def _():
            main.outward(k).start()

    def give_back(k):
        return pltpu.make_async_remote_copy(
            src_ref=sums.at[k + 2 * half],
            dst_ref=sums.at[k],
            send_sem=lend_sems.at[2, k],
            recv_sem=lend_sems.at[3, k],
            device_id={"section": jnp.maximum(section - 2, 0)},
        )

    def own(k):
        @pl.when(k >= 2 * half)
        def _():
            lend(k - 2 * half).wait_recv()
            grads[rows_of(k)] = borrowed[k - 2 * half].astype(f32)

        return grads[rows_of(k)]

    def write_out(k):
        return pltpu.make_async_copy(sums.at[k], sums_out.at[k], out_sems.at[k])

    def done(k):
        @pl.when(k >= 2 * half)
        def _():
            give_back(k - 2 * half).start()

        @pl.when(k < 2 * half)
        def _():
            write_out(k).start()

    skips = (
        (lambda k: (k >= 2 * half) & end) if FAR_LEND else None,
        (lambda k: (k >= 2 * half) & end) if FAR_BACK else None,
    )
    main = Line(place, line, [*line_refs[0:3], sums, line_refs[3]], own, done, pass_on, skips)
    tap_line = Line(place, line, [*line_refs[4:7], tap_sums, line_refs[7]], lambda k: taps[k])
    lent = borrowed.shape[0]
    begin = jnp.where(lender, lent, jnp.where(last, half, 0))
    borrows = last & (count > 2)
    returns = borrows & jnp.logical_not(end) if FAR_BACK else borrows
    finish_at = jnp.where(borrows, 2 * half + lent, 2 * half)

    def kernel_grad(acc, value, ref, size):
        for c in range(size):
            sums_of = [None] * size
            for start in range(0, height, GROUP):
                left = value(pl.ds(start, GROUP), pl.ds(start * width, flat_group))
                moved = ref[
                    pl.ds(start, GROUP + size - 1), pl.ds(EDGE + size - 1 - c - size // 2, width)
                ]
                for r in range(size):
                    part = left * moved[size - 1 - r : size - 1 - r + GROUP]
                    part = jnp.sum(part.reshape(flat_group // 8, 8, LANES), axis=0)
                    sums_of[r] = part if sums_of[r] is None else sums_of[r] + part
            for r in range(size):
                acc[r * size + c] += sums_of[r]

    def kernel_grads(n, b):
        def second_value(_, where):
            return a2[n, where, cols(b)].astype(f32).reshape(GROUP, width, LANES)

        def first_value(some, _):
            return jnp.maximum(xin(n, b, some), 0.0)

        @pl.when(jnp.logical_not(last))
        def _():
            kernel_grad(acc5.at[b], second_value, s5g.at[n, b], 5)

        kernel_grad(acc3.at[b], first_value, s3g.at[n, b], 3)

        @pl.when(n == images - 1)
        def _():
            @pl.when(jnp.logical_not(last))
            def _():
                taps[b, pl.ds(0, 25)] = jnp.sum(acc5[b], axis=1)

            taps[b, pl.ds(TAP_SMALL, 9)] = jnp.sum(acc3[b], axis=1)

    waits = section < count - 2

    def product(at, left, right, start, end):
        shape = ((end - start) * rows, chans)
        left = left[pl.ds(start, end - start)].reshape(shape)
        right = right[pl.ds(start, end - start)].reshape(shape)
        part = dot(left, right, contract_first)
        if start == 0:
            grads[pl.ds(at, chans)] = part
        else:
            grads[pl.ds(at, chans)] += part

    def closing(at, left, right):
        @pl.when(waits)
        def _():
            product(at, left, right, images - 1, images)

        @pl.when(jnp.logical_not(waits))
        def _():
            product(at, left, right, 0, images)

    def weight_grads():
        @pl.when(jnp.logical_not(last))
        def _():
            closing(0, d2, gin)

            @pl.when((main.outer == 0) & jnp.logical_not(lender))
            def _():
                @pl.loop(0, AHEAD)
                def _(k):
                    main.gather(k)

        def hand_out(start, stop):
            @pl.when(lender)
            def _():
                @pl.loop(start, stop)
                def _(k):
                    main.out[k] = grads[rows_of(k)].astype(main.out.dtype)

                    @pl.when(end & FAR_LEND)
                    def _():
                        lend_far(k).start()

                    @pl.when(jnp.logical_not(end & FAR_LEND))
                    def _():
                        lend(k).start()

        hand_out(0, min(half, lent))
        closing(chans, d1, gp1)
        hand_out(min(half, lent), lent)

    @pl.loop(0, images)
    def _(n):
        @pl.when(jnp.logical_not(last))
        def _():
            for part in range(2):
                hand_over(n, part).wait_recv()
            tmp[...] = dot(gin[n], w2t[...])

            @pl.loop(0, blocks)
            def _(b):
                shifts = s5g.at[n, b]
                fill(shifts, tmp[:, cols(b)].reshape(height, width, LANES), 5)

                def put(_, where, back):
                    live = a2[n, where, cols(b)].astype(f32) > 0
                    gp1[n, where, cols(b)] = jnp.where(live, back, 0.0).astype(bf16)

                conv(shifts, k5, 5, b, True, put)

        @pl.when(last)
        def _():
            grad = factors[place, pl.ds(8 + n, 1)]
            gin[n] = jnp.broadcast_to(grad, (rows, chans)).astype(bf16)
            back = back_rows[pl.ds(n, 1)]
            live = a2[n].astype(f32) > 0
            gp1[n] = jnp.where(live, back * spread5[...], 0.0).astype(bf16)

        @pl.when((section == 0) & (n == images - 1))
        def _():
            weight_grads()

        @pl.when(last)
        def _():
            tmp[...] = dot(gp1[n], w1[...], contract_last)

        @pl.when(jnp.logical_not(last))
        def _():
            tmp[...] = dot(gp1[n], w1t[...])

        def first_back(b, part):
            def put(some, where, back):
                live = xin(n, b, some).reshape(flat_group, LANES) > 0
                grad = gin[n, where, cols(b)].astype(f32) + jnp.where(live, back, 0.0)
                gout[n, where, cols(b)] = grad.astype(bf16)

            starts = range(part * half_height, (part + 1) * half_height, GROUP)
            conv(s3g.at[n, b], k3, 3, b, True, put, starts)

        @pl.loop(0, blocks)
        def _(b):
            fill(s3g.at[n, b], tmp[:, cols(b)].reshape(height, width, LANES), 3)

            @pl.when(section > 0)
            def _():
                first_back(b, 0)

        @pl.when(section > 0)
        def _():
            hand_over(n, 0).start()

            @pl.loop(0, blocks)
            def _(b):
                first_back(b, 1)

            hand_over(n, 1).start()

        @pl.when(waits & (n == images - 2))
        def _():
            product(0, d2, gin, 0, images - 1)
            product(chans, d1, gp1, 0, images - 1)

    @pl.when(late)
    def _():
        second_depth(images // 2, images)

    @pl.when(section > 0)
    def _():
        weight_grads()

    busy = blocks * images
    taps[:, pl.ds(32, 8)] = jnp.zeros((blocks, 8, LANES), f32)

    @pl.when(last)
    def _():
        total = back_rows[pl.ds(0, 1)] * windows[0]
        for n in range(1, images):
            total = total + back_rows[pl.ds(n, 1)] * windows[n]
        for b in range(blocks):
            taps[b, pl.ds(0, 25)] = total[:25, b * LANES : (b + 1) * LANES]


    behind = LAG * (line - 1)
    sent = jnp.where(last | lender, 0, AHEAD)

    @pl.loop(0, jnp.maximum(finish_at - begin, busy + blocks) + behind)
    def _(step):
        for phase in range(3):
            tap_line.advance(phase, step - (busy - blocks + 1), 0, blocks)
            main.advance(phase, step, begin, finish_at - begin, sent)
            if phase == 0:

                @pl.when(step < busy)
                def _():
                    kernel_grads(step // blocks, step % blocks)

    @pl.when(last)
    def _():
        for away in range(1, line):
            take(away).wait_recv()
        left = factors[:, pl.ds(0, 8)].reshape(line * 8, chans)
        right = factors[:, pl.ds(8, 8)].reshape(line * 8, chans)
        left = jnp.concatenate(three_parts(left), axis=0).astype(bf16)
        right = jnp.concatenate([right, right, right], axis=0).astype(bf16)
        value = dot(left, right, contract_first)
        sums[pl.ds(0, half)] = value.reshape(half, chunk_rows, chans).astype(sums.dtype)

        @pl.loop(0, half)
        def _(k):
            write_out(k).start()

        for away in range(1, line):
            give(away).wait_send()

    @pl.loop(0, blocks)
    def _(k):
        tap_line.drain(k)

    @pl.loop(begin, finish_at)
    def _(k):
        main.drain(k)

    @pl.when(lender)
    def _():
        @pl.loop(0, lent)
        def _(k):
            give_back(k).wait_recv()
            write_out(k).start()
            lend(k).wait_send()

    @pl.when(returns)
    def _():
        @pl.loop(0, lent)
        def _(k):
            give_back(k).wait_send()

    @pl.when(section > 0)
    def _():
        @pl.loop(0, images)
        def _(n):
            for part in range(2):
                hand_over(n, part).wait_send()

    @pl.loop(0, 2 * half)
    def _(k):
        write_out(k).wait()


def finish(
    sums, taps, grad_first, grad_second, grad_small, grad_large,
    narrow, wide, taps_in, small, large, in_sem, out_sem,
):
    pieces, length = narrow.shape[0], narrow.shape[1]
    per_output = pieces // 2
    loads = [
        pltpu.make_async_copy(sums.at[pl.ds(p * length, length)], narrow.at[p], in_sem.at[p])
        for p in range(pieces)
    ]
    stores = [
        pltpu.make_async_copy(
            wide.at[p],
            (grad_second, grad_first)[p // per_output].at[pl.ds(p % per_output * length, length)],
            out_sem.at[p],
        )
        for p in range(pieces)
    ]
    loads.append(pltpu.make_async_copy(taps, taps_in, in_sem.at[pieces]))
    stores.append(pltpu.make_async_copy(small, grad_small, out_sem.at[pieces]))
    stores.append(pltpu.make_async_copy(large, grad_large, out_sem.at[pieces + 1]))
    for load in loads:
        load.start()
    for p in range(pieces):
        loads[p].wait()
        wide[p] = narrow[p].astype(f32)
        stores[p].start()
    loads[pieces].wait()
    for block in range(taps_in.shape[0]):
        where = pl.ds(block * LANES, LANES)
        for tap in range(25):
            large[tap, :, where] = taps_in[block, pl.ds(tap, 1)]
        for tap in range(9):
            small[tap, :, where] = taps_in[block, pl.ds(TAP_SMALL + tap, 1)]
    stores[pieces].start()
    stores[pieces + 1].start()
    for store in stores:
        store.wait()


def per_device(
    activations, depth_small, point_first, depth_large, point_second, head_weight, offsets, labels
):
    x = activations[0]
    images, height, width, chans = x.shape
    rows = height * width
    blocks = chans // LANES
    vmem = pl.BlockSpec(memory_space=pltpu.VMEM)
    smem = pl.BlockSpec(memory_space=pltpu.SMEM)
    anywhere = pl.BlockSpec(memory_space=pl.ANY)

    padded = width + 2 * EDGE
    line = lax.axis_size("dp")
    link = bf16 if line <= 4 else f32
    half = chans // CHUNK_ROWS
    lent = half * LENT // 8
    slots = 2 * half + lent

    def line_scratch(count, length, wide, dtype):
        return [pltpu.VMEM((count, length, wide), dtype)] * 3 + [
            pltpu.SemaphoreType.DMA((6, count))
        ]

    sums, tap_sums = pl.pallas_call(
        kernel,
        out_shape=(
            jax.ShapeDtypeStruct((2 * half, CHUNK_ROWS, chans), link),
            jax.ShapeDtypeStruct((blocks, TAP_ROWS, LANES), f32),
        ),
        in_specs=[smem, smem, anywhere, vmem, anywhere, vmem, anywhere, anywhere],
        out_specs=(anywhere, vmem),
        scratch_shapes=[
            pltpu.VMEM((slots, CHUNK_ROWS, chans), link),
            pltpu.SemaphoreType.DMA((2 * half,)),
            pltpu.VMEM((images, rows, chans), bf16),
            pltpu.VMEM((images, rows, chans), bf16),
            pltpu.VMEM((images, rows, chans), bf16),
            pltpu.VMEM((images, rows, chans), bf16),
            pltpu.VMEM((images, rows, chans), bf16),
            pltpu.VMEM((images, rows, chans), bf16),
            pltpu.VMEM((rows, chans), f32),
            pltpu.VMEM((height + 4, padded, LANES), f32),
            pltpu.VMEM((height + 2, padded, LANES), f32),
            pltpu.VMEM((images, blocks, height + 4, padded, LANES), f32),
            pltpu.VMEM((images, blocks, height + 2, padded, LANES), f32),
            pltpu.VMEM((images, 8, chans), f32),
            pltpu.VMEM((blocks, 9, 8, LANES), f32),
            pltpu.VMEM((blocks, 25, 8, LANES), f32),
            pltpu.VMEM((blocks, TAP_ROWS, LANES), f32),
            pltpu.VMEM((slots * CHUNK_ROWS, chans), f32),
            pltpu.VMEM((images, MASK_ROWS, chans), f32),
            pltpu.VMEM((MASK_ROWS, chans), f32),
            pltpu.VMEM((rows, chans), f32),
            pltpu.VMEM((MASK_ROWS, rows), bf16),
            pltpu.VMEM((line, 16, chans), f32),
            pltpu.VMEM((chans, chans), bf16),
            pltpu.VMEM((chans, chans), bf16),
            pltpu.VMEM((16, chans), f32),
            pltpu.VMEM((lent, CHUNK_ROWS, chans), link),
            pltpu.VMEM(x.shape, bf16),
            pltpu.VMEM((chans, chans), bf16),
            pltpu.VMEM((chans, chans), bf16),
            pltpu.VMEM(head_weight.shape, bf16),
            pltpu.SemaphoreType.DMA((images + 3,)),
            pltpu.SemaphoreType.DMA((images, 2)),
            pltpu.SemaphoreType.DMA((images, 2)),
            pltpu.SemaphoreType.DMA((line,)),
            pltpu.SemaphoreType.DMA((line,)),
            pltpu.SemaphoreType.DMA((4, lent)),
            *line_scratch(slots, CHUNK_ROWS, chans, link),
            *line_scratch(blocks, TAP_ROWS, LANES, f32),
        ],
        compiler_params=pltpu.CompilerParams(
            collective_id=0, has_side_effects=True, vmem_limit_bytes=56 << 20
        ),
        name="sections",
    )(
        offsets,
        labels,
        x,
        depth_small[0].reshape(9, 1, chans),
        point_first[0],
        depth_large[0].reshape(25, 1, chans),
        point_second[0],
        head_weight,
    )
    sum_first, sum_second, sum_small, sum_large = pl.pallas_call(
        finish,
        out_shape=(
            jax.ShapeDtypeStruct((chans, chans), f32),
            jax.ShapeDtypeStruct((chans, chans), f32),
            jax.ShapeDtypeStruct((9, 1, chans), f32),
            jax.ShapeDtypeStruct((25, 1, chans), f32),
        ),
        in_specs=[anywhere] * 2,
        out_specs=(anywhere,) * 4,
        scratch_shapes=[
            pltpu.VMEM((PIECES, 2 * chans // PIECES, chans), link),
            pltpu.VMEM((PIECES, 2 * chans // PIECES, chans), f32),
            pltpu.VMEM((blocks, TAP_ROWS, LANES), f32),
            pltpu.VMEM((9, 1, chans), f32),
            pltpu.VMEM((25, 1, chans), f32),
            pltpu.SemaphoreType.DMA((PIECES + 1,)),
            pltpu.SemaphoreType.DMA((PIECES + 2,)),
        ],
        compiler_params=pltpu.CompilerParams(vmem_limit_bytes=60 << 20),
        name="finish",
    )(sums.reshape(2 * chans, chans), tap_sums)
    return (
        sum_first[None],
        sum_second[None],
        sum_small.reshape(1, 3, 3, chans),
        sum_large.reshape(1, 5, 5, chans),
    )


def solution(mesh):
    placed = (
        P("section", ("groups", "dp"), None, None, None),
        P("section", None, None, None),
        P("section", None, None),
        P("section", None, None, None),
        P("section", None, None),
        P(),
        P(("groups", "dp")),
        P(("groups", "dp")),
    )
    return jax.shard_map(
        per_device,
        mesh=mesh,
        in_specs=placed,
        out_specs=(
            P("section", "groups", None),
            P("section", "groups", None),
            P("section", "groups", None, None),
            P("section", "groups", None, None),
        ),
        check_vma=False,
    )
```

```python
import jax
import jax.numpy as jnp
from jax import lax
from jax.experimental import pallas as pl
from jax.experimental.pallas import tpu as pltpu
from jax.sharding import PartitionSpec as P

BAND = 4
LOSS_SCALE = 64.0
LANES = 128
CHUNK_ROWS = 64
LAG = 4
AHEAD = 4
LENT = 11
FAR_LEND = False
FAR_BACK = True
TAP_ROWS = 40
TAP_SMALL = 25
MASK_ROWS = 32
PIECES = 4
GROUP = 4
EDGE = 8
f32 = jnp.float32
bf16 = jnp.bfloat16
contract_last = (((1,), (1,)), ((), ()))
contract_first = (((0,), (0,)), ((), ()))


def dot(a, b, dims=(((1,), (0,)), ((), ()))):
    return lax.dot_general(a, b, dims, preferred_element_type=f32)


def split_dot(values, matrix, dims):
    rows = values.shape[0]
    high = values.astype(bf16).astype(f32)
    rest = values - high
    mid = rest.astype(bf16).astype(f32)
    low = (rest - mid).astype(bf16).astype(f32)
    parts = jnp.concatenate([high, mid, low, jnp.zeros_like(low)], axis=0).astype(bf16)
    out = dot(parts, matrix, dims)
    return out[:rows] + out[rows : 2 * rows] + out[2 * rows : 3 * rows]


def three_parts(values):
    high = values.astype(bf16).astype(f32)
    rest = values - high
    mid = rest.astype(bf16).astype(f32)
    return high, mid, (rest - mid).astype(bf16).astype(f32)


class Line:
    def __init__(self, place, line, refs, get, done=None, pass_on=None, skips=(None, None)):
        self.place, self.line = place, line
        self.out, self.inner, self.across, self.final, self.sems = refs
        self.get, self.done, self.skips = get, done, skips
        self.pass_on = pass_on or (lambda k: self.outward(k).start())
        self.left = place < line // 2
        self.outer = jnp.where(self.left, place, line - 1 - place)
        self.deep = line // 2 - 1
        self.middle = self.outer == self.deep

    def copy(self, k, src, dst, lane, step):
        way = jnp.where(self.left, step, -step)
        return pltpu.make_async_remote_copy(
            src_ref=src.at[k],
            dst_ref=dst.at[k],
            send_sem=self.sems.at[lane, k],
            recv_sem=self.sems.at[3 + lane, k],
            device_id={"dp": jnp.clip(self.place + way, 0, self.line - 1)},
        )

    def inward(self, k):
        return self.copy(k, self.out, self.inner, 0, 1)

    def exchange(self, k):
        return self.copy(k, self.out, self.across, 1, 1)

    def outward(self, k):
        return self.copy(k, self.final, self.final, 2, -1)

    def advance(self, phase, step, first, chunks, sent=0):
        lag, active, act = (
            (LAG * self.outer, True, self.gather),
            (LAG * (self.deep + 1), self.middle, self.total),
            (LAG * (2 * self.deep + 1 - self.outer), jnp.logical_not(self.middle), self.spread),
        )[phase]
        k = step - lag

        if phase == 0:
            active = (self.outer > 0) | (k + first >= sent)
        skip = self.skips[phase // 2]
        if phase != 1 and skip is not None:
            active = active & jnp.logical_not(skip(k + first))

        @pl.when(active & (k >= 0) & (k < chunks))
        def _():
            act(k + first)

    def gather(self, k):
        dtype = self.out.dtype
        end = self.outer == 0

        @pl.when(end)
        def _():
            self.out[k] = self.get(k).astype(dtype)

        @pl.when(jnp.logical_not(end))
        def _():
            self.inward(k).wait_recv()
            self.out[k] = (self.get(k) + self.inner[k].astype(f32)).astype(dtype)

        @pl.when(self.middle)
        def _():
            self.exchange(k).start()

        @pl.when(jnp.logical_not(self.middle))
        def _():
            self.inward(k).start()

    def total(self, k):
        self.exchange(k).wait_recv()
        value = self.out[k].astype(f32) + self.across[k].astype(f32)
        self.final[k] = value.astype(self.final.dtype)

        @pl.when(self.outer > 0)
        def _():
            self.pass_on(k)

        if self.done is not None:
            self.done(k)

    def spread(self, k):
        self.outward(k).wait_recv()

        @pl.when(self.outer > 0)
        def _():
            self.pass_on(k)

        if self.done is not None:
            self.done(k)

    def drain(self, k):
        @pl.when(self.middle)
        def _():
            self.exchange(k).wait_send()

        sends = jnp.logical_not(self.middle)
        if self.skips[0] is not None:
            sends = sends & jnp.logical_not(self.skips[0](k))

        @pl.when(sends)
        def _():
            self.inward(k).wait_send()

        @pl.when(self.outer > 0)
        def _():
            self.outward(k).wait_send()


def kernel(
    offsets, labels, x_in, k3, w1_in, k5, w2_in, head_in,
    sums_out, tap_sums,
    sums, out_sems, d1, a2, d2, gin, gp1, gout, tmp, s5f, s3f, s5g, s3g, pool, acc3, acc5, taps,
    grads, windows, k5_rows, spread5, push, factors,
    w1t, w2t, back_rows, borrowed, x, w1, w2, head, load_sems, send_sem, recv_sem, factor_send, factor_recv, lend_sems, *line_refs,
):
    section = lax.axis_index("section")
    count = lax.axis_size("section")
    images, height, width, chans = x.shape
    rows = height * width
    blocks = chans // LANES
    last = section == count - 1
    scale = 1.0 / rows

    def load(source, target, index):
        return pltpu.make_async_copy(source, target, load_sems.at[index])

    def load_x(n):
        return load(x_in.at[n], x.at[n], n)

    load_w1, load_w2 = load(w1_in, w1, images), load(w2_in, w2, images + 1)
    load_head = load(head_in, head, images + 2)

    for n in range(images):
        load_x(n).start()
    load_w1.start()
    load_w2.start()

    @pl.when(last)
    def _():
        load_head.start()

    barrier = pltpu.get_barrier_semaphore()

    @pl.when(section > 0)
    def _():
        pl.semaphore_signal(barrier, inc=1, device_id={"section": section - 1})

    @pl.when(section < count - 1)
    def _():
        pl.semaphore_signal(barrier, inc=1, device_id={"section": section + 1})

    place = lax.axis_index("dp")
    line = lax.axis_size("dp")

    for away in range(1, line):
        pl.semaphore_signal(barrier, inc=1, device_id={"dp": lax.rem(place + away, line)})

    lender = section == count - 3

    @pl.when(lender)
    def _():
        pl.semaphore_signal(barrier, inc=1, device_id={"section": jnp.minimum(section + 2, count - 1)})

    @pl.when(last & (count > 2))
    def _():
        pl.semaphore_signal(barrier, inc=1, device_id={"section": jnp.maximum(section - 2, 0)})

    on_left = place < line // 2
    outer = jnp.where(on_left, place, line - 1 - place)
    inner_place = jnp.clip(jnp.where(on_left, place + 1, place - 1), 0, line - 1)
    outer_place = jnp.clip(jnp.where(on_left, place - 1, place + 1), 0, line - 1)
    end = (outer == 0) & (line > 2)
    lends_far = lender & end
    backs_far = last & (count > 2) & (outer == 1)

    @pl.when(lends_far)
    def _():
        pl.semaphore_signal(
            barrier,
            inc=1,
            device_id={"dp": inner_place, "section": jnp.minimum(section + 2, count - 1)},
        )

    @pl.when(backs_far)
    def _():
        pl.semaphore_signal(
            barrier, inc=1, device_id={"dp": outer_place, "section": jnp.maximum(section - 2, 0)}
        )

    def cols(block):
        return pl.ds(pl.multiple_of(block * LANES, LANES), LANES)

    col_index = lax.broadcasted_iota(jnp.int32, (1, width, LANES), 1)

    def fill(ref, value, size):
        ref[pl.ds(size // 2, height), pl.ds(EDGE, width)] = value

    def clear(ref, size):
        radius = size // 2
        side = jnp.zeros((height + 2 * radius, EDGE, LANES), f32)
        ref[:, pl.ds(0, EDGE)] = side
        ref[:, pl.ds(EDGE + width, EDGE)] = side
        zero = jnp.zeros((radius, width, LANES), f32)
        ref[pl.ds(0, radius), pl.ds(EDGE, width)] = zero
        ref[pl.ds(radius + height, radius), pl.ds(EDGE, width)] = zero

    flat_group = GROUP * width

    def conv(ref, weights, size, block, flip, put):
        for start in range(0, height, GROUP):
            total = None
            for c in range(size):
                moved = ref[pl.ds(start, GROUP + size - 1), pl.ds(EDGE + c - size // 2, width)]
                for r in range(size):
                    tap = r * size + c
                    tap = size * size - 1 - tap if flip else tap
                    part = weights[tap, :, cols(block)] * moved[r : r + GROUP]
                    total = part if total is None else total + part
            put(pl.ds(start, GROUP), pl.ds(start * width, flat_group), total.reshape(flat_group, LANES))

    def kept(image):
        away = col_index - offsets[image]
        away = jnp.where(away < 0, away + width, away)
        return jnp.where((away < BAND) | (section > 0), 1.0, 0.0)

    def xin(image, block, some=slice(None)):
        return x[image, some, :, cols(block)].astype(f32) * kept(image)

    clear(s5f, 5)
    clear(s3f, 3)

    acc5[...] = jnp.zeros_like(acc5)
    acc3[...] = jnp.zeros_like(acc3)

    @pl.loop(0, images)
    def _(n):
        @pl.loop(0, blocks)
        def _(b):
            clear(s3g.at[n, b], 3)

            @pl.when(jnp.logical_not(last))
            def _():
                clear(s5g.at[n, b], 5)

    def window_mask():
        tap = lax.broadcasted_iota(jnp.int32, (MASK_ROWS, rows), 0)
        spot = lax.broadcasted_iota(jnp.int32, (MASK_ROWS, rows), 1)
        i, h = jnp.zeros_like(tap), jnp.zeros_like(spot)
        for step in range(1, 5):
            i = i + jnp.where(tap >= 5 * step, 1, 0)
        for step in range(1, height):
            h = h + jnp.where(spot >= width * step, 1, 0)
        down, along = h - i + 2, (spot - width * h) - (tap - 5 * i) + 2
        inside = (down >= 0) & (down < height) & (along >= 0) & (along < width) & (tap < 25)
        return jnp.where(inside, 1.0, 0.0)

    @pl.when(last)
    def _():
        mask = window_mask()
        push[...] = mask.astype(bf16)
        k5_rows[pl.ds(24, 8)] = jnp.zeros((8, chans), f32)
        for tap in range(25):
            k5_rows[pl.ds(tap, 1)] = k5[tap]
        parts = jnp.concatenate(three_parts(k5_rows[...]), axis=0).astype(bf16)
        masks = jnp.concatenate([mask, mask, mask], axis=0).astype(bf16)
        spread5[...] = dot(masks, parts, contract_first)

    @pl.loop(0, images)
    def _(n):
        load_x(n).wait()

        @pl.loop(0, blocks)
        def _(b):
            value = xin(n, b)
            pool[n, :, cols(b)] = jnp.sum(value.reshape(rows // 8, 8, LANES), axis=0)
            fill(s3f, jnp.maximum(value, 0.0), 3)

            def put(_, where, out):
                d1[n, where, cols(b)] = out.astype(bf16)

            conv(s3f, k3, 3, b, False, put)

    flat = (images * rows, chans)
    load_w1.wait()
    a2[...] = jnp.maximum(dot(d1[...].reshape(flat), w1[...]), 0.0).astype(bf16).reshape(a2.shape)

    @pl.when(last)
    def _():
        for n in range(images):
            windows[n] = dot(push[...], a2[n])

    def second_depth(start, end):
        @pl.loop(start, end)
        def _(n):
            @pl.loop(0, blocks)
            def _(b):
                value = a2[n, :, cols(b)].astype(f32).reshape(height, width, LANES)
                fill(s5f, value, 5)

                def put(_, where, out):
                    d2[n, where, cols(b)] = out.astype(bf16)

                conv(s5f, k5, 5, b, False, put)

    late = section == count - 2

    load_w2.wait()
    early = jnp.where(late, images // 2, images)

    @pl.when(jnp.logical_not(last))
    def _():
        second_depth(0, early)
        w1t[...] = w1[...].T
        w2t[...] = w2[...].T

    classes = head.shape[0]

    @pl.when(last)
    def _():
        load_head.wait()
        x_sums = [jnp.sum(pool[n], axis=0, keepdims=True) for n in range(images)]
        d2_sums = [
            jnp.sum(k5_rows[...] * windows[n], axis=0, keepdims=True) for n in range(images)
        ]
        twice = -(-2 * images // 8) * 8
        fill_rows = [jnp.zeros((twice - 2 * images, chans), f32)] if twice > 2 * images else []
        x_sum = jnp.concatenate(x_sums + x_sums + fill_rows, axis=0)
        d2_sum = jnp.concatenate(d2_sums + d2_sums + fill_rows, axis=0)
        pooled = (x_sum + split_dot(d2_sum, w2[...], (((1,), (0,)), ((), ())))) * scale
        rest = jnp.zeros((LANES - twice, chans), f32)
        wide = jnp.concatenate([pooled, rest], axis=0)
        high = wide.astype(bf16)
        mid = (wide - high.astype(f32)).astype(bf16)
        logits = dot(head[...], high, contract_last) + dot(head[...], mid, contract_last)
        class_index = lax.broadcasted_iota(jnp.int32, (classes, LANES), 0)
        lane = lax.broadcasted_iota(jnp.int32, (1, LANES), 1)
        label_row = jnp.full((1, LANES), -1, jnp.int32)
        for n in range(images):
            label_row = jnp.where((lane == n) | (lane == n + images), labels[n], label_row)
        dlog = LOSS_SCALE * (logits - jnp.where(class_index == label_row, 1.0, 0.0))
        high = dlog.astype(bf16).astype(f32)
        part = jnp.where(lane < images, high, dlog - high).astype(bf16)
        both = dot(part, head[...], contract_first)
        grad = ((both[:images] + both[images : 2 * images]) * scale).astype(bf16).astype(f32)
        pad = jnp.zeros((8 - images, chans), f32)
        factors[place, pl.ds(0, 8)] = jnp.concatenate([*d2_sums, pad], axis=0)
        factors[place, pl.ds(8, 8)] = jnp.concatenate([grad, pad], axis=0)
        wide = jnp.concatenate([grad, jnp.zeros((16 - images, chans), f32)], axis=0)
        back_rows[...] = dot(wide.astype(bf16), w2[...], contract_last)

    def hand_over(n):
        return pltpu.make_async_remote_copy(
            src_ref=gout.at[n],
            dst_ref=gin.at[n],
            send_sem=send_sem.at[n],
            recv_sem=recv_sem.at[n],
            device_id={"section": jnp.maximum(section - 1, 0)},
        )

    pl.semaphore_wait(
        barrier,
        jnp.where(section > 0, 1, 0)
        + jnp.where(section < count - 1, 1, 0)
        + jnp.where(lender | (last & (count > 2)), 1, 0)
        + jnp.where(lends_far | backs_far, 1, 0)
        + (line - 1),
    )

    def give(away):
        other = lax.rem(place + away, line)
        return pltpu.make_async_remote_copy(
            src_ref=factors.at[place],
            dst_ref=factors.at[place],
            send_sem=factor_send.at[away],
            recv_sem=factor_recv.at[away],
            device_id={"dp": other},
        )

    def take(away):
        other = lax.rem(place + line - away, line)
        return pltpu.make_async_remote_copy(
            src_ref=factors.at[other],
            dst_ref=factors.at[other],
            send_sem=factor_send.at[away],
            recv_sem=factor_recv.at[away],
            device_id={"dp": lax.rem(place + away, line)},
        )

    @pl.when(last)
    def _():
        for away in range(1, line):
            give(away).start()

    chunk_rows = CHUNK_ROWS
    half = chans // chunk_rows

    def rows_of(k):
        return pl.ds(pl.multiple_of(k * chunk_rows, chunk_rows), chunk_rows)

    def lend(k):
        return pltpu.make_async_remote_copy(
            src_ref=line_refs[0].at[k],
            dst_ref=borrowed.at[k],
            send_sem=lend_sems.at[0, k],
            recv_sem=lend_sems.at[1, k],
            device_id={"section": jnp.minimum(section + 2, count - 1)},
        )

    def lend_far(k):
        return pltpu.make_async_remote_copy(
            src_ref=line_refs[0].at[k],
            dst_ref=line_refs[1].at[k + 2 * half],
            send_sem=lend_sems.at[0, k],
            recv_sem=line_refs[3].at[3, k + 2 * half],
            device_id={"dp": inner_place, "section": jnp.minimum(section + 2, count - 1)},
        )

    def back_far(k):
        return pltpu.make_async_remote_copy(
            src_ref=sums.at[k],
            dst_ref=sums.at[k - 2 * half],
            send_sem=line_refs[3].at[2, k],
            recv_sem=lend_sems.at[3, k - 2 * half],
            device_id={"dp": outer_place, "section": jnp.maximum(section - 2, 0)},
        )

    def pass_on(k):
        far = (k >= 2 * half) & (outer == 1) & FAR_BACK

        @pl.when(far)
        def _():
            back_far(k).start()

        @pl.when(jnp.logical_not(far))
        def _():
            main.outward(k).start()

    def give_back(k):
        return pltpu.make_async_remote_copy(
            src_ref=sums.at[k + 2 * half],
            dst_ref=sums.at[k],
            send_sem=lend_sems.at[2, k],
            recv_sem=lend_sems.at[3, k],
            device_id={"section": jnp.maximum(section - 2, 0)},
        )

    def own(k):
        @pl.when(k >= 2 * half)
        def _():
            lend(k - 2 * half).wait_recv()
            grads[rows_of(k)] = borrowed[k - 2 * half].astype(f32)

        return grads[rows_of(k)]

    def write_out(k):
        return pltpu.make_async_copy(sums.at[k], sums_out.at[k], out_sems.at[k])

    def done(k):
        @pl.when(k >= 2 * half)
        def _():
            give_back(k - 2 * half).start()

        @pl.when(k < 2 * half)
        def _():
            write_out(k).start()

    skips = (
        (lambda k: (k >= 2 * half) & end) if FAR_LEND else None,
        (lambda k: (k >= 2 * half) & end) if FAR_BACK else None,
    )
    main = Line(place, line, [*line_refs[0:3], sums, line_refs[3]], own, done, pass_on, skips)
    tap_line = Line(place, line, [*line_refs[4:7], tap_sums, line_refs[7]], lambda k: taps[k])
    lent = borrowed.shape[0]
    begin = jnp.where(lender, lent, jnp.where(last, half, 0))
    borrows = last & (count > 2)
    returns = borrows & jnp.logical_not(end) if FAR_BACK else borrows
    finish_at = jnp.where(borrows, 2 * half + lent, 2 * half)

    def kernel_grad(acc, value, ref, size):
        for c in range(size):
            sums_of = [None] * size
            for start in range(0, height, GROUP):
                left = value(pl.ds(start, GROUP), pl.ds(start * width, flat_group))
                moved = ref[
                    pl.ds(start, GROUP + size - 1), pl.ds(EDGE + size - 1 - c - size // 2, width)
                ]
                for r in range(size):
                    part = left * moved[size - 1 - r : size - 1 - r + GROUP]
                    part = jnp.sum(part.reshape(flat_group // 8, 8, LANES), axis=0)
                    sums_of[r] = part if sums_of[r] is None else sums_of[r] + part
            for r in range(size):
                acc[r * size + c] += sums_of[r]

    def kernel_grads(n, b):
        def second_value(_, where):
            return a2[n, where, cols(b)].astype(f32).reshape(GROUP, width, LANES)

        def first_value(some, _):
            return jnp.maximum(xin(n, b, some), 0.0)

        @pl.when(jnp.logical_not(last))
        def _():
            kernel_grad(acc5.at[b], second_value, s5g.at[n, b], 5)

        kernel_grad(acc3.at[b], first_value, s3g.at[n, b], 3)

        @pl.when(n == images - 1)
        def _():
            @pl.when(jnp.logical_not(last))
            def _():
                taps[b, pl.ds(0, 25)] = jnp.sum(acc5[b], axis=1)

            taps[b, pl.ds(TAP_SMALL, 9)] = jnp.sum(acc3[b], axis=1)

    waits = section < count - 2

    def product(at, left, right, start, end):
        shape = ((end - start) * rows, chans)
        left = left[pl.ds(start, end - start)].reshape(shape)
        right = right[pl.ds(start, end - start)].reshape(shape)
        part = dot(left, right, contract_first)
        if start == 0:
            grads[pl.ds(at, chans)] = part
        else:
            grads[pl.ds(at, chans)] += part

    def closing(at, left, right):
        @pl.when(waits)
        def _():
            product(at, left, right, images - 1, images)

        @pl.when(jnp.logical_not(waits))
        def _():
            product(at, left, right, 0, images)

    def weight_grads():
        @pl.when(jnp.logical_not(last))
        def _():
            closing(0, d2, gin)

            @pl.when((main.outer == 0) & jnp.logical_not(lender))
            def _():
                @pl.loop(0, AHEAD)
                def _(k):
                    main.gather(k)

        def hand_out(start, stop):
            @pl.when(lender)
            def _():
                @pl.loop(start, stop)
                def _(k):
                    main.out[k] = grads[rows_of(k)].astype(main.out.dtype)

                    @pl.when(end & FAR_LEND)
                    def _():
                        lend_far(k).start()

                    @pl.when(jnp.logical_not(end & FAR_LEND))
                    def _():
                        lend(k).start()

        hand_out(0, min(half, lent))
        closing(chans, d1, gp1)
        hand_out(min(half, lent), lent)

    @pl.loop(0, images)
    def _(n):
        @pl.when(jnp.logical_not(last))
        def _():
            hand_over(n).wait_recv()
            tmp[...] = dot(gin[n], w2t[...])

            @pl.loop(0, blocks)
            def _(b):
                shifts = s5g.at[n, b]
                fill(shifts, tmp[:, cols(b)].reshape(height, width, LANES), 5)

                def put(_, where, back):
                    live = a2[n, where, cols(b)].astype(f32) > 0
                    gp1[n, where, cols(b)] = jnp.where(live, back, 0.0).astype(bf16)

                conv(shifts, k5, 5, b, True, put)

        @pl.when(last)
        def _():
            grad = factors[place, pl.ds(8 + n, 1)]
            gin[n] = jnp.broadcast_to(grad, (rows, chans)).astype(bf16)
            back = back_rows[pl.ds(n, 1)]
            live = a2[n].astype(f32) > 0
            gp1[n] = jnp.where(live, back * spread5[...], 0.0).astype(bf16)

        @pl.when((section == 0) & (n == images - 1))
        def _():
            weight_grads()

        @pl.when(last)
        def _():
            tmp[...] = dot(gp1[n], w1[...], contract_last)

        @pl.when(jnp.logical_not(last))
        def _():
            tmp[...] = dot(gp1[n], w1t[...])

        @pl.loop(0, blocks)
        def _(b):
            shifts = s3g.at[n, b]
            fill(shifts, tmp[:, cols(b)].reshape(height, width, LANES), 3)

            @pl.when(section > 0)
            def _():
                def put(some, where, back):
                    live = xin(n, b, some).reshape(flat_group, LANES) > 0
                    grad = gin[n, where, cols(b)].astype(f32) + jnp.where(live, back, 0.0)
                    gout[n, where, cols(b)] = grad.astype(bf16)

                conv(shifts, k3, 3, b, True, put)

        @pl.when(section > 0)
        def _():
            hand_over(n).start()

        @pl.when(waits & (n == images - 2))
        def _():
            product(0, d2, gin, 0, images - 1)
            product(chans, d1, gp1, 0, images - 1)

    @pl.when(late)
    def _():
        second_depth(images // 2, images)

    @pl.when(section > 0)
    def _():
        weight_grads()

    busy = blocks * images
    taps[:, pl.ds(32, 8)] = jnp.zeros((blocks, 8, LANES), f32)

    @pl.when(last)
    def _():
        total = back_rows[pl.ds(0, 1)] * windows[0]
        for n in range(1, images):
            total = total + back_rows[pl.ds(n, 1)] * windows[n]
        for b in range(blocks):
            taps[b, pl.ds(0, 25)] = total[:25, b * LANES : (b + 1) * LANES]


    behind = LAG * (line - 1)
    sent = jnp.where(last | lender, 0, AHEAD)

    @pl.loop(0, jnp.maximum(finish_at - begin, busy + blocks) + behind)
    def _(step):
        for phase in range(3):
            tap_line.advance(phase, step - (busy - blocks + 1), 0, blocks)
            main.advance(phase, step, begin, finish_at - begin, sent)
            if phase == 0:

                @pl.when(step < busy)
                def _():
                    kernel_grads(step // blocks, step % blocks)

    @pl.when(last)
    def _():
        for away in range(1, line):
            take(away).wait_recv()
        left = factors[:, pl.ds(0, 8)].reshape(line * 8, chans)
        right = factors[:, pl.ds(8, 8)].reshape(line * 8, chans)
        left = jnp.concatenate(three_parts(left), axis=0).astype(bf16)
        right = jnp.concatenate([right, right, right], axis=0).astype(bf16)
        value = dot(left, right, contract_first)
        sums[pl.ds(0, half)] = value.reshape(half, chunk_rows, chans).astype(sums.dtype)

        @pl.loop(0, half)
        def _(k):
            write_out(k).start()

        for away in range(1, line):
            give(away).wait_send()

    @pl.loop(0, blocks)
    def _(k):
        tap_line.drain(k)

    @pl.loop(begin, finish_at)
    def _(k):
        main.drain(k)

    @pl.when(lender)
    def _():
        @pl.loop(0, lent)
        def _(k):
            give_back(k).wait_recv()
            write_out(k).start()
            lend(k).wait_send()

    @pl.when(returns)
    def _():
        @pl.loop(0, lent)
        def _(k):
            give_back(k).wait_send()

    @pl.when(section > 0)
    def _():
        @pl.loop(0, images)
        def _(n):
            hand_over(n).wait_send()

    @pl.loop(0, 2 * half)
    def _(k):
        write_out(k).wait()


def finish(
    sums, taps, grad_first, grad_second, grad_small, grad_large,
    narrow, wide, taps_in, small, large, in_sem, out_sem,
):
    pieces, length = narrow.shape[0], narrow.shape[1]
    per_output = pieces // 2
    loads = [
        pltpu.make_async_copy(sums.at[pl.ds(p * length, length)], narrow.at[p], in_sem.at[p])
        for p in range(pieces)
    ]
    stores = [
        pltpu.make_async_copy(
            wide.at[p],
            (grad_second, grad_first)[p // per_output].at[pl.ds(p % per_output * length, length)],
            out_sem.at[p],
        )
        for p in range(pieces)
    ]
    loads.append(pltpu.make_async_copy(taps, taps_in, in_sem.at[pieces]))
    stores.append(pltpu.make_async_copy(small, grad_small, out_sem.at[pieces]))
    stores.append(pltpu.make_async_copy(large, grad_large, out_sem.at[pieces + 1]))
    loads[pieces].start()
    for load in loads[:pieces]:
        load.start()
    loads[pieces].wait()
    for block in range(taps_in.shape[0]):
        where = pl.ds(block * LANES, LANES)
        for tap in range(25):
            large[tap, :, where] = taps_in[block, pl.ds(tap, 1)]
        for tap in range(9):
            small[tap, :, where] = taps_in[block, pl.ds(TAP_SMALL + tap, 1)]
    stores[pieces].start()
    stores[pieces + 1].start()
    for p in range(pieces):
        loads[p].wait()
        wide[p] = narrow[p].astype(f32)
        stores[p].start()
    for store in stores:
        store.wait()


def per_device(
    activations, depth_small, point_first, depth_large, point_second, head_weight, offsets, labels
):
    x = activations[0]
    images, height, width, chans = x.shape
    rows = height * width
    blocks = chans // LANES
    vmem = pl.BlockSpec(memory_space=pltpu.VMEM)
    smem = pl.BlockSpec(memory_space=pltpu.SMEM)
    anywhere = pl.BlockSpec(memory_space=pl.ANY)

    padded = width + 2 * EDGE
    line = lax.axis_size("dp")
    link = bf16 if line <= 4 else f32
    half = chans // CHUNK_ROWS
    lent = half * LENT // 8
    slots = 2 * half + lent

    def line_scratch(count, length, wide, dtype):
        return [pltpu.VMEM((count, length, wide), dtype)] * 3 + [
            pltpu.SemaphoreType.DMA((6, count))
        ]

    sums, tap_sums = pl.pallas_call(
        kernel,
        out_shape=(
            jax.ShapeDtypeStruct((2 * half, CHUNK_ROWS, chans), link),
            jax.ShapeDtypeStruct((blocks, TAP_ROWS, LANES), f32),
        ),
        in_specs=[smem, smem, anywhere, vmem, anywhere, vmem, anywhere, anywhere],
        out_specs=(anywhere, vmem),
        scratch_shapes=[
            pltpu.VMEM((slots, CHUNK_ROWS, chans), link),
            pltpu.SemaphoreType.DMA((2 * half,)),
            pltpu.VMEM((images, rows, chans), bf16),
            pltpu.VMEM((images, rows, chans), bf16),
            pltpu.VMEM((images, rows, chans), bf16),
            pltpu.VMEM((images, rows, chans), bf16),
            pltpu.VMEM((images, rows, chans), bf16),
            pltpu.VMEM((images, rows, chans), bf16),
            pltpu.VMEM((rows, chans), f32),
            pltpu.VMEM((height + 4, padded, LANES), f32),
            pltpu.VMEM((height + 2, padded, LANES), f32),
            pltpu.VMEM((images, blocks, height + 4, padded, LANES), f32),
            pltpu.VMEM((images, blocks, height + 2, padded, LANES), f32),
            pltpu.VMEM((images, 8, chans), f32),
            pltpu.VMEM((blocks, 9, 8, LANES), f32),
            pltpu.VMEM((blocks, 25, 8, LANES), f32),
            pltpu.VMEM((blocks, TAP_ROWS, LANES), f32),
            pltpu.VMEM((slots * CHUNK_ROWS, chans), f32),
            pltpu.VMEM((images, MASK_ROWS, chans), f32),
            pltpu.VMEM((MASK_ROWS, chans), f32),
            pltpu.VMEM((rows, chans), f32),
            pltpu.VMEM((MASK_ROWS, rows), bf16),
            pltpu.VMEM((line, 16, chans), f32),
            pltpu.VMEM((chans, chans), bf16),
            pltpu.VMEM((chans, chans), bf16),
            pltpu.VMEM((16, chans), f32),
            pltpu.VMEM((lent, CHUNK_ROWS, chans), link),
            pltpu.VMEM(x.shape, bf16),
            pltpu.VMEM((chans, chans), bf16),
            pltpu.VMEM((chans, chans), bf16),
            pltpu.VMEM(head_weight.shape, bf16),
            pltpu.SemaphoreType.DMA((images + 3,)),
            pltpu.SemaphoreType.DMA((images,)),
            pltpu.SemaphoreType.DMA((images,)),
            pltpu.SemaphoreType.DMA((line,)),
            pltpu.SemaphoreType.DMA((line,)),
            pltpu.SemaphoreType.DMA((4, lent)),
            *line_scratch(slots, CHUNK_ROWS, chans, link),
            *line_scratch(blocks, TAP_ROWS, LANES, f32),
        ],
        compiler_params=pltpu.CompilerParams(
            collective_id=0, has_side_effects=True, vmem_limit_bytes=56 << 20
        ),
        name="sections",
    )(
        offsets,
        labels,
        x,
        depth_small[0].reshape(9, 1, chans),
        point_first[0],
        depth_large[0].reshape(25, 1, chans),
        point_second[0],
        head_weight,
    )
    sum_first, sum_second, sum_small, sum_large = pl.pallas_call(
        finish,
        out_shape=(
            jax.ShapeDtypeStruct((chans, chans), f32),
            jax.ShapeDtypeStruct((chans, chans), f32),
            jax.ShapeDtypeStruct((9, 1, chans), f32),
            jax.ShapeDtypeStruct((25, 1, chans), f32),
        ),
        in_specs=[anywhere] * 2,
        out_specs=(anywhere,) * 4,
        scratch_shapes=[
            pltpu.VMEM((PIECES, 2 * chans // PIECES, chans), link),
            pltpu.VMEM((PIECES, 2 * chans // PIECES, chans), f32),
            pltpu.VMEM((blocks, TAP_ROWS, LANES), f32),
            pltpu.VMEM((9, 1, chans), f32),
            pltpu.VMEM((25, 1, chans), f32),
            pltpu.SemaphoreType.DMA((PIECES + 1,)),
            pltpu.SemaphoreType.DMA((PIECES + 2,)),
        ],
        compiler_params=pltpu.CompilerParams(vmem_limit_bytes=60 << 20),
        name="finish",
    )(sums.reshape(2 * chans, chans), tap_sums)
    return (
        sum_first[None],
        sum_second[None],
        sum_small.reshape(1, 3, 3, chans),
        sum_large.reshape(1, 5, 5, chans),
    )


def solution(mesh):
    placed = (
        P("section", ("groups", "dp"), None, None, None),
        P("section", None, None, None),
        P("section", None, None),
        P("section", None, None, None),
        P("section", None, None),
        P(),
        P(("groups", "dp")),
        P(("groups", "dp")),
    )
    return jax.shard_map(
        per_device,
        mesh=mesh,
        in_specs=placed,
        out_specs=(
            P("section", "groups", None),
            P("section", "groups", None),
            P("section", "groups", None, None),
            P("section", "groups", None, None),
        ),
        check_vma=False,
    )
```
